32 devices in a mesh: dp: 4 (over z), seq: 2 (over x), tensor: 4 (over y, core).
Axes of the slice: x: 2, y: 2, z: 4, core: 2. Of those that a mesh axis runs over, the one named last changes fastest.
Arguments:
- inputs: bfloat16 [4, 4096, 768], P('dp', 'seq'), may hold values from -6 to 6
- pass_embed: float32 [768], replicated, may hold values from -3 to 3
- norm1_gain: float32 [768], replicated, may hold values from 0.5 to 1.5
- norm1_shift: float32 [768], replicated, may hold values from -1 to 1
- w_qkv: bfloat16 [3, 768, 768], P(None, None, 'tensor'), may hold values from -0.21875 to 0.21875
- b_qv: float32 [2, 768], P(None, 'tensor'), may hold values from -1 to 1
- w_out: bfloat16 [768, 768], P('tensor'), may hold values from -0.875 to 0.875
- b_out: float32 [768], replicated, may hold values from -1 to 1
- norm2_gain: float32 [768], replicated, may hold values from 0.5 to 1.5
- norm2_shift: float32 [768], replicated, may hold values from -1 to 1
- w_up: bfloat16 [768, 3072], P(None, 'tensor'), may hold values from -0.21875 to 0.21875
- b_up: float32 [3072], P('tensor'), may hold values from -1.5 to 1.5
- w_down: bfloat16 [3072, 768], P('tensor'), may hold values from -0.109375 to 0.109375
- b_down: float32 [768], replicated, may hold values from -1 to 1
- out_grad: bfloat16 [4, 4096, 768], P('dp', 'seq'), may hold values from -6 to 6
- seg_id: int32 [4, 4096], P('dp'), may hold values from 0 to 12, as said below
- parent: int32 [4, 13], P('dp'), may hold values from 0 to 4, as said below
Outputs:
- output: bfloat16 [4, 4096, 768], P('dp', ('seq', 'tensor'))
- input_grad: bfloat16 [4, 4096, 768], P('dp', ('seq', 'tensor'))
- grad_pass: float32 [768], replicated
- grad_norm1_gain: float32 [768], replicated
- grad_norm1_shift: float32 [768], replicated
- grad_w_qkv: float32 [3, 768, 768], P(None, None, 'tensor')
- grad_b_qv: float32 [2, 768], P(None, 'tensor')
- grad_w_out: float32 [768, 768], P('tensor')
- grad_b_out: float32 [768], replicated
- grad_norm2_gain: float32 [768], replicated
- grad_norm2_shift: float32 [768], replicated
- grad_w_up: float32 [768, 3072], P(None, 'tensor')
- grad_b_up: float32 [3072], P('tensor')
- grad_w_down: float32 [3072, 768], P('tensor')
- grad_b_down: float32 [768], replicated
The draws below stay inside these ranges and needn't reach their ends.
Inputs may be any that keep to these rules, and one draw needn't show every extreme that they name: `seg_id`: in each tree segment 0 (the trunk) covers 1024 consecutive tokens starting at a multiple of 1024; each other segment covers 256 consecutive tokens starting at a multiple of 256. Segment 0 is its own parent; segments 1 to 4 have parent 0; each of them is the parent of exactly two of the other segments.
All inputs are finite; a program needn't handle non-finite values.
Results may differ from the reference program's by a relative error of at most 0.019.
Values may be sent and summed in bfloat16 or wider, within the bound.
No kernel may reach another device: no remote copies, remote signals or barrier semaphores. Data moves between devices by JAX's collectives and lax.ppermute only.
A program may use at most 256 MiB of HBM per device.

```python
import jax
import jax.numpy as jnp
from jax import lax

D = 768
HEADS = 12
HD = 64
FF = 3072
TRUNK = 1024
PIECE = 256
BRANCHES = 4
SEGS = 13
TREE_LEN = 4096
TREES = 4


def layout_one(tree_key):
    wide = TRUNK // PIECE
    slots = TREE_LEN // PIECE
    others = SEGS - 1
    start_key, order_key, leaf_key = jax.random.split(tree_key, 3)
    trunk_at = jax.random.randint(start_key, (), 0, TREE_LEN // TRUNK, dtype=jnp.int32) * wide
    order = jax.random.permutation(order_key, others).astype(jnp.int32) + 1
    slot_ids = jnp.arange(slots, dtype=jnp.int32)
    in_trunk = (slot_ids >= trunk_at) & (slot_ids < trunk_at + wide)
    ranks = jnp.cumsum(jnp.where(in_trunk, 0, 1).astype(jnp.int32)) - 1
    slot_seg = jnp.where(in_trunk, 0, order[jnp.clip(ranks, 0, others - 1)]).astype(jnp.int32)
    seg_tokens = jnp.broadcast_to(slot_seg[:, None], (slots, PIECE)).reshape(TREE_LEN)
    leaves = jax.random.permutation(leaf_key, 2 * BRANCHES).astype(jnp.int32)
    parents = jnp.concatenate([jnp.zeros((1 + BRANCHES,), jnp.int32), 1 + leaves // 2])
    return (seg_tokens, parents)


def layout_all(key):
    tree_keys = jax.random.split(jax.random.fold_in(key, 7), TREES)
    return jax.vmap(layout_one)(tree_keys)


def draw_seg_id(key, part):
    return layout_all(key)[0]


def draw_parent(key, part):
    return layout_all(key)[1]


def shard_levels(own_key, extent, cuts, smallest, high):
    factor_of = 1.0
    for axis_at, shards_of in cuts:
        heights = jax.random.uniform(jax.random.fold_in(jax.random.fold_in(own_key, 6), axis_at), (shards_of,), jnp.float32, smallest / len(cuts), high / len(cuts))
        factor_of = factor_of * jnp.repeat(jnp.exp(heights), extent[axis_at] // shards_of).reshape((-1,) + (1,) * (len(extent) - 1 - axis_at))
    return factor_of


def noise(own_key, shape, scale, bound, shards=(), kind=jnp.bfloat16):
    values = jax.random.normal(own_key, shape, jnp.float32) * scale
    if len(shards) > 0:
        values = shard_levels(own_key, shape, shards, -0.22, 0.18) * values
    return jnp.clip(values, min=-bound, max=bound).astype(kind)


def setup_inputs(seed: int = 0) -> dict:
    arg_keys = jax.random.split(jax.random.key(seed), 18)
    inputs = noise(arg_keys[0], (TREES, TREE_LEN, D), 1.0, 6.0, ((0, 4), (1, 2)))
    pass_embed = noise(arg_keys[1], (D,), 0.5, 3.0, (), jnp.float32)
    norm1_gain = jnp.clip(1.0 + 0.1 * jax.random.normal(arg_keys[2], (D,), jnp.float32), 0.5, 1.5)
    norm1_shift = noise(arg_keys[3], (D,), 0.2, 1.0, (), jnp.float32)
    w_qkv = noise(arg_keys[4], (3, D, D), D ** -0.5, 0.21875, ((2, 4),))
    b_qv = noise(arg_keys[5], (2, D), 0.2, 1.0, ((1, 4),), jnp.float32)
    w_out = noise(arg_keys[6], (D, D), (D // 16) ** -0.5, 0.875, ((0, 4),))
    b_out = noise(arg_keys[7], (D,), 0.2, 1.0, (), jnp.float32)
    norm2_gain = jnp.clip(1.0 + 0.1 * jax.random.normal(arg_keys[8], (D,), jnp.float32), 0.5, 1.5)
    norm2_shift = noise(arg_keys[9], (D,), 0.2, 1.0, (), jnp.float32)
    w_up = noise(arg_keys[10], (D, FF), D ** -0.5, 0.21875, ((1, 4),))
    b_up = noise(arg_keys[11], (FF,), 0.3, 1.5, ((0, 4),), jnp.float32)
    w_down = noise(arg_keys[12], (FF, D), FF ** -0.5, 0.109375, ((0, 4),))
    b_down = noise(arg_keys[13], (D,), 0.2, 1.0, (), jnp.float32)
    out_grad = noise(arg_keys[14], (TREES, TREE_LEN, D), 1.0, 6.0, ((0, 4), (1, 2)))
    seg_id = draw_seg_id(jax.random.fold_in(arg_keys[17], 71), 0)
    parent = draw_parent(jax.random.fold_in(arg_keys[17], 71), 0)
    return {"inputs": inputs, "pass_embed": pass_embed, "norm1_gain": norm1_gain, "norm1_shift": norm1_shift, "w_qkv": w_qkv, "b_qv": b_qv, "w_out": w_out, "b_out": b_out, "norm2_gain": norm2_gain, "norm2_shift": norm2_shift, "w_up": w_up, "b_up": b_up, "w_down": w_down, "b_down": b_down, "out_grad": out_grad, "seg_id": seg_id, "parent": parent}


@jax.custom_vjp
def low(v):
    return lax.optimization_barrier(v.astype(jnp.bfloat16)).astype(jnp.float32)

@jax.custom_vjp
def low_back(v):
    return v

def low_keep(v):
    return (low(v), None)

def low_pass(kept, grad):
    return (grad,)

def back_keep(v):
    return (v, None)

def back_low(kept, grad):
    return (low(grad),)
low.defvjp(low_keep, low_pass)
low_back.defvjp(back_keep, back_low)
EPS = 1e-05
ROOT = 0.7978845608028654
HIGH = lax.Precision.HIGHEST

def layer_norm(values, gain_vec, shift_vec):
    row_mean = lax.optimization_barrier(jnp.mean(values, -1, keepdims=True))
    centred = values - row_mean
    row_var = lax.optimization_barrier(jnp.mean(centred * centred, -1, keepdims=True))
    return centred * lax.rsqrt(row_var + EPS) * gain_vec + shift_vec

def gelu_tanh(values):
    return 0.5 * values * (1.0 + jnp.tanh(ROOT * (values + 0.044715 * values * values * values)))

def matmul(left, right):
    return jnp.dot(left, right, precision=HIGH)

def ancestry(parent_row):
    labels = jnp.arange(parent_row.shape[0], dtype=jnp.int32)
    step_up = ((parent_row[:, None] == labels[None, :]) & (labels[:, None] != labels[None, :])).astype(jnp.float32)
    return step_up + matmul(step_up, step_up)

def tree_forward(seg_row, parent_row, inputs, pass_embed, norm1_gain, norm1_shift, w_qkv, b_qv, w_out, b_out, norm2_gain, norm2_shift, w_up, b_up, w_down, b_down):
    length = inputs.shape[0]
    residual = inputs + pass_embed
    normed = low(layer_norm(residual, norm1_gain, norm1_shift))
    queries = low(low_back(matmul(normed, w_qkv[0]) + b_qv[0]))
    key_proj = low(low_back(matmul(normed, w_qkv[1])))
    value_proj = low(low_back(matmul(normed, w_qkv[2]) + b_qv[1]))
    key_heads = key_proj.reshape(length, HEADS, HD)
    value_heads = value_proj.reshape(length, HEADS, HD)
    blk_width = min(512, length)
    blk_count = length // blk_width
    query_blocks = queries.reshape(blk_count, blk_width, HEADS, HD)
    positions = jnp.arange(length, dtype=jnp.int32)
    seg_labels = jnp.arange(SEGS, dtype=jnp.int32)
    key_hot = (seg_labels[:, None] == seg_row[None, :]).astype(jnp.float32)
    reach_keys = matmul(ancestry(parent_row), key_hot)

    def one_block(pieces):
        query_block, blk_start = pieces
        seg_query = lax.dynamic_slice_in_dim(seg_row, blk_start, blk_width)
        pos_query = blk_start + jnp.arange(blk_width, dtype=jnp.int32)
        visible = (seg_query[:, None] == seg_row[None, :]) & (pos_query[:, None] >= positions[None, :]) | (reach_keys[seg_query] > 0.5)
        raw_score = jnp.einsum('qhd,khd->hqk', query_block, key_heads, precision=HIGH) * 0.125
        scores = jnp.where(visible[None], low_back(raw_score), -jnp.inf)
        row_top = lax.optimization_barrier(jnp.max(scores, -1, keepdims=True))
        weights = jnp.exp(scores - row_top)
        prob_low = low(weights / lax.optimization_barrier(jnp.sum(weights, -1, keepdims=True)))
        return jnp.einsum('hqk,khd->qhd', prob_low, value_heads, precision=HIGH)
    starts = blk_width * jnp.arange(blk_count, dtype=jnp.int32)
    mixture = lax.map(jax.checkpoint(one_block), (query_blocks, starts)).reshape(length, D)
    mixture = low(low_back(mixture))
    middle = residual + low_back(matmul(mixture, w_out)) + b_out
    lifted = low(layer_norm(middle, norm2_gain, norm2_shift))
    pre_act = low_back(matmul(lifted, w_up) + b_up)
    active = low(gelu_tanh(pre_act))
    return middle + low_back(matmul(active, w_down)) + b_down

def reference(inputs, pass_embed, norm1_gain, norm1_shift, w_qkv, b_qv, w_out, b_out, norm2_gain, norm2_shift, w_up, b_up, w_down, b_down, out_grad, seg_id, parent):
    params = tuple((weight.astype(jnp.float32) for weight in (pass_embed, norm1_gain, norm1_shift, w_qkv, b_qv, w_out, b_out, norm2_gain, norm2_shift, w_up, b_up, w_down, b_down)))

    def one_tree(totals, pieces):
        tree_in, tree_grad, seg_row, parent_row = pieces

        def forward(tree_x, *weights):
            return tree_forward(seg_row, parent_row, tree_x, *weights)
        result, pullback = jax.vjp(forward, tree_in.astype(jnp.float32), *params)
        gradients = pullback(tree_grad.astype(jnp.float32))
        totals = tuple((old_sum + new_grad for old_sum, new_grad in zip(totals, gradients[1:])))
        return (totals, (result.astype(jnp.bfloat16), gradients[0].astype(jnp.bfloat16)))
    zero_sums = tuple((jnp.zeros(weight.shape, jnp.float32) for weight in params))
    summed, (outputs, input_grads) = lax.scan(one_tree, zero_sums, (inputs, out_grad, seg_id, parent))
    return (outputs, input_grads, summed[0], summed[1], summed[2], summed[3], summed[4], summed[5], summed[6], summed[7], summed[8], summed[9], summed[10], summed[11], summed[12])
```

```python
import functools

import jax
import jax.numpy as jnp
from jax import lax
from jax.experimental import pallas as pl
from jax.experimental.pallas import tpu as pltpu
from jax.sharding import PartitionSpec as P

HD = 64
BLK = 256
TRUNK_BLOCKS = 4
LANE = 256
EPS = 1e-05
ROOT = 0.7978845608028654
BF = jnp.bfloat16
F4 = jnp.float32
NT = (((1,), (1,)), ((), ()))
NN = (((1,), (0,)), ((), ()))
TN = (((0,), (0,)), ((), ()))


def dot(left, right, dims=NN):
    return lax.dot_general(left, right, dims, preferred_element_type=F4)


def norm_stats(values):
    row_mean = jnp.mean(values, -1, keepdims=True)
    centred = values - row_mean
    inv_std = lax.rsqrt(jnp.mean(centred * centred, -1, keepdims=True) + EPS)
    return (centred * inv_std, inv_std)


def norm_back(grad_out, normal, inv_std, gain_vec):
    scaled = grad_out * gain_vec
    return inv_std * (
        scaled
        - jnp.mean(scaled, -1, keepdims=True)
        - normal * jnp.mean(scaled * normal, -1, keepdims=True)
    )


def gelu_parts(pre_act):
    cubic_term = 0.044715 * pre_act * pre_act * pre_act
    tangent = jnp.tanh(ROOT * (pre_act + cubic_term))
    gelu_value = 0.5 * pre_act * (1.0 + tangent)
    gelu_slope = 0.5 * (1.0 + tangent) + 0.5 * pre_act * (1.0 - tangent * tangent) * ROOT * (
        1.0 + 3.0 * 0.044715 * pre_act * pre_act
    )
    return (gelu_value, gelu_slope)


def block_rows(pos, count=1):
    return pl.ds(pl.multiple_of(pos * BLK, BLK), count * BLK)


def head_masks(shape, heads):
    lane = lax.broadcasted_iota(jnp.int32, shape, 1) // HD
    return [lane == h for h in range(heads)]


def each_tile(order_ref, tile):
    trunk = [order_ref[i] for i in range(TRUNK_BLOCKS)]
    base = order_ref[16]
    tile(trunk[0], trunk[1], [], [(trunk[0], True)], [(trunk[0], False), (trunk[1], True)])
    tile(
        trunk[2],
        trunk[3],
        [(trunk[0], 2)],
        [(trunk[2], True)],
        [(trunk[2], False), (trunk[3], True)],
    )

    def branch(i, carry):
        one, two = order_ref[4 + 2 * i], order_ref[5 + 2 * i]
        tile(one, two, [(base, 4)], [(one, True)], [(two, True)])
        return carry

    lax.fori_loop(0, 2, branch, 0)

    def leaf(i, carry):
        one, two = order_ref[8 + 2 * i], order_ref[9 + 2 * i]
        tile(one, two, [(base, 4), (order_ref[4 + i], 1)], [(one, True)], [(two, True)])
        return carry

    lax.fori_loop(0, 4, leaf, 0)


def attend_kernel(heads, rows, order_ref, part_ref, qkv_ref, out_ref, lse_ref):
    part = part_ref[0]

    def q_at(pos):
        return qkv_ref[pl.ds(pl.multiple_of(pos * BLK + part * rows, rows), rows), 0:LANE]

    def k_at(pos, count=1):
        return qkv_ref[block_rows(pos, count), LANE : 2 * LANE]

    def v_at(pos, count=1):
        return qkv_ref[block_rows(pos, count), 2 * LANE : 3 * LANE]

    row_at = lax.broadcasted_iota(jnp.int32, (rows, BLK), 0) + part * rows
    causal = row_at >= lax.broadcasted_iota(jnp.int32, (rows, BLK), 1)
    masks = head_masks((2 * rows, LANE), heads)

    def tile(first, second, shared, parts_a, parts_b):
        q = jnp.concatenate([q_at(first), q_at(second)], 0) * BF(0.125)
        result = jnp.zeros((2 * rows, LANE), F4)
        log_cols = []
        for h in range(heads):
            qm = jnp.where(masks[h], q, BF(0))
            halves = [qm[:rows], qm[rows:]]
            wide = [dot(qm, k_at(p, c), NT) for p, c in shared]
            own = [
                [
                    jnp.where(causal, dot(halves[i], k_at(p), NT), -jnp.inf)
                    if diag
                    else dot(halves[i], k_at(p), NT)
                    for p, diag in parts
                ]
                for i, parts in enumerate((parts_a, parts_b))
            ]
            tops = []
            for i in range(2):
                tops.append(
                    functools.reduce(
                        jnp.maximum,
                        [
                            jnp.max(s, 1, keepdims=True)
                            for s in [w[i * rows : (i + 1) * rows] for w in wide] + own[i]
                        ],
                    )
                )
            top = jnp.concatenate(tops, 0)
            mix = jnp.zeros((2 * rows, LANE), F4)
            total = jnp.zeros((2 * rows, 1), F4)
            for s, (p, c) in zip(wide, shared):
                e = jnp.exp(s - top)
                total = total + jnp.sum(e, 1, keepdims=True)
                mix = mix + dot(e.astype(BF), v_at(p, c))
            extra = []
            sums = []
            for i, parts in enumerate((parts_a, parts_b)):
                m_i = jnp.zeros((rows, LANE), F4)
                t_i = jnp.zeros((rows, 1), F4)
                for s, (p, _) in zip(own[i], parts):
                    e = jnp.exp(s - tops[i])
                    t_i = t_i + jnp.sum(e, 1, keepdims=True)
                    m_i = m_i + dot(e.astype(BF), v_at(p))
                extra.append(m_i)
                sums.append(t_i)
            total = total + jnp.concatenate(sums, 0)
            mix = (mix + jnp.concatenate(extra, 0)) / total
            result = jnp.where(masks[h], mix, result)
            log_cols.append(top + jnp.log(total))
        low = result.astype(BF)[:, : heads * HD]
        out_ref[first] = low[:rows]
        out_ref[second] = low[rows:]
        lane = lax.broadcasted_iota(jnp.int32, (2 * rows, 128), 1)
        cols = jnp.zeros((2 * rows, 128), F4)
        for h in range(heads):
            cols = jnp.where(lane == h, log_cols[h], cols)
        flat = jnp.transpose(cols)[:8]
        lse_ref[first] = flat[:, :rows]
        lse_ref[second] = flat[:, rows:]

    each_tile(order_ref, tile)


def in_vmem(count):
    return [pl.BlockSpec(memory_space=pltpu.VMEM)] * count


def in_smem(count):
    return [pl.BlockSpec(memory_space=pltpu.SMEM)] * count


def attend(qkv, order, part, heads, rows):
    blocks = qkv.shape[0] // BLK
    return pl.pallas_call(
        functools.partial(attend_kernel, heads, rows),
        out_shape=(
            jax.ShapeDtypeStruct((blocks, rows, heads * HD), BF),
            jax.ShapeDtypeStruct((blocks, 8, rows), F4),
        ),
        in_specs=in_smem(2) + in_vmem(1),
        out_specs=in_vmem(2),
        compiler_params=pltpu.CompilerParams(vmem_limit_bytes=56 << 20),
        cost_estimate=pl.CostEstimate(
            flops=25_000_000_000, bytes_accessed=10_000_000, transcendentals=9_000_000
        ),
        name="tree_attend",
    )(order, part, qkv)


def attend_back_kernel(
    heads, rows, order_ref, part_ref, qkv_ref, mix_ref, grad_ref, lse_ref, out_ref, acc_k, acc_v
):
    part = part_ref[0]
    width = heads * HD

    def q_rows(pos):
        return pl.ds(pl.multiple_of(pos * BLK + part * rows, rows), rows)

    def k_at(pos, count=1):
        return qkv_ref[block_rows(pos, count), LANE : 2 * LANE]

    def v_at(pos, count=1):
        return qkv_ref[block_rows(pos, count), 2 * LANE : 3 * LANE]

    key_at = lax.broadcasted_iota(jnp.int32, (BLK, rows), 0)
    causal = (lax.broadcasted_iota(jnp.int32, (BLK, rows), 1) + part * rows) >= key_at
    masks = head_masks((2 * rows, LANE), heads)
    acc_k[...] = jnp.zeros_like(acc_k)
    acc_v[...] = jnp.zeros_like(acc_v)
    out_ref[:, 0:LANE] = jnp.zeros((out_ref.shape[0], LANE), BF)
    pick = (
        lax.broadcasted_iota(jnp.int32, (8, LANE), 1) // HD
        == lax.broadcasted_iota(jnp.int32, (8, LANE), 0)
    ).astype(BF)
    pad = jnp.zeros((2 * rows, LANE - width), BF)

    def tile(first, second, shared, parts_a, parts_b):
        q = jnp.concatenate(
            [qkv_ref[q_rows(first), 0:LANE], qkv_ref[q_rows(second), 0:LANE]], 0
        ) * BF(0.125)
        grad = jnp.concatenate([jnp.concatenate([grad_ref[first], grad_ref[second]], 0), pad], 1)
        mix = jnp.concatenate([jnp.concatenate([mix_ref[first], mix_ref[second]], 0), pad], 1)
        inner = dot(pick, (grad.astype(F4) * mix.astype(F4)).astype(BF), NT)
        lse = jnp.concatenate([lse_ref[first], lse_ref[second]], 1)
        qms = [jnp.where(masks[h], q, BF(0)) for h in range(heads)]
        gms = [jnp.where(masks[h], grad, BF(0)) for h in range(heads)]

        def pieces(keys, values, h, cut, diag):
            e = jnp.exp(dot(keys, qms[h][cut], NT) - lse[h : h + 1, cut])
            if diag:
                e = jnp.where(causal, e, 0.0)
            t = dot(values, gms[h][cut], NT)
            return e.astype(BF), (e * (t - inner[h : h + 1, cut])).astype(BF)

        def strip(pos, count, cut, diag, grad_q):
            keys, values = k_at(pos, count), v_at(pos, count)
            es = []
            ds = []
            for h in range(heads):
                e, d = pieces(keys, values, h, cut, diag)
                es.append(e)
                ds.append(d)
                grad_q = grad_q + jnp.where(masks[h][cut], dot(d, keys, TN), 0.0)
            acc_v[block_rows(pos, count), :] += dot(
                jnp.concatenate(es, 1), jnp.concatenate([g[cut] for g in gms], 0)
            )
            acc_k[block_rows(pos, count), :] += dot(
                jnp.concatenate(ds, 1), jnp.concatenate([g[cut] for g in qms], 0)
            )
            return grad_q

        grad_q = jnp.zeros((2 * rows, LANE), F4)
        for pos, count in shared:
            grad_q = strip(pos, count, slice(0, 2 * rows), False, grad_q)
        halves = []
        for i, parts in enumerate((parts_a, parts_b)):
            half = jnp.zeros((rows, LANE), F4)
            for pos, diag in parts:
                half = strip(pos, 1, slice(i * rows, (i + 1) * rows), diag, half)
            halves.append(half)
        grad_q = ((grad_q + jnp.concatenate(halves, 0)) * 0.125).astype(BF)
        out_ref[q_rows(first), 0:LANE] = grad_q[:rows]
        out_ref[q_rows(second), 0:LANE] = grad_q[rows:]

    each_tile(order_ref, tile)
    out_ref[:, LANE : 2 * LANE] = acc_k[...].astype(BF)
    out_ref[:, 2 * LANE :] = acc_v[...].astype(BF)


def attend_back(qkv, mix, grad, lse, order, part, heads, rows):
    length = qkv.shape[0]
    return pl.pallas_call(
        functools.partial(attend_back_kernel, heads, rows),
        out_shape=jax.ShapeDtypeStruct((length, 3 * LANE), BF),
        in_specs=in_smem(2) + in_vmem(4),
        out_specs=in_vmem(1)[0],
        scratch_shapes=[pltpu.VMEM((length, LANE), F4), pltpu.VMEM((length, LANE), F4)],
        compiler_params=pltpu.CompilerParams(vmem_limit_bytes=60 << 20),
        cost_estimate=pl.CostEstimate(
            flops=45_000_000_000, bytes_accessed=20_000_000, transcendentals=9_000_000
        ),
        name="tree_attend_back",
    )(order, part, qkv, mix, grad, lse)


def project_kernel(place_ref, *refs):
    x_ref, pass_ref, gain_ref, shift_ref, w_ref, b_ref = refs[:6]
    normed_ref, qkv_ref = refs[-2:]
    residual = x_ref[...].astype(F4) + pass_ref[...]
    normal, _ = norm_stats(residual)
    normed = (normal * gain_ref[...] + shift_ref[...]).astype(BF)
    normed_ref[...] = normed
    qkv_ref[...] = (dot(normed, w_ref[...]) + b_ref[...]).astype(BF)


def project(rows, place, offset, length, pass_embed, gain, shift, weight, bias, before=None):
    width = weight.shape[1]
    depth = rows.shape[1]
    vec = pl.BlockSpec((1, depth), lambda i, place: (0, 0))
    specs = [
        pl.BlockSpec((BLK, depth), lambda i, place: (place[i], 0)),
        vec,
        vec,
        vec,
        pl.BlockSpec((depth, width), lambda i, place: (0, 0)),
        pl.BlockSpec((1, width), lambda i, place: (0, 0)),
    ]
    operands = [rows, pass_embed[None], gain[None], shift[None], weight, bias[None]]
    aliases = {}
    if before is not None:
        specs += [pl.BlockSpec(memory_space=pl.ANY)] * 2
        operands += list(before)
        aliases = {7: 0, 8: 1}
    count = rows.shape[0] // BLK
    return pl.pallas_call(
        project_kernel,
        out_shape=(
            jax.ShapeDtypeStruct((length, depth), BF),
            jax.ShapeDtypeStruct((length, width), BF),
        ),
        grid_spec=pltpu.PrefetchScalarGridSpec(
            num_scalar_prefetch=1,
            grid=(count,),
            in_specs=specs,
            out_specs=(
                pl.BlockSpec((BLK, depth), lambda i, place: (offset + i, 0)),
                pl.BlockSpec((BLK, width), lambda i, place: (offset + i, 0)),
            ),
        ),
        input_output_aliases=aliases,
        compiler_params=pltpu.CompilerParams(vmem_limit_bytes=24 << 20),
        cost_estimate=pl.CostEstimate(
            flops=2 * rows.shape[0] * depth * width,
            bytes_accessed=rows.shape[0] * (2 * depth + width) * 2,
            transcendentals=rows.shape[0],
        ),
        name="norm_project",
    )(place, *operands)


def send(values, axis, partner):
    size = lax.axis_size(axis)
    return lax.ppermute(values, axis, [(i, partner(i)) for i in range(size)])


def hop(values, step):
    return send(values, "tensor", lambda i: i ^ step)


def cross(values):
    return send(values, "seq", lambda i: i ^ 1)


def add_low(left, right):
    return (left.astype(F4) + right.astype(F4)).astype(BF)


def slot(values, index, size, axis=0):
    return lax.dynamic_slice_in_dim(values, index * size, size, axis)


class Paired:
    def __init__(self, block_len):
        self.me = lax.axis_index("seq")
        self.rank = lax.axis_index("tensor")
        self.sub = block_len // 4
        self.per = self.sub // BLK

    def position(self, natural, blocks):
        half = blocks // 2
        s, b = natural // half, natural % half
        return half * (s ^ self.me) + self.per * ((b // self.per) ^ self.rank) + b % self.per

    def near(self, values):
        return jnp.concatenate([slot(values, self.rank ^ r, self.sub) for r in range(4)], 0)

    def place(self, count):
        spot = jnp.arange(count, dtype=jnp.int32)
        return self.per * ((spot // self.per) ^ self.rank) + spot % self.per

    def far(self, values):
        mine = cross(slot(values, self.rank, self.sub))
        return self.spread(mine)

    def spread(self, own):
        core = hop(own, 1)
        other = hop(own, 2)
        diag = hop(other, 1)
        return jnp.concatenate([own, core, other, diag], 0)

    def gather_weight(self, own):
        return jnp.concatenate([own, hop(own, 1), hop(own, 2), hop(own, 3)], 0)

    def collect(self, partial):
        size = partial.shape[0] // 4
        piece = [partial[r * size : (r + 1) * size] for r in range(4)]
        got = hop(jnp.concatenate([piece[1], piece[3]], 0), 1)
        away = hop(add_low(piece[2], got[size:]), 2)
        return piece[0].astype(F4) + got[:size].astype(F4) + away.astype(F4)

    def collect_all(self, partial):
        size = partial.shape[0] // 8
        piece = partial.reshape(2, 2, 2, size, partial.shape[1])
        got = hop(piece[:, :, 1], 1)
        chip = add_low(piece[:, :, 0], got)
        got = cross(chip[1])
        pair = add_low(chip[0], got)
        away = hop(pair[1], 2)
        return pair[0].astype(F4) + away.astype(F4)

    def to_tokens(self, mixture):
        blocks, rows, width = mixture.shape
        piece = mixture.reshape(2, 4, self.per, rows, width)
        columns = []
        for r in range(4):
            here = piece[0, r] if r == 0 else self.both(piece[0, r], 0, r)
            there = self.both(piece[1, r], 1, r)
            first = jnp.where(self.me == 0, here, there)
            second = jnp.where(self.me == 0, there, here)
            columns.append(jnp.stack([first, second], 1).reshape(self.sub, width))
        return jnp.concatenate(columns, 1)

    def to_heads(self, grads, rows):
        width = grads.shape[1] // 4
        parts = grads.reshape(self.per, 2, rows, 4, width)
        mine = jnp.where(self.me == 0, parts[:, 0], parts[:, 1])
        theirs = jnp.where(self.me == 0, parts[:, 1], parts[:, 0])
        here = [
            mine[:, :, r] if r == 0 else self.both(mine[:, :, r], 0, r) for r in range(4)
        ]
        there = [self.both(theirs[:, :, r], 1, r) for r in range(4)]
        return jnp.concatenate(here + there, 0)

    def both(self, values, step_seq, step_tensor):
        return send(
            values, ("seq", "tensor"), lambda i: (i // 4 ^ step_seq) * 4 + (i % 4 ^ step_tensor)
        )


class Plain:
    def __init__(self, block_len):
        self.me = lax.axis_index("seq")
        self.rank = lax.axis_index("tensor")
        self.sub = block_len // lax.axis_size("tensor")
        self.seq = lax.axis_size("seq")
        self.tensor = lax.axis_size("tensor")

    def position(self, natural, blocks):
        return natural

    def near(self, values):
        return values

    def place(self, count):
        return jnp.arange(count, dtype=jnp.int32)

    def spread(self, own):
        return lax.all_gather(own, "tensor", axis=0, tiled=True)

    def gather_weight(self, own):
        return lax.all_gather(own, "tensor", axis=0, tiled=True)

    def collect(self, partial):
        return lax.psum_scatter(partial, "tensor", scatter_dimension=0, tiled=True).astype(F4)

    def collect_all(self, partial):
        return lax.psum_scatter(
            partial, ("seq", "tensor"), scatter_dimension=0, tiled=True
        ).astype(F4)

    def to_tokens(self, mixture):
        blocks, rows, width = mixture.shape
        full = lax.all_gather(mixture, ("seq", "tensor"), axis=0)
        full = full.reshape(self.seq, self.tensor, blocks, rows, width)
        full = full.transpose(2, 0, 3, 1, 4).reshape(blocks * self.seq * rows, -1)
        return slot(full, self.me * self.tensor + self.rank, self.sub)

    def to_heads(self, grads, rows):
        full = lax.all_gather(grads, ("seq", "tensor"), axis=0, tiled=True)
        full = full.reshape(-1, self.seq, rows, self.tensor, grads.shape[1] // self.tensor)
        part = slot(full, self.me, 1, 1)[:, 0]
        return slot(part, self.rank, 1, 2)[:, :, 0]


def tree_order(seg_row, parent_row, position):
    blocks = seg_row.shape[0] // BLK
    segs = parent_row.shape[0]
    slot_seg = seg_row[::BLK]
    labels = jnp.arange(segs, dtype=jnp.int32)
    above = jnp.sum(jnp.where(slot_seg[:, None] == labels[None, :], parent_row[None, :], 0), 1)
    natural = jnp.arange(blocks, dtype=jnp.int32)
    key = jnp.where(
        slot_seg == 0,
        natural,
        jnp.where(above == 0, 100 + slot_seg, 1000 + 16 * above + slot_seg),
    )
    rank = jnp.sum((key[None, :] < key[:, None]).astype(jnp.int32), 1)
    where = position(natural, blocks)
    order = jnp.sum(jnp.where(rank[:, None] == natural[None, :], where[:, None], 0), 0)
    base = order[0] // TRUNK_BLOCKS * TRUNK_BLOCKS
    return jnp.concatenate([order, base[None]]).astype(jnp.int32)


def padded(values, axis):
    widths = [(0, 0)] * values.ndim
    widths[axis] = (0, LANE - values.shape[axis])
    return jnp.pad(values, widths)


def total(values):
    return jnp.sum(values, axis=0)


def reduce_grads(arrays):
    low = [a.astype(BF) for a in arrays]
    return [a.astype(F4) for a in lax.psum(low, ("dp", "seq"))]


def local(
    inputs,
    pass_embed,
    norm1_gain,
    norm1_shift,
    w_qkv,
    b_qv,
    w_out,
    b_out,
    norm2_gain,
    norm2_shift,
    w_up,
    b_up,
    w_down,
    b_down,
    out_grad,
    seg_id,
    parent,
):
    x = inputs[0]
    dy_block = out_grad[0]
    block_len, depth = x.shape
    length = seg_id.shape[1]
    seq, tensor = lax.axis_size("seq"), lax.axis_size("tensor")
    width = w_qkv.shape[2]
    heads = width // HD
    rows = BLK // seq
    paired = seq == 2 and tensor == 4 and block_len % (4 * BLK) == 0
    move = Paired(block_len) if paired else Plain(block_len)

    order = tree_order(seg_id[0], parent[0], move.position)
    part = move.me[None].astype(jnp.int32)

    w_cols = jnp.concatenate([padded(w_qkv[i], 1) for i in range(3)], 1)
    zero = jnp.zeros((LANE,), F4)
    b_cols = jnp.concatenate([padded(b_qv[0], 0), zero, padded(b_qv[1], 0)])
    norm_args = (length, pass_embed, norm1_gain, norm1_shift, w_cols, b_cols)
    if paired:
        far = move.far(x)
        count = block_len // BLK
        made = project(x, move.place(count), 0, *norm_args)
        straight = jnp.arange(count, dtype=jnp.int32)
        normed, qkv = project(far, straight, count, *norm_args, before=made)
    else:
        full = lax.all_gather(x, "seq", axis=0, tiled=True)
        normed, qkv = project(full, move.place(length // BLK), 0, *norm_args)

    mixture, lse = attend(qkv, order, part, heads, rows)

    out_weight = move.gather_weight(w_out)
    mix_own = move.to_tokens(mixture)
    x_own = slot(x, move.rank, move.sub)
    dy_own = slot(dy_block, move.rank, move.sub).astype(F4)
    residual = x_own.astype(F4) + pass_embed
    middle = residual + dot(mix_own, out_weight) + b_out
    norm_two, inv_two = norm_stats(middle)
    lifted = move.spread((norm_two * norm2_gain + norm2_shift).astype(BF))

    dy = move.near(dy_block)
    pre_act = dot(lifted, w_up) + b_up
    gelu_value, gelu_slope = gelu_parts(pre_act)
    active = gelu_value.astype(BF)
    grad_pre = (dot(dy, w_down, NT) * gelu_slope).astype(BF)
    grad_lift = move.collect(dot(grad_pre, w_up, NT).astype(BF))
    output = (middle + move.collect(dot(active, w_down).astype(BF)) + b_down).astype(BF)
    grad_w_down = dot(active, dy, TN)
    grad_w_up = dot(lifted, grad_pre, TN)
    grad_b_up = total(grad_pre.astype(F4))

    grad_middle = dy_own + norm_back(grad_lift, norm_two, inv_two, norm2_gain)
    proj_low = grad_middle.astype(BF)
    grad_mix = move.to_heads(dot(proj_low, out_weight, NT).astype(BF), rows)
    grad_w_out = move.collect(dot(mix_own, proj_low, TN).astype(BF))

    grad_w_up, grad_w_down, grad_w_out = reduce_grads([grad_w_up, grad_w_down, grad_w_out])

    grads = attend_back(qkv, mixture, grad_mix, lse, order, part, heads, rows)

    grad_w_cols = dot(normed, grads, TN)
    grad_norm = move.collect_all(dot(grads, w_cols, NT).astype(BF))
    (grad_w_cols,) = reduce_grads([grad_w_cols])
    grad_w_qkv = jnp.stack([grad_w_cols[:, i * LANE : i * LANE + width] for i in range(3)])
    sums = total(grads.astype(F4))
    grad_b_qv = jnp.stack([sums[:width], sums[2 * LANE : 2 * LANE + width]])

    norm_one, inv_one = norm_stats(residual)
    grad_resid = grad_middle + norm_back(grad_norm, norm_one, inv_one, norm1_gain)
    input_grad = grad_resid.astype(BF)

    own_sums = jnp.stack(
        [
            total(grad_resid),
            total(grad_norm * norm_one),
            total(grad_norm),
            total(grad_middle),
            total(grad_lift * norm_two),
            total(grad_lift),
            total(dy_own),
        ]
    )
    own_sums = lax.psum(own_sums, ("dp", "seq", "tensor"))
    grad_b_qv, grad_b_up = lax.psum((grad_b_qv, grad_b_up), ("dp", "seq"))
    return (
        output[None],
        input_grad[None],
        own_sums[0],
        own_sums[1],
        own_sums[2],
        grad_w_qkv,
        grad_b_qv,
        grad_w_out,
        own_sums[3],
        own_sums[4],
        own_sums[5],
        grad_w_up,
        grad_b_up,
        grad_w_down,
        own_sums[6],
    )


def solution(mesh):
    return jax.shard_map(
        local,
        mesh=mesh,
        in_specs=(
            P("dp", "seq", None),
            P(),
            P(),
            P(),
            P(None, None, "tensor"),
            P(None, "tensor"),
            P("tensor", None),
            P(),
            P(),
            P(),
            P(None, "tensor"),
            P("tensor"),
            P("tensor", None),
            P(),
            P("dp", "seq", None),
            P("dp", None),
            P("dp", None),
        ),
        out_specs=(
            P("dp", ("seq", "tensor"), None),
            P("dp", ("seq", "tensor"), None),
            P(),
            P(),
            P(),
            P(None, None, "tensor"),
            P(None, "tensor"),
            P("tensor", None),
            P(),
            P(),
            P(),
            P(None, "tensor"),
            P("tensor"),
            P("tensor", None),
            P(),
        ),
        check_vma=False,
    )
```

```python
import functools

import jax
import jax.numpy as jnp
from jax import lax
from jax.experimental import pallas as pl
from jax.experimental.pallas import tpu as pltpu
from jax.sharding import PartitionSpec as P

HD = 64
BLK = 256
TRUNK_BLOCKS = 4
LANE = 256
EPS = 1e-05
ROOT = 0.7978845608028654
BF = jnp.bfloat16
F4 = jnp.float32
NT = (((1,), (1,)), ((), ()))
NN = (((1,), (0,)), ((), ()))
TN = (((0,), (0,)), ((), ()))


def dot(left, right, dims=NN):
    return lax.dot_general(left, right, dims, preferred_element_type=F4)


def norm_stats(values):
    row_mean = jnp.mean(values, -1, keepdims=True)
    centred = values - row_mean
    inv_std = lax.rsqrt(jnp.mean(centred * centred, -1, keepdims=True) + EPS)
    return (centred * inv_std, inv_std)


def norm_back(grad_out, normal, inv_std, gain_vec):
    scaled = grad_out * gain_vec
    return inv_std * (
        scaled
        - jnp.mean(scaled, -1, keepdims=True)
        - normal * jnp.mean(scaled * normal, -1, keepdims=True)
    )


def gelu_parts(pre_act):
    cubic_term = 0.044715 * pre_act * pre_act * pre_act
    tangent = jnp.tanh(ROOT * (pre_act + cubic_term))
    gelu_value = 0.5 * pre_act * (1.0 + tangent)
    gelu_slope = 0.5 * (1.0 + tangent) + 0.5 * pre_act * (1.0 - tangent * tangent) * ROOT * (
        1.0 + 3.0 * 0.044715 * pre_act * pre_act
    )
    return (gelu_value, gelu_slope)


def block_rows(pos, count=1):
    return pl.ds(pl.multiple_of(pos * BLK, BLK), count * BLK)


def head_masks(shape, heads):
    lane = lax.broadcasted_iota(jnp.int32, shape, 1) // HD
    return [lane == h for h in range(heads)]


def each_tile(order_ref, tile):
    trunk = [order_ref[i] for i in range(TRUNK_BLOCKS)]
    base = order_ref[16]
    tile(trunk[0], trunk[1], [], [(trunk[0], True)], [(trunk[0], False), (trunk[1], True)])
    tile(
        trunk[2],
        trunk[3],
        [(trunk[0], 2)],
        [(trunk[2], True)],
        [(trunk[2], False), (trunk[3], True)],
    )

    def branch(i, carry):
        one, two = order_ref[4 + 2 * i], order_ref[5 + 2 * i]
        tile(one, two, [(base, 4)], [(one, True)], [(two, True)])
        return carry

    lax.fori_loop(0, 2, branch, 0)

    def leaf(i, carry):
        one, two = order_ref[8 + 2 * i], order_ref[9 + 2 * i]
        tile(one, two, [(base, 4), (order_ref[4 + i], 1)], [(one, True)], [(two, True)])
        return carry

    lax.fori_loop(0, 4, leaf, 0)


def attend_kernel(heads, rows, order_ref, part_ref, qkv_ref, out_ref, lse_ref):
    part = part_ref[0]

    def q_at(pos):
        return qkv_ref[pl.ds(pl.multiple_of(pos * BLK + part * rows, rows), rows), 0:LANE]

    def k_at(pos, count=1):
        return qkv_ref[block_rows(pos, count), LANE : 2 * LANE]

    def v_at(pos, count=1):
        return qkv_ref[block_rows(pos, count), 2 * LANE : 3 * LANE]

    row_at = lax.broadcasted_iota(jnp.int32, (rows, BLK), 0) + part * rows
    causal = row_at >= lax.broadcasted_iota(jnp.int32, (rows, BLK), 1)
    masks = head_masks((2 * rows, LANE), heads)

    def tile(first, second, shared, parts_a, parts_b):
        q = jnp.concatenate([q_at(first), q_at(second)], 0) * BF(0.125)
        result = jnp.zeros((2 * rows, LANE), F4)
        log_cols = []
        for h in range(heads):
            qm = jnp.where(masks[h], q, BF(0))
            halves = [qm[:rows], qm[rows:]]
            wide = [dot(qm, k_at(p, c), NT) for p, c in shared]
            own = [
                [
                    jnp.where(causal, dot(halves[i], k_at(p), NT), -jnp.inf)
                    if diag
                    else dot(halves[i], k_at(p), NT)
                    for p, diag in parts
                ]
                for i, parts in enumerate((parts_a, parts_b))
            ]
            tops = []
            for i in range(2):
                tops.append(
                    functools.reduce(
                        jnp.maximum,
                        [
                            jnp.max(s, 1, keepdims=True)
                            for s in [w[i * rows : (i + 1) * rows] for w in wide] + own[i]
                        ],
                    )
                )
            top = jnp.concatenate(tops, 0)
            mix = jnp.zeros((2 * rows, LANE), F4)
            total = jnp.zeros((2 * rows, 1), F4)
            for s, (p, c) in zip(wide, shared):
                e = jnp.exp(s - top)
                total = total + jnp.sum(e, 1, keepdims=True)
                mix = mix + dot(e.astype(BF), v_at(p, c))
            extra = []
            sums = []
            for i, parts in enumerate((parts_a, parts_b)):
                m_i = jnp.zeros((rows, LANE), F4)
                t_i = jnp.zeros((rows, 1), F4)
                for s, (p, _) in zip(own[i], parts):
                    e = jnp.exp(s - tops[i])
                    t_i = t_i + jnp.sum(e, 1, keepdims=True)
                    m_i = m_i + dot(e.astype(BF), v_at(p))
                extra.append(m_i)
                sums.append(t_i)
            total = total + jnp.concatenate(sums, 0)
            mix = (mix + jnp.concatenate(extra, 0)) / total
            result = jnp.where(masks[h], mix, result)
            log_cols.append(top + jnp.log(total))
        low = result.astype(BF)[:, : heads * HD]
        out_ref[first] = low[:rows]
        out_ref[second] = low[rows:]
        lane = lax.broadcasted_iota(jnp.int32, (2 * rows, 128), 1)
        cols = jnp.zeros((2 * rows, 128), F4)
        for h in range(heads):
            cols = jnp.where(lane == h, log_cols[h], cols)
        flat = jnp.transpose(cols)[:8]
        lse_ref[first] = flat[:, :rows]
        lse_ref[second] = flat[:, rows:]

    each_tile(order_ref, tile)


def in_vmem(count):
    return [pl.BlockSpec(memory_space=pltpu.VMEM)] * count


def in_smem(count):
    return [pl.BlockSpec(memory_space=pltpu.SMEM)] * count


def attend(qkv, order, part, heads, rows):
    blocks = qkv.shape[0] // BLK
    return pl.pallas_call(
        functools.partial(attend_kernel, heads, rows),
        out_shape=(
            jax.ShapeDtypeStruct((blocks, rows, heads * HD), BF),
            jax.ShapeDtypeStruct((blocks, 8, rows), F4),
        ),
        in_specs=in_smem(2) + in_vmem(1),
        out_specs=in_vmem(2),
        compiler_params=pltpu.CompilerParams(vmem_limit_bytes=56 << 20),
        cost_estimate=pl.CostEstimate(
            flops=25_000_000_000, bytes_accessed=10_000_000, transcendentals=9_000_000
        ),
        name="tree_attend",
    )(order, part, qkv)


def attend_back_kernel(
    heads, rows, order_ref, part_ref, qkv_ref, mix_ref, grad_ref, lse_ref, out_ref, acc_k, acc_v
):
    part = part_ref[0]
    width = heads * HD

    def q_rows(pos):
        return pl.ds(pl.multiple_of(pos * BLK + part * rows, rows), rows)

    def k_at(pos, count=1):
        return qkv_ref[block_rows(pos, count), LANE : 2 * LANE]

    def v_at(pos, count=1):
        return qkv_ref[block_rows(pos, count), 2 * LANE : 3 * LANE]

    key_at = lax.broadcasted_iota(jnp.int32, (BLK, rows), 0)
    causal = (lax.broadcasted_iota(jnp.int32, (BLK, rows), 1) + part * rows) >= key_at
    masks = head_masks((2 * rows, LANE), heads)
    acc_k[...] = jnp.zeros_like(acc_k)
    acc_v[...] = jnp.zeros_like(acc_v)
    out_ref[:, 0:LANE] = jnp.zeros((out_ref.shape[0], LANE), BF)
    pick = (
        lax.broadcasted_iota(jnp.int32, (8, LANE), 1) // HD
        == lax.broadcasted_iota(jnp.int32, (8, LANE), 0)
    ).astype(BF)
    pad = jnp.zeros((2 * rows, LANE - width), BF)

    def tile(first, second, shared, parts_a, parts_b):
        q = jnp.concatenate(
            [qkv_ref[q_rows(first), 0:LANE], qkv_ref[q_rows(second), 0:LANE]], 0
        ) * BF(0.125)
        grad = jnp.concatenate([jnp.concatenate([grad_ref[first], grad_ref[second]], 0), pad], 1)
        mix = jnp.concatenate([jnp.concatenate([mix_ref[first], mix_ref[second]], 0), pad], 1)
        inner = dot(pick, (grad.astype(F4) * mix.astype(F4)).astype(BF), NT)
        lse = jnp.concatenate([lse_ref[first], lse_ref[second]], 1)
        qms = [jnp.where(masks[h], q, BF(0)) for h in range(heads)]
        gms = [jnp.where(masks[h], grad, BF(0)) for h in range(heads)]

        def pieces(keys, values, h, cut, diag):
            e = jnp.exp(dot(keys, qms[h][cut], NT) - lse[h : h + 1, cut])
            if diag:
                e = jnp.where(causal, e, 0.0)
            t = dot(values, gms[h][cut], NT)
            return e.astype(BF), (e * (t - inner[h : h + 1, cut])).astype(BF)

        def strip(pos, count, cut, diag, grad_q):
            keys, values = k_at(pos, count), v_at(pos, count)
            es = []
            ds = []
            for h in range(heads):
                e, d = pieces(keys, values, h, cut, diag)
                es.append(e)
                ds.append(d)
                grad_q = grad_q + jnp.where(masks[h][cut], dot(d, keys, TN), 0.0)
            acc_v[block_rows(pos, count), :] += dot(
                jnp.concatenate(es, 1), jnp.concatenate([g[cut] for g in gms], 0)
            )
            acc_k[block_rows(pos, count), :] += dot(
                jnp.concatenate(ds, 1), jnp.concatenate([g[cut] for g in qms], 0)
            )
            return grad_q

        grad_q = jnp.zeros((2 * rows, LANE), F4)
        for pos, count in shared:
            grad_q = strip(pos, count, slice(0, 2 * rows), False, grad_q)
        halves = []
        for i, parts in enumerate((parts_a, parts_b)):
            half = jnp.zeros((rows, LANE), F4)
            for pos, diag in parts:
                half = strip(pos, 1, slice(i * rows, (i + 1) * rows), diag, half)
            halves.append(half)
        grad_q = ((grad_q + jnp.concatenate(halves, 0)) * 0.125).astype(BF)
        out_ref[q_rows(first), 0:LANE] = grad_q[:rows]
        out_ref[q_rows(second), 0:LANE] = grad_q[rows:]

    each_tile(order_ref, tile)
    out_ref[:, LANE : 2 * LANE] = acc_k[...].astype(BF)
    out_ref[:, 2 * LANE :] = acc_v[...].astype(BF)


def attend_back(qkv, mix, grad, lse, order, part, heads, rows):
    length = qkv.shape[0]
    return pl.pallas_call(
        functools.partial(attend_back_kernel, heads, rows),
        out_shape=jax.ShapeDtypeStruct((length, 3 * LANE), BF),
        in_specs=in_smem(2) + in_vmem(4),
        out_specs=in_vmem(1)[0],
        scratch_shapes=[pltpu.VMEM((length, LANE), F4), pltpu.VMEM((length, LANE), F4)],
        compiler_params=pltpu.CompilerParams(vmem_limit_bytes=60 << 20),
        cost_estimate=pl.CostEstimate(
            flops=45_000_000_000, bytes_accessed=20_000_000, transcendentals=9_000_000
        ),
        name="tree_attend_back",
    )(order, part, qkv, mix, grad, lse)


def project_kernel(place_ref, *refs):
    x_ref, pass_ref, gain_ref, shift_ref, w_ref, b_ref = refs[:6]
    normed_ref, qkv_ref = refs[-2:]
    residual = x_ref[...].astype(F4) + pass_ref[...]
    normal, _ = norm_stats(residual)
    normed = (normal * gain_ref[...] + shift_ref[...]).astype(BF)
    normed_ref[...] = normed
    qkv_ref[...] = (dot(normed, w_ref[...]) + b_ref[...]).astype(BF)


def project(rows, place, offset, length, pass_embed, gain, shift, weight, bias, before=None):
    width = weight.shape[1]
    depth = rows.shape[1]
    vec = pl.BlockSpec((1, depth), lambda i, place: (0, 0))
    specs = [
        pl.BlockSpec((BLK, depth), lambda i, place: (place[i], 0)),
        vec,
        vec,
        vec,
        pl.BlockSpec((depth, width), lambda i, place: (0, 0)),
        pl.BlockSpec((1, width), lambda i, place: (0, 0)),
    ]
    operands = [rows, pass_embed[None], gain[None], shift[None], weight, bias[None]]
    aliases = {}
    if before is not None:
        specs += [pl.BlockSpec(memory_space=pl.ANY)] * 2
        operands += list(before)
        aliases = {7: 0, 8: 1}
    count = rows.shape[0] // BLK
    return pl.pallas_call(
        project_kernel,
        out_shape=(
            jax.ShapeDtypeStruct((length, depth), BF),
            jax.ShapeDtypeStruct((length, width), BF),
        ),
        grid_spec=pltpu.PrefetchScalarGridSpec(
            num_scalar_prefetch=1,
            grid=(count,),
            in_specs=specs,
            out_specs=(
                pl.BlockSpec((BLK, depth), lambda i, place: (offset + i, 0)),
                pl.BlockSpec((BLK, width), lambda i, place: (offset + i, 0)),
            ),
        ),
        input_output_aliases=aliases,
        compiler_params=pltpu.CompilerParams(vmem_limit_bytes=24 << 20),
        cost_estimate=pl.CostEstimate(
            flops=2 * rows.shape[0] * depth * width,
            bytes_accessed=rows.shape[0] * (2 * depth + width) * 2,
            transcendentals=rows.shape[0],
        ),
        name="norm_project",
    )(place, *operands)


def vec_spec(depth):
    return pl.BlockSpec((1, depth), lambda i, at: (0, 0))


def own_rows_spec(depth, step, fixed=False):
    if fixed:
        return pl.BlockSpec((step, depth), lambda i, at: (at[0] + i, 0))
    return pl.BlockSpec((step, depth), lambda i, at: (i, 0))


def pieces_spec(count, step, width):
    return pl.BlockSpec((count, step, width), lambda i, at: (0, i, 0))


def whole_spec(shape):
    return pl.BlockSpec(shape, lambda i, at: (0,) * len(shape))


def grid_of(steps, ins, outs, scratch=()):
    return pltpu.PrefetchScalarGridSpec(
        num_scalar_prefetch=1,
        grid=(steps,),
        in_specs=ins,
        out_specs=outs,
        scratch_shapes=list(scratch),
    )


def own_forward_kernel(
    count, at_ref, x_ref, pass_ref, mix_ref, w_ref, b_ref, gain_ref, shift_ref, mid_ref, lift_ref
):
    middle = x_ref[...].astype(F4) + pass_ref[...] + b_ref[...]
    for r in range(count):
        middle = middle + dot(mix_ref[r], w_ref[r])
    mid_ref[...] = middle
    normal, _ = norm_stats(middle)
    lift_ref[...] = (normal * gain_ref[...] + shift_ref[...]).astype(BF)


def own_forward(x, at, pass_embed, mixed, weight, bias, gain, shift):
    count, sub, width = mixed.shape
    depth = x.shape[1]
    step = 128
    vec = vec_spec(depth)
    return pl.pallas_call(
        functools.partial(own_forward_kernel, count),
        out_shape=(
            jax.ShapeDtypeStruct((sub, depth), F4),
            jax.ShapeDtypeStruct((sub, depth), BF),
        ),
        grid_spec=grid_of(
            sub // step,
            [
                own_rows_spec(depth, step, True),
                vec,
                pieces_spec(count, step, width),
                whole_spec(weight.shape),
                vec,
                vec,
                vec,
            ],
            (own_rows_spec(depth, step), own_rows_spec(depth, step)),
        ),
        cost_estimate=pl.CostEstimate(
            flops=2 * sub * depth * depth, bytes_accessed=sub * depth * 10, transcendentals=sub
        ),
        name="own_forward",
    )(at * (sub // step), x, pass_embed[None], mixed, weight, bias[None], gain[None], shift[None])


def own_backward_kernel(count, parts, at_ref, *refs):
    grad_parts = refs[:parts]
    mid_ref, dy_ref, gain_ref, w_ref, mix_ref, gm_ref, gmix_ref, gw_ref, sums_ref, acc = refs[parts:]
    step = pl.program_id(0)

    @pl.when(step == 0)
    def _():
        acc[...] = jnp.zeros_like(acc)
        sums_ref[...] = jnp.zeros_like(sums_ref)

    grad_lift = functools.reduce(jnp.add, [g[...].astype(F4) for g in grad_parts])
    normal, inv = norm_stats(mid_ref[...])
    dy = dy_ref[...].astype(F4)
    grad_middle = dy + norm_back(grad_lift, normal, inv, gain_ref[...])
    gm_ref[...] = grad_middle
    low = grad_middle.astype(BF)
    for r in range(count):
        gmix_ref[r] = dot(low, w_ref[r], NT).astype(BF)
        acc[r] += dot(mix_ref[r], low, TN)
    for i, values in enumerate((grad_middle, grad_lift * normal, grad_lift, dy)):
        sums_ref[i : i + 1, :] += jnp.sum(values, 0, keepdims=True)

    @pl.when(step == pl.num_programs(0) - 1)
    def _():
        gw_ref[...] = acc[...].astype(BF)


def own_backward(grad_parts, middle, dy, at, gain, weight, mixed):
    count, sub, width = mixed.shape
    depth = dy.shape[1]
    step = 128
    rows = own_rows_spec(depth, step)
    return pl.pallas_call(
        functools.partial(own_backward_kernel, count, len(grad_parts)),
        out_shape=(
            jax.ShapeDtypeStruct((sub, depth), F4),
            jax.ShapeDtypeStruct((count, sub, width), BF),
            jax.ShapeDtypeStruct((count, width, depth), BF),
            jax.ShapeDtypeStruct((8, depth), F4),
        ),
        grid_spec=grid_of(
            sub // step,
            [rows] * len(grad_parts)
            + [
                rows,
                own_rows_spec(depth, step, True),
                vec_spec(depth),
                whole_spec(weight.shape),
                pieces_spec(count, step, width),
            ],
            (
                rows,
                pieces_spec(count, step, width),
                whole_spec((count, width, depth)),
                whole_spec((8, depth)),
            ),
            [pltpu.VMEM((count, width, depth), F4)],
        ),
        cost_estimate=pl.CostEstimate(
            flops=4 * sub * depth * depth, bytes_accessed=sub * depth * 20, transcendentals=sub
        ),
        name="own_backward",
    )(at * (sub // step), *grad_parts, middle, dy, gain[None], weight, mixed)


def last_norm_kernel(counts, at_ref, *refs):
    split = counts[0]
    left, right = refs[:split], refs[split : split + counts[1]]
    x_ref, pass_ref, gain_ref, gm_ref, out_ref, sums_ref = refs[split + counts[1] :]

    @pl.when(pl.program_id(0) == 0)
    def _():
        sums_ref[...] = jnp.zeros_like(sums_ref)

    grad_norm = jnp.concatenate(
        [functools.reduce(jnp.add, [g[...].astype(F4) for g in side]) for side in (left, right)], 1
    )
    normal, inv = norm_stats(x_ref[...].astype(F4) + pass_ref[...])
    grad_resid = gm_ref[...] + norm_back(grad_norm, normal, inv, gain_ref[...])
    out_ref[...] = grad_resid.astype(BF)
    for i, values in enumerate((grad_resid, grad_norm * normal, grad_norm)):
        sums_ref[i : i + 1, :] += jnp.sum(values, 0, keepdims=True)


def last_norm(left, right, x, at, pass_embed, gain, grad_middle):
    sub, depth = grad_middle.shape
    step = 128
    return pl.pallas_call(
        functools.partial(last_norm_kernel, (len(left), len(right))),
        out_shape=(
            jax.ShapeDtypeStruct((sub, depth), BF),
            jax.ShapeDtypeStruct((8, depth), F4),
        ),
        grid_spec=grid_of(
            sub // step,
            [own_rows_spec(depth // 2, step)] * (len(left) + len(right))
            + [
                own_rows_spec(depth, step, True),
                vec_spec(depth),
                vec_spec(depth),
                own_rows_spec(depth, step),
            ],
            (own_rows_spec(depth, step), whole_spec((8, depth))),
        ),
        name="last_norm",
    )(at * (sub // step), *left, *right, x, pass_embed[None], gain[None], grad_middle)


def units_kernel(place_ref, *refs):
    lift_ref, dy_ref, up_ref, bias_ref, down_ref = refs[:5]
    keep_ref, active_ref, pre_ref, glift_ref, out_ref = refs[-5:]
    lifted = lift_ref[...]
    keep_ref[...] = lifted
    pre_act = dot(lifted, up_ref[...]) + bias_ref[...]
    value, slope = gelu_parts(pre_act)
    active = value.astype(BF)
    active_ref[...] = active
    grad_pre = (dot(dy_ref[...], down_ref[...], NT) * slope).astype(BF)
    pre_ref[...] = grad_pre
    glift_ref[...] = dot(grad_pre, up_ref[...], NT).astype(BF)
    out_ref[...] = dot(active, down_ref[...]).astype(BF)


def units(lifted, dy, place, w_up, b_up, w_down, before=None):
    rows, depth = lifted.shape
    length = dy.shape[0]
    wide = w_up.shape[1]
    step = min(BLK, rows)
    near = pl.BlockSpec((step, depth), lambda i, place: (i, 0))
    spot = pl.BlockSpec((step, depth), lambda i, place: (place[i], 0))
    spot_wide = pl.BlockSpec((step, wide), lambda i, place: (place[i], 0))
    specs = [near, spot, whole_spec(w_up.shape), vec_spec(wide), whole_spec(w_down.shape)]
    operands = [lifted, dy, w_up, b_up[None], w_down]
    aliases = {}
    if before is not None:
        specs += [pl.BlockSpec(memory_space=pl.ANY)] * 3
        operands += list(before)
        aliases = {6: 0, 7: 1, 8: 2}
    return pl.pallas_call(
        units_kernel,
        out_shape=(
            jax.ShapeDtypeStruct((length, depth), BF),
            jax.ShapeDtypeStruct((length, wide), BF),
            jax.ShapeDtypeStruct((length, wide), BF),
            jax.ShapeDtypeStruct((rows, depth), BF),
            jax.ShapeDtypeStruct((rows, depth), BF),
        ),
        grid_spec=grid_of(rows // step, specs, (spot, spot_wide, spot_wide, near, near)),
        input_output_aliases=aliases,
        compiler_params=pltpu.CompilerParams(vmem_limit_bytes=40 << 20),
        cost_estimate=pl.CostEstimate(
            flops=8 * rows * depth * wide,
            bytes_accessed=rows * depth * 14 + 4 * depth * wide,
            transcendentals=rows * wide,
        ),
        name="units",
    )(place, *operands)


def unit_grads_kernel(place_ref, lift_ref, pre_ref, active_ref, dy_ref, up_ref, down_ref, sum_ref, acc_up, acc_down):
    @pl.when(pl.program_id(0) == 0)
    def _():
        acc_up[...] = jnp.zeros_like(acc_up)
        acc_down[...] = jnp.zeros_like(acc_down)
        sum_ref[...] = jnp.zeros_like(sum_ref)

    acc_up[...] += dot(lift_ref[...], pre_ref[...], TN)
    acc_down[...] += dot(active_ref[...], dy_ref[...], TN)
    sum_ref[0:1, :] += jnp.sum(pre_ref[...].astype(F4), 0, keepdims=True)

    @pl.when(pl.program_id(0) == pl.num_programs(0) - 1)
    def _():
        up_ref[...] = acc_up[...].astype(BF)
        down_ref[...] = acc_down[...].astype(BF)


def unit_grads(lifted, grad_pre, active, dy, at):
    rows, depth = lifted.shape
    wide = active.shape[1]
    step = min(512, rows)
    return pl.pallas_call(
        unit_grads_kernel,
        out_shape=(
            jax.ShapeDtypeStruct((depth, wide), BF),
            jax.ShapeDtypeStruct((wide, depth), BF),
            jax.ShapeDtypeStruct((8, wide), F4),
        ),
        grid_spec=grid_of(
            rows // step,
            [
                own_rows_spec(depth, step),
                own_rows_spec(wide, step),
                own_rows_spec(wide, step),
                own_rows_spec(depth, step),
            ],
            (whole_spec((depth, wide)), whole_spec((wide, depth)), whole_spec((8, wide))),
            [pltpu.VMEM((depth, wide), F4), pltpu.VMEM((wide, depth), F4)],
        ),
        compiler_params=pltpu.CompilerParams(vmem_limit_bytes=40 << 20),
        cost_estimate=pl.CostEstimate(
            flops=4 * rows * depth * wide, bytes_accessed=rows * depth * 8, transcendentals=0
        ),
        name="unit_grads",
    )(at, lifted, grad_pre, active, dy)


def norm_grads_kernel(at_ref, grads_ref, w_ref, keep_ref, send_ref):
    low = dot(grads_ref[...], w_ref[...], NT).astype(BF)
    step = pl.program_id(0)

    @pl.when(step % 2 == 0)
    def _():
        keep_ref[...] = low

    @pl.when(step % 2 == 1)
    def _():
        send_ref[...] = low


def norm_grads(grads, weight, at, side, size):
    length, wide = grads.shape
    half = weight.shape[0] // 2
    out = jax.ShapeDtypeStruct((length // 2, half), BF)
    spec = pl.BlockSpec((size, half), lambda i, at: (i // 2, 0))
    return pl.pallas_call(
        norm_grads_kernel,
        out_shape=(out, out),
        grid_spec=grid_of(
            length // size,
            [
                own_rows_spec(wide, size),
                pl.BlockSpec((half, wide), lambda i, at: (side, 0)),
            ],
            (spec, spec),
        ),
        compiler_params=pltpu.CompilerParams(vmem_limit_bytes=24 << 20),
        cost_estimate=pl.CostEstimate(
            flops=2 * length * wide * half, bytes_accessed=length * wide * 3, transcendentals=0
        ),
        name="norm_grads",
    )(at, grads, weight)


def projection_grads_kernel(width, at_ref, normed_ref, grads_ref, out_ref, sum_ref, acc):
    @pl.when(pl.program_id(0) == 0)
    def _():
        acc[...] = jnp.zeros_like(acc)
        sum_ref[...] = jnp.zeros_like(sum_ref)

    acc[...] += dot(normed_ref[...], grads_ref[...], TN)
    sum_ref[0:1, :] += jnp.sum(grads_ref[...].astype(F4), 0, keepdims=True)

    @pl.when(pl.program_id(0) == pl.num_programs(0) - 1)
    def _():
        out_ref[...] = jnp.concatenate(
            [acc[:, i * LANE : i * LANE + width] for i in range(3)], 1
        ).astype(BF)


def projection_grads(normed, grads, width, at):
    length, depth = normed.shape
    wide = grads.shape[1]
    step = 512
    return pl.pallas_call(
        functools.partial(projection_grads_kernel, width),
        out_shape=(
            jax.ShapeDtypeStruct((depth, 3 * width), BF),
            jax.ShapeDtypeStruct((8, wide), F4),
        ),
        grid_spec=grid_of(
            length // step,
            [own_rows_spec(depth, step), own_rows_spec(wide, step)],
            (whole_spec((depth, 3 * width)), whole_spec((8, wide))),
            [pltpu.VMEM((depth, wide), F4)],
        ),
        compiler_params=pltpu.CompilerParams(vmem_limit_bytes=32 << 20),
        cost_estimate=pl.CostEstimate(
            flops=2 * length * depth * wide, bytes_accessed=length * depth * 4, transcendentals=0
        ),
        name="projection_grads",
    )(at, normed, grads)


def send(values, axis, partner):
    size = lax.axis_size(axis)
    return lax.ppermute(values, axis, [(i, partner(i)) for i in range(size)])


def hop(values, step):
    return send(values, "tensor", lambda i: i ^ step)


def cross(values):
    return send(values, "seq", lambda i: i ^ 1)


def both(values, step_seq, step_tensor):
    return send(
        values, ("seq", "tensor"), lambda i: (i // 4 ^ step_seq) * 4 + (i % 4 ^ step_tensor)
    )


def add_low(left, right):
    return (left.astype(F4) + right.astype(F4)).astype(BF)


def slot(values, index, size, axis=0):
    return lax.dynamic_slice_in_dim(values, index * size, size, axis)


class Paired:
    def __init__(self, block_len):
        self.me = lax.axis_index("seq")
        self.rank = lax.axis_index("tensor")
        self.sub = block_len // 4
        self.per = self.sub // BLK

    def position(self, natural, blocks):
        half = blocks // 2
        s, b = natural // half, natural % half
        return half * (s ^ self.me) + self.per * ((b // self.per) ^ self.rank) + b % self.per

    def place(self, count):
        spot = jnp.arange(count, dtype=jnp.int32)
        return self.per * ((spot // self.per) ^ self.rank) + spot % self.per

    def far(self, values):
        mine = cross(slot(values, self.rank, self.sub))
        return jnp.concatenate(self.spread(mine), 0)

    def spread(self, own):
        core = hop(own, 1)
        other = hop(own, 2)
        diag = hop(other, 1)
        return [own, core, other, diag]

    def unit_places(self):
        spot = jnp.arange(self.per, dtype=jnp.int32)
        return [self.per * (self.rank ^ r) + spot for r in range(4)]

    def gather_weight(self, own):
        return jnp.stack([own, hop(own, 1), hop(own, 2), hop(own, 3)])

    def collect(self, piece):
        away = hop(add_low(piece[2], hop(piece[3], 1)), 2)
        return [piece[0], hop(piece[1], 1), away]

    def collect_all(self, grads, weight):
        chip = []
        for side in range(2):
            keep, away = norm_grads(grads, weight, self.rank[None], side, self.sub)
            chip.append(add_low(keep, hop(away, 1)).reshape(2, 2, self.sub, -1))
        one, two = chip
        one = add_low(one[0], cross(one[1]))
        two = add_low(two[:, 0], hop(two[:, 1], 2))
        return [one[0], hop(one[1], 2)], [two[0], cross(two[1])]

    def sum_small(self, shared, ranked):
        rows = []
        if shared is not None:
            shared = shared + hop(shared, 1)
            rows.append(shared + hop(shared, 2))
        if ranked is not None:
            rows.append(ranked)
        values = jnp.concatenate(rows, 0)
        values = values + cross(values)
        dp = lax.axis_size("dp")
        others = [
            lax.ppermute(values, "dp", [(i, (i + r) % dp) for i in range(dp)])
            for r in range(1, dp)
        ]
        return functools.reduce(jnp.add, others, values)

    def sum_grads(self, values):
        dp = lax.axis_size("dp")
        at = lax.axis_index("dp")
        size = values.shape[0] // dp

        def shifted(arrays):
            return [
                lax.ppermute(a, "dp", [(i, (i + r) % dp) for i in range(dp)])
                for r, a in enumerate(arrays, 1)
            ]

        mine = slot(values, at, size).astype(F4)
        for got in shifted([slot(values, (at + r) % dp, size) for r in range(1, dp)]):
            mine = mine + got.astype(F4)
        mine = mine.astype(BF)
        half = size // 2
        whole = add_low(slot(mine, self.me, half), cross(slot(mine, 1 - self.me, half)))
        other = cross(whole)
        low, high = jnp.where(self.me == 0, whole, other), jnp.where(self.me == 0, other, whole)
        mine = jnp.concatenate([low, high], 0)
        out = jnp.zeros_like(values)
        for r, got in enumerate([mine] + shifted([mine] * (dp - 1))):
            out = lax.dynamic_update_slice_in_dim(out, got, (at - r + dp) % dp * size, 0)
        return out.astype(F4)

    def to_tokens(self, mixture):
        blocks, rows, width = mixture.shape
        piece = mixture.reshape(2, 4, self.per, rows, width)
        columns = []
        for r in range(4):
            here = piece[0, r] if r == 0 else both(piece[0, r], 0, r)
            there = both(piece[1, r], 1, r)
            first = jnp.where(self.me == 0, here, there)
            second = jnp.where(self.me == 0, there, here)
            columns.append(jnp.stack([first, second], 1).reshape(self.sub, width))
        return jnp.stack(columns)

    def to_heads(self, grads, rows):
        parts = grads.reshape(4, self.per, 2, rows, grads.shape[2])
        mine = jnp.where(self.me == 0, parts[:, :, 0], parts[:, :, 1])
        theirs = jnp.where(self.me == 0, parts[:, :, 1], parts[:, :, 0])
        here = [mine[r] if r == 0 else both(mine[r], 0, r) for r in range(4)]
        there = [both(theirs[r], 1, r) for r in range(4)]
        return jnp.concatenate(here + there, 0)


class Plain:
    def __init__(self, block_len):
        self.me = lax.axis_index("seq")
        self.rank = lax.axis_index("tensor")
        self.seq = lax.axis_size("seq")
        self.tensor = lax.axis_size("tensor")
        self.block_len = block_len
        self.sub = block_len // self.tensor

    def position(self, natural, blocks):
        return natural

    def place(self, count):
        return jnp.arange(count, dtype=jnp.int32)

    def spread(self, own):
        return [lax.all_gather(own, "tensor", axis=0, tiled=True)]

    def unit_places(self):
        return [jnp.arange(pl.cdiv(self.block_len, BLK), dtype=jnp.int32)]

    def gather_weight(self, own):
        return lax.all_gather(own, "tensor", axis=0)

    def collect(self, piece):
        whole = jnp.concatenate(piece, 0)
        return [lax.psum_scatter(whole, "tensor", scatter_dimension=0, tiled=True)]

    def collect_all(self, grads, weight):
        size = grads.shape[0] // 8
        sides = []
        for side in range(2):
            keep, away = norm_grads(grads, weight, self.rank[None], side, size)
            half = keep.shape[1]
            whole = jnp.stack([keep.reshape(4, size, half), away.reshape(4, size, half)], 1)
            sides.append(
                [
                    lax.psum_scatter(
                        whole.reshape(-1, half),
                        ("seq", "tensor"),
                        scatter_dimension=0,
                        tiled=True,
                    )
                ]
            )
        return sides

    def sum_small(self, shared, ranked):
        rows = []
        if shared is not None:
            rows.append(lax.psum(shared, ("dp", "seq", "tensor")))
        if ranked is not None:
            rows.append(lax.psum(ranked, ("dp", "seq")))
        return jnp.concatenate(rows, 0)

    def sum_grads(self, values):
        return lax.psum(values, ("dp", "seq")).astype(F4)

    def to_tokens(self, mixture):
        blocks, rows, width = mixture.shape
        full = lax.all_gather(mixture, ("seq", "tensor"), axis=0)
        full = full.reshape(self.seq, self.tensor, blocks, rows, width)
        full = full.transpose(1, 2, 0, 3, 4).reshape(self.tensor, -1, width)
        return slot(full, self.me * self.tensor + self.rank, self.sub, 1)

    def to_heads(self, grads, rows):
        full = lax.all_gather(grads, ("seq", "tensor"), axis=1, tiled=True)
        full = full.reshape(self.tensor, -1, self.seq, rows, grads.shape[2])
        return slot(slot(full, self.me, 1, 2)[:, :, 0], self.rank, 1)[0]


def tree_order(seg_row, parent_row, position):
    blocks = seg_row.shape[0] // BLK
    segs = parent_row.shape[0]
    slot_seg = seg_row[::BLK]
    labels = jnp.arange(segs, dtype=jnp.int32)
    above = jnp.sum(jnp.where(slot_seg[:, None] == labels[None, :], parent_row[None, :], 0), 1)
    natural = jnp.arange(blocks, dtype=jnp.int32)
    key = jnp.where(
        slot_seg == 0,
        natural,
        jnp.where(above == 0, 100 + slot_seg, 1000 + 16 * above + slot_seg),
    )
    rank = jnp.sum((key[None, :] < key[:, None]).astype(jnp.int32), 1)
    where = position(natural, blocks)
    order = jnp.sum(jnp.where(rank[:, None] == natural[None, :], where[:, None], 0), 0)
    base = order[0] // TRUNK_BLOCKS * TRUNK_BLOCKS
    return jnp.concatenate([order, base[None]]).astype(jnp.int32)


def padded(values, axis):
    widths = [(0, 0)] * values.ndim
    widths[axis] = (0, LANE - values.shape[axis])
    return jnp.pad(values, widths)


def total(values):
    return jnp.sum(values, axis=0)


def reduce_grads(arrays):
    low = [a.astype(BF) for a in arrays]
    return [a.astype(F4) for a in lax.psum(low, ("dp", "seq"))]


def local(
    inputs,
    pass_embed,
    norm1_gain,
    norm1_shift,
    w_qkv,
    b_qv,
    w_out,
    b_out,
    norm2_gain,
    norm2_shift,
    w_up,
    b_up,
    w_down,
    b_down,
    out_grad,
    seg_id,
    parent,
):
    x = inputs[0]
    dy_block = out_grad[0]
    block_len, depth = x.shape
    length = seg_id.shape[1]
    seq, tensor = lax.axis_size("seq"), lax.axis_size("tensor")
    width = w_qkv.shape[2]
    heads = width // HD
    rows = BLK // seq
    paired = seq == 2 and tensor == 4 and block_len % (4 * BLK) == 0
    move = Paired(block_len) if paired else Plain(block_len)

    order = tree_order(seg_id[0], parent[0], move.position)
    part = move.me[None].astype(jnp.int32)

    w_cols = jnp.concatenate([padded(w_qkv[i], 1) for i in range(3)], 1)
    zero = jnp.zeros((LANE,), F4)
    b_cols = jnp.concatenate([padded(b_qv[0], 0), zero, padded(b_qv[1], 0)])
    norm_args = (length, pass_embed, norm1_gain, norm1_shift, w_cols, b_cols)
    if paired:
        far = move.far(x)
        count = block_len // BLK
        made = project(x, move.place(count), 0, *norm_args)
        straight = jnp.arange(count, dtype=jnp.int32)
        normed, qkv = project(far, straight, count, *norm_args, before=made)
    else:
        full = lax.all_gather(x, "seq", axis=0, tiled=True)
        normed, qkv = project(full, move.place(length // BLK), 0, *norm_args)

    mixture, lse = attend(qkv, order, part, heads, rows)

    at = move.rank[None].astype(jnp.int32)
    out_weight = move.gather_weight(w_out)
    mixed = move.to_tokens(mixture)
    middle, lifted_own = own_forward(
        x, at, pass_embed, mixed, out_weight, b_out, norm2_gain, norm2_shift
    )

    kept = None
    lift_pieces = []
    out_pieces = []
    for lifted, place in zip(move.spread(lifted_own), move.unit_places()):
        *kept, lift_piece, out_piece = units(lifted, dy_block, place, w_up, b_up, w_down, kept)
        lift_pieces.append(lift_piece)
        out_pieces.append(out_piece)
    lift_all, active, grad_pre = kept
    grad_lift = move.collect(lift_pieces)
    out_terms = move.collect(out_pieces)
    output = functools.reduce(jnp.add, [t.astype(F4) for t in out_terms], middle + b_down)
    output = output.astype(BF)
    grad_w_up, grad_w_down, up_sums = unit_grads(lift_all, grad_pre, active, dy_block, at)

    grad_middle, grad_mix, grad_w_out, early = own_backward(
        grad_lift, middle, dy_block, at, norm2_gain, out_weight, mixed
    )
    grad_mix = move.to_heads(grad_mix, rows)
    grad_w_out = move.collect(list(grad_w_out))
    grad_w_out = functools.reduce(jnp.add, [t.astype(F4) for t in grad_w_out])
    if not paired:
        grad_w_out = grad_w_out.reshape(width, depth)
    grad_w_up, grad_w_down, grad_w_out = reduce_grads([grad_w_up, grad_w_down, grad_w_out])
    early = move.sum_small(early[:4], up_sums[:1])

    grads = attend_back(qkv, mixture, grad_mix, lse, order, part, heads, rows)

    left, right = move.collect_all(grads, w_cols)
    grad_w_cols, col_sums = projection_grads(normed, grads, width, at)
    grad_w_cols = move.sum_grads(grad_w_cols)
    grad_w_qkv = jnp.stack([grad_w_cols[:, i * width : (i + 1) * width] for i in range(3)])
    col_sums = move.sum_small(None, col_sums[:1])[0]
    grad_b_qv = jnp.stack([col_sums[:width], col_sums[2 * LANE : 2 * LANE + width]])

    input_grad, late = last_norm(left, right, x, at, pass_embed, norm1_gain, grad_middle)
    late = move.sum_small(late[:3], None)
    return (
        output[None],
        input_grad[None],
        late[0],
        late[1],
        late[2],
        grad_w_qkv,
        grad_b_qv,
        grad_w_out,
        early[0],
        early[1],
        early[2],
        grad_w_up,
        early[4],
        grad_w_down,
        early[3],
    )


def solution(mesh):
    return jax.shard_map(
        local,
        mesh=mesh,
        in_specs=(
            P("dp", "seq", None),
            P(),
            P(),
            P(),
            P(None, None, "tensor"),
            P(None, "tensor"),
            P("tensor", None),
            P(),
            P(),
            P(),
            P(None, "tensor"),
            P("tensor"),
            P("tensor", None),
            P(),
            P("dp", "seq", None),
            P("dp", None),
            P("dp", None),
        ),
        out_specs=(
            P("dp", ("seq", "tensor"), None),
            P("dp", ("seq", "tensor"), None),
            P(),
            P(),
            P(),
            P(None, None, "tensor"),
            P(None, "tensor"),
            P("tensor", None),
            P(),
            P(),
            P(),
            P(None, "tensor"),
            P("tensor"),
            P("tensor", None),
            P(),
        ),
        check_vma=False,
    )
```

```python
import functools

import jax
import jax.numpy as jnp
from jax import lax
from jax.experimental import pallas as pl
from jax.experimental.pallas import tpu as pltpu
from jax.sharding import PartitionSpec as P

HD = 64
BLK = 256
TRUNK_BLOCKS = 4
LANE = 256
PIECES = 8
EPS = 1e-05
ROOT = 0.7978845608028654
BF = jnp.bfloat16
F4 = jnp.float32
NT = (((1,), (1,)), ((), ()))
NN = (((1,), (0,)), ((), ()))
TN = (((0,), (0,)), ((), ()))
LIGHT = pl.CostEstimate(flops=1000, bytes_accessed=1000, transcendentals=0)


def takes(us):
    return pl.CostEstimate(flops=int(us * 1.1e9), bytes_accessed=1000, transcendentals=0)


def in_hbm(values):
    return pltpu.with_memory_space_constraint(values, pltpu.HBM)


def in_vmem_space(values):
    return pltpu.with_memory_space_constraint(values, pltpu.VMEM)


def dot(left, right, dims=NN):
    return lax.dot_general(left, right, dims, preferred_element_type=F4)


def norm_stats(values):
    row_mean = jnp.mean(values, -1, keepdims=True)
    centred = values - row_mean
    inv_std = lax.rsqrt(jnp.mean(centred * centred, -1, keepdims=True) + EPS)
    return (centred * inv_std, inv_std)


def norm_back(grad_out, normal, inv_std, gain_vec):
    scaled = grad_out * gain_vec
    return inv_std * (
        scaled
        - jnp.mean(scaled, -1, keepdims=True)
        - normal * jnp.mean(scaled * normal, -1, keepdims=True)
    )


def gelu_parts(pre_act):
    cubic_term = 0.044715 * pre_act * pre_act * pre_act
    tangent = jnp.tanh(ROOT * (pre_act + cubic_term))
    gelu_value = 0.5 * pre_act * (1.0 + tangent)
    gelu_slope = 0.5 * (1.0 + tangent) + 0.5 * pre_act * (1.0 - tangent * tangent) * ROOT * (
        1.0 + 3.0 * 0.044715 * pre_act * pre_act
    )
    return (gelu_value, gelu_slope)


def block_rows(pos, count=1):
    return pl.ds(pl.multiple_of(pos * BLK, BLK), count * BLK)


def head_masks(shape, heads):
    lane = lax.broadcasted_iota(jnp.int32, shape, 1) // HD
    return [lane == h for h in range(heads)]


def each_tile(order_ref, tile):
    trunk = [order_ref[i] for i in range(TRUNK_BLOCKS)]
    base = order_ref[16]
    tile(trunk[0], trunk[1], [], [(trunk[0], True)], [(trunk[0], False), (trunk[1], True)])
    tile(
        trunk[2],
        trunk[3],
        [(trunk[0], 2)],
        [(trunk[2], True)],
        [(trunk[2], False), (trunk[3], True)],
    )

    def deep(i, carry):
        one, two = order_ref[4 + 2 * i], order_ref[5 + 2 * i]
        above = order_ref[jnp.maximum(2 + i, 4)]
        tile(one, two, [(base, 4), (above, 1)], [(one, True)], [(two, True)], i >= 2)
        return carry

    lax.fori_loop(0, 6, deep, 0)


def attend_kernel(heads, rows, order_ref, part_ref, qkv_ref, out_ref, lse_ref):
    part = part_ref[0]

    def q_at(pos):
        return qkv_ref[pl.ds(pl.multiple_of(pos * BLK + part * rows, rows), rows), 0:LANE]

    def k_at(pos, count=1):
        return qkv_ref[block_rows(pos, count), LANE : 2 * LANE]

    def v_at(pos, count=1):
        return qkv_ref[block_rows(pos, count), 2 * LANE : 3 * LANE]

    row_at = lax.broadcasted_iota(jnp.int32, (rows, BLK), 0) + part * rows
    causal = row_at >= lax.broadcasted_iota(jnp.int32, (rows, BLK), 1)
    masks = head_masks((2 * rows, LANE), heads)

    def tile(first, second, shared, parts_a, parts_b, use_last=None):
        q = jnp.concatenate([q_at(first), q_at(second)], 0) * BF(0.125)
        result = jnp.zeros((2 * rows, LANE), F4)
        log_cols = []
        for h in range(heads):
            qm = jnp.where(masks[h], q, BF(0))
            halves = [qm[:rows], qm[rows:]]
            wide = [dot(qm, k_at(p, c), NT) for p, c in shared]
            if use_last is not None:
                wide[-1] = wide[-1] + jnp.where(use_last, 0.0, -jnp.inf)
            own = [
                [
                    jnp.where(causal, dot(halves[i], k_at(p), NT), -jnp.inf)
                    if diag
                    else dot(halves[i], k_at(p), NT)
                    for p, diag in parts
                ]
                for i, parts in enumerate((parts_a, parts_b))
            ]
            tops = []
            for i in range(2):
                tops.append(
                    functools.reduce(
                        jnp.maximum,
                        [
                            jnp.max(s, 1, keepdims=True)
                            for s in [w[i * rows : (i + 1) * rows] for w in wide] + own[i]
                        ],
                    )
                )
            top = jnp.concatenate(tops, 0)
            mix = jnp.zeros((2 * rows, LANE), F4)
            total = jnp.zeros((2 * rows, 1), F4)
            for s, (p, c) in zip(wide, shared):
                e = jnp.exp(s - top)
                total = total + jnp.sum(e, 1, keepdims=True)
                mix = mix + dot(e.astype(BF), v_at(p, c))
            extra = []
            sums = []
            for i, parts in enumerate((parts_a, parts_b)):
                m_i = jnp.zeros((rows, LANE), F4)
                t_i = jnp.zeros((rows, 1), F4)
                for s, (p, _) in zip(own[i], parts):
                    e = jnp.exp(s - tops[i])
                    t_i = t_i + jnp.sum(e, 1, keepdims=True)
                    m_i = m_i + dot(e.astype(BF), v_at(p))
                extra.append(m_i)
                sums.append(t_i)
            total = total + jnp.concatenate(sums, 0)
            mix = (mix + jnp.concatenate(extra, 0)) / total
            result = jnp.where(masks[h], mix, result)
            log_cols.append(top + jnp.log(total))
        low = result.astype(BF)[:, : heads * HD]
        out_ref[first] = low[:rows]
        out_ref[second] = low[rows:]
        lane = lax.broadcasted_iota(jnp.int32, (2 * rows, 128), 1)
        cols = jnp.zeros((2 * rows, 128), F4)
        for h in range(heads):
            cols = jnp.where(lane == h, log_cols[h], cols)
        flat = jnp.transpose(cols)[:8]
        lse_ref[first] = flat[:, :rows]
        lse_ref[second] = flat[:, rows:]

    each_tile(order_ref, tile)


def in_vmem(count):
    return [pl.BlockSpec(memory_space=pltpu.VMEM)] * count


def in_smem(count):
    return [pl.BlockSpec(memory_space=pltpu.SMEM)] * count


def attend(qkv, order, part, heads, rows):
    blocks = qkv.shape[0] // BLK
    return pl.pallas_call(
        functools.partial(attend_kernel, heads, rows),
        out_shape=(
            pltpu.HBM((blocks, rows, heads * HD), BF),
            pltpu.HBM((blocks, 8, rows), F4),
        ),
        in_specs=in_smem(2) + in_vmem(1),
        out_specs=in_vmem(2),
        compiler_params=pltpu.CompilerParams(vmem_limit_bytes=24 << 20),
        cost_estimate=takes(25),
        name="tree_attend",
    )(order, part, in_vmem_space(qkv))


def attend_back_kernel(heads, rows, terms, order_ref, part_ref, *refs):
    qkv_ref, mix_ref, grad_ref, lse_ref, normed_ref, w_ref = refs[:6]
    term_refs = refs[6 : 6 + terms]
    norm_refs = refs[6 + terms : 10 + terms]
    proj_ref, sum_ref, acc_q, acc_k, acc_v, acc_w = refs[10 + terms :]
    length = qkv_ref.shape[0]
    part = part_ref[0]
    width = heads * HD

    def q_rows(pos):
        return pl.ds(pl.multiple_of(pos * BLK + part * rows, rows), rows)

    def k_at(pos, count=1):
        return qkv_ref[block_rows(pos, count), LANE : 2 * LANE]

    def v_at(pos, count=1):
        return qkv_ref[block_rows(pos, count), 2 * LANE : 3 * LANE]

    key_at = lax.broadcasted_iota(jnp.int32, (BLK, rows), 0)
    causal = (lax.broadcasted_iota(jnp.int32, (BLK, rows), 1) + part * rows) >= key_at
    masks = head_masks((2 * rows, LANE), heads)
    acc_k[...] = jnp.zeros_like(acc_k)
    acc_v[...] = jnp.zeros_like(acc_v)
    acc_q[...] = jnp.zeros_like(acc_q)
    pick = (
        lax.broadcasted_iota(jnp.int32, (8, LANE), 1) // HD
        == lax.broadcasted_iota(jnp.int32, (8, LANE), 0)
    ).astype(BF)
    pad = jnp.zeros((2 * rows, LANE - width), BF)

    def tile(first, second, shared, parts_a, parts_b, use_last=None):
        q = jnp.concatenate(
            [qkv_ref[q_rows(first), 0:LANE], qkv_ref[q_rows(second), 0:LANE]], 0
        ) * BF(0.125)
        grad = jnp.concatenate([jnp.concatenate([grad_ref[first], grad_ref[second]], 0), pad], 1)
        mix = jnp.concatenate([jnp.concatenate([mix_ref[first], mix_ref[second]], 0), pad], 1)
        inner = dot(pick, (grad.astype(F4) * mix.astype(F4)).astype(BF), NT)
        lse = jnp.concatenate([lse_ref[first], lse_ref[second]], 1)
        qms = [jnp.where(masks[h], q, BF(0)) for h in range(heads)]
        gms = [jnp.where(masks[h], grad, BF(0)) for h in range(heads)]

        def pieces(keys, values, h, cut, diag, bias):
            e = jnp.exp(dot(keys, qms[h][cut], NT) - (lse[h : h + 1, cut] + bias))
            if diag:
                e = jnp.where(causal, e, 0.0)
            t = dot(values, gms[h][cut], NT)
            return e.astype(BF), (e * (t - inner[h : h + 1, cut])).astype(BF)

        def strip(pos, count, cut, diag, grad_q, bias=0.0):
            keys, values = k_at(pos, count), v_at(pos, count)
            es = []
            ds = []
            for h in range(heads):
                e, d = pieces(keys, values, h, cut, diag, bias)
                es.append(e)
                ds.append(d)
                grad_q = grad_q + jnp.where(masks[h][cut], dot(d, keys, TN), 0.0)
            acc_v[block_rows(pos, count), :] += dot(
                jnp.concatenate(es, 1), jnp.concatenate([g[cut] for g in gms], 0)
            )
            acc_k[block_rows(pos, count), :] += dot(
                jnp.concatenate(ds, 1), jnp.concatenate([g[cut] for g in qms], 0)
            )
            return grad_q

        grad_q = jnp.zeros((2 * rows, LANE), F4)
        for i, (pos, count) in enumerate(shared):
            bias = 0.0
            if use_last is not None and i == len(shared) - 1:
                bias = jnp.where(use_last, 0.0, jnp.inf)
            grad_q = strip(pos, count, slice(0, 2 * rows), False, grad_q, bias)
        halves = []
        for i, parts in enumerate((parts_a, parts_b)):
            half = jnp.zeros((rows, LANE), F4)
            for pos, diag in parts:
                half = strip(pos, 1, slice(i * rows, (i + 1) * rows), diag, half)
            halves.append(half)
        grad_q = ((grad_q + jnp.concatenate(halves, 0)) * 0.125).astype(BF)
        acc_q[q_rows(first), :] = grad_q[:rows]
        acc_q[q_rows(second), :] = grad_q[rows:]

    each_tile(order_ref, tile)

    half = w_ref.shape[0] // 2
    size = length // PIECES
    acc_w[...] = jnp.zeros_like(acc_w)
    sum_ref[...] = jnp.zeros_like(sum_ref)

    def pair(i, carry):
        for odd in range(2):
            at = pl.ds(pl.multiple_of((2 * i + odd) * size, size), size)
            grads = jnp.concatenate(
                [acc_q[at, :], acc_k[at, :].astype(BF), acc_v[at, :].astype(BF)], 1
            )
            spot = pl.ds(pl.multiple_of(i * size, size), size)
            for side in range(2):
                low = dot(grads, w_ref[side * half : (side + 1) * half, :], NT).astype(BF)
                norm_refs[2 * side + odd][spot, :] = low
            acc_w[...] += dot(normed_ref[at, :], grads, TN)
            sum_ref[0:1, :] += jnp.sum(grads.astype(F4), 0, keepdims=True)
        return carry

    lax.fori_loop(0, PIECES // 2, pair, 0)
    rest = add_all([r[...] for r in term_refs]).astype(BF)
    fill = LANE - width
    for i in range(3):
        whole = acc_w[:, i * LANE : i * LANE + width].astype(BF)
        proj_ref[:, i * LANE : (i + 1) * LANE] = jnp.concatenate(
            [whole, rest[:, i * fill : (i + 1) * fill]], 1
        )


def attend_back(qkv, mix, grad, lse, normed, weight, out_terms, order, part, heads, rows):
    length, depth = normed.shape
    half = jax.ShapeDtypeStruct((length // 2, depth // 2), BF)
    return pl.pallas_call(
        functools.partial(attend_back_kernel, heads, rows, len(out_terms)),
        out_shape=(
            half,
            half,
            half,
            half,
            jax.ShapeDtypeStruct((depth, 3 * LANE), BF),
            jax.ShapeDtypeStruct((8, 3 * LANE), F4),
        ),
        in_specs=in_smem(2) + in_vmem(6 + len(out_terms)),
        out_specs=in_vmem(6),
        scratch_shapes=[
            pltpu.VMEM((length, LANE), BF),
            pltpu.VMEM((length, LANE), F4),
            pltpu.VMEM((length, LANE), F4),
            pltpu.VMEM((depth, 3 * LANE), F4),
        ],
        compiler_params=pltpu.CompilerParams(vmem_limit_bytes=40 << 20),
        cost_estimate=LIGHT,
        name="tree_attend_back",
    )(
        order,
        part,
        in_vmem_space(qkv),
        mix,
        grad,
        lse,
        in_vmem_space(normed),
        weight,
        *out_terms,
    )


def project_kernel(count, place_ref, *refs):
    x_refs = refs[:count]
    pass_ref, gain_ref, shift_ref, w_ref, b_ref = refs[count : count + 5]
    normed_ref, qkv_ref = refs[-2:]
    x = x_refs[0][...]
    for i in range(1, count):
        x = jnp.where(pl.program_id(0) == i, x_refs[i][...], x)
    normal, _ = norm_stats(x.astype(F4) + pass_ref[...])
    normed = (normal * gain_ref[...] + shift_ref[...]).astype(BF)
    normed_ref[...] = normed
    qkv_ref[...] = (dot(normed, w_ref[...]) + b_ref[...]).astype(BF)


def project(pieces, place, offset, length, pass_embed, gain, shift, weight, bias, before=None):
    width = weight.shape[1]
    depth = weight.shape[0]
    count = len(pieces)
    step = pieces[0].shape[0] if count > 1 else min(512, pieces[0].shape[0])
    if count > 1:
        specs = [whole_spec((step, depth))] * count
        steps = count
    else:
        specs = [pl.BlockSpec((step, depth), lambda i, place: (place[i], 0))]
        steps = pieces[0].shape[0] // step
    vec = vec_spec(depth)
    specs += [vec, vec, vec, whole_spec((depth, width)), vec_spec(width)]
    operands = [*pieces, pass_embed[None], gain[None], shift[None], weight, bias[None]]
    aliases = {}
    if before is not None:
        aliases = {len(specs) + 1: 0, len(specs) + 2: 1}
        specs += [pl.BlockSpec(memory_space=pl.ANY)] * 2
        operands += [in_vmem_space(b) for b in before]
    return pl.pallas_call(
        functools.partial(project_kernel, count),
        out_shape=(pltpu.VMEM((length, depth), BF), pltpu.VMEM((length, width), BF)),
        grid_spec=grid_of(
            steps,
            specs,
            (
                pl.BlockSpec((step, depth), lambda i, place: (offset + i, 0)),
                pl.BlockSpec((step, width), lambda i, place: (offset + i, 0)),
            ),
        ),
        input_output_aliases=aliases,
        compiler_params=pltpu.CompilerParams(vmem_limit_bytes=48 << 20),
        cost_estimate=takes(5),
        name="norm_project",
    )(place, *operands)


def vec_spec(depth):
    return pl.BlockSpec((1, depth), lambda i, at: (0, 0))


def own_rows_spec(depth, step, fixed=False):
    if fixed:
        return pl.BlockSpec((step, depth), lambda i, at: (at[0] + i, 0))
    return pl.BlockSpec((step, depth), lambda i, at: (i, 0))


def pieces_spec(count, step, width):
    return pl.BlockSpec((count, step, width), lambda i, at: (0, i, 0))


def whole_spec(shape):
    return pl.BlockSpec(shape, lambda i, at: (0,) * len(shape))


def grid_of(steps, ins, outs, scratch=()):
    return pltpu.PrefetchScalarGridSpec(
        num_scalar_prefetch=1,
        grid=(steps,),
        in_specs=ins,
        out_specs=outs,
        scratch_shapes=list(scratch),
    )


def own_forward_kernel(
    count, at_ref, x_ref, pass_ref, mix_ref, w_ref, b_ref, gain_ref, shift_ref, mid_ref, lift_ref
):
    middle = x_ref[...].astype(F4) + pass_ref[...] + b_ref[...]
    for r in range(count):
        middle = middle + dot(mix_ref[r], w_ref[r])
    mid_ref[...] = middle
    normal, _ = norm_stats(middle)
    lift_ref[...] = (normal * gain_ref[...] + shift_ref[...]).astype(BF)


def own_forward(x, at, pass_embed, mixed, weight, bias, gain, shift):
    count, sub, width = mixed.shape
    depth = x.shape[1]
    step = min(512, sub)
    vec = vec_spec(depth)
    return pl.pallas_call(
        functools.partial(own_forward_kernel, count),
        out_shape=(
            pltpu.HBM((sub, depth), F4),
            jax.ShapeDtypeStruct((sub, depth), BF),
        ),
        grid_spec=grid_of(
            sub // step,
            [
                own_rows_spec(depth, step, True),
                vec,
                pieces_spec(count, step, width),
                whole_spec(weight.shape),
                vec,
                vec,
                vec,
            ],
            (own_rows_spec(depth, step), own_rows_spec(depth, step)),
        ),
        cost_estimate=takes(3),
        compiler_params=pltpu.CompilerParams(vmem_limit_bytes=48 << 20),
        name="own_forward",
    )(at * (sub // step), x, pass_embed[None], mixed, weight, bias[None], gain[None], shift[None])


def own_backward_kernel(count, parts, at_ref, *refs):
    grad_parts = refs[:parts]
    mid_ref, dy_ref, gain_ref, w_ref, mix_ref, gm_ref, gmix_ref, gw_ref, sums_ref, acc = refs[parts:]
    step = pl.program_id(0)

    @pl.when(step == 0)
    def _():
        acc[...] = jnp.zeros_like(acc)
        sums_ref[...] = jnp.zeros_like(sums_ref)

    grad_lift = functools.reduce(jnp.add, [g[...].astype(F4) for g in grad_parts])
    normal, inv = norm_stats(mid_ref[...])
    dy = dy_ref[...].astype(F4)
    grad_middle = dy + norm_back(grad_lift, normal, inv, gain_ref[...])
    gm_ref[...] = grad_middle
    low = grad_middle.astype(BF)
    for r in range(count):
        gmix_ref[r] = dot(low, w_ref[r], NT).astype(BF)
        acc[r] += dot(low, mix_ref[r], TN)
    for i, values in enumerate((grad_middle, grad_lift * normal, grad_lift, dy)):
        sums_ref[i : i + 1, :] += jnp.sum(values, 0, keepdims=True)

    @pl.when(step == pl.num_programs(0) - 1)
    def _():
        gw_ref[...] = acc[...].astype(BF)


def own_backward(grad_parts, middle, dy, at, gain, weight, mixed):
    count, sub, width = mixed.shape
    depth = dy.shape[1]
    step = min(512, sub)
    rows = own_rows_spec(depth, step)
    return pl.pallas_call(
        functools.partial(own_backward_kernel, count, len(grad_parts)),
        out_shape=(
            pltpu.HBM((sub, depth), F4),
            jax.ShapeDtypeStruct((count, sub, width), BF),
            jax.ShapeDtypeStruct((count, depth, width), BF),
            jax.ShapeDtypeStruct((8, depth), F4),
        ),
        grid_spec=grid_of(
            sub // step,
            [rows] * len(grad_parts)
            + [
                rows,
                own_rows_spec(depth, step, True),
                vec_spec(depth),
                whole_spec(weight.shape),
                pieces_spec(count, step, width),
            ],
            (
                rows,
                pieces_spec(count, step, width),
                whole_spec((count, depth, width)),
                whole_spec((8, depth)),
            ),
            [pltpu.VMEM((count, depth, width), F4)],
        ),
        cost_estimate=takes(6),
        compiler_params=pltpu.CompilerParams(vmem_limit_bytes=48 << 20),
        name="own_backward",
    )(at * (sub // step), *grad_parts, in_hbm(middle), dy, gain[None], weight, mixed)


def last_norm_kernel(counts, at_ref, *refs):
    split = counts[0]
    left, right = refs[:split], refs[split : split + counts[1]]
    x_ref, pass_ref, gain_ref, gm_ref, out_ref, sums_ref = refs[split + counts[1] :]

    @pl.when(pl.program_id(0) == 0)
    def _():
        sums_ref[...] = jnp.zeros_like(sums_ref)

    grad_norm = jnp.concatenate(
        [functools.reduce(jnp.add, [g[...].astype(F4) for g in side]) for side in (left, right)], 1
    )
    normal, inv = norm_stats(x_ref[...].astype(F4) + pass_ref[...])
    grad_resid = gm_ref[...] + norm_back(grad_norm, normal, inv, gain_ref[...])
    out_ref[...] = grad_resid.astype(BF)
    for i, values in enumerate((grad_resid, grad_norm * normal, grad_norm)):
        sums_ref[i : i + 1, :] += jnp.sum(values, 0, keepdims=True)


def last_norm(left, right, x, at, pass_embed, gain, grad_middle):
    sub, depth = grad_middle.shape
    step = min(512, sub)
    return pl.pallas_call(
        functools.partial(last_norm_kernel, (len(left), len(right))),
        out_shape=(
            jax.ShapeDtypeStruct((sub, depth), BF),
            jax.ShapeDtypeStruct((8, depth), F4),
        ),
        grid_spec=grid_of(
            sub // step,
            [own_rows_spec(depth // 2, step)] * (len(left) + len(right))
            + [
                own_rows_spec(depth, step, True),
                vec_spec(depth),
                vec_spec(depth),
                own_rows_spec(depth, step),
            ],
            (own_rows_spec(depth, step), whole_spec((8, depth))),
        ),
        compiler_params=pltpu.CompilerParams(vmem_limit_bytes=48 << 20),
        name="last_norm",
    )(at * (sub // step), *left, *right, x, pass_embed[None], gain[None], in_hbm(grad_middle))


def units_kernel(count, place_ref, *refs):
    lift_refs = refs[:count]
    dy_ref, up_ref, bias_ref, down_ref = refs[count : count + 4]
    outs = refs[-(3 + 2 * count) :]
    keep_ref, active_ref, pre_ref = outs[:3]
    step = pl.program_id(0)
    lifted = lift_refs[0][...]
    for i in range(1, count):
        lifted = jnp.where(step == i, lift_refs[i][...], lifted)
    keep_ref[...] = lifted
    pre_act = dot(lifted, up_ref[...]) + bias_ref[...]
    value, slope = gelu_parts(pre_act)
    active = value.astype(BF)
    active_ref[...] = active
    grad_pre = (dot(dy_ref[...], down_ref[...], NT) * slope).astype(BF)
    pre_ref[...] = grad_pre
    grad_lift = dot(grad_pre, up_ref[...], NT).astype(BF)
    out = dot(active, down_ref[...]).astype(BF)
    for i in range(count):

        @pl.when(step == i)
        def _():
            outs[3 + i][...] = grad_lift
            outs[3 + count + i][...] = out


def units(lifted, dy, place, w_up, b_up, w_down, before=None):
    step, depth = lifted[0].shape
    count = len(lifted)
    length = dy.shape[0]
    wide = w_up.shape[1]
    spot = pl.BlockSpec((step, depth), lambda i, place: (place[i], 0))
    spot_wide = pl.BlockSpec((step, wide), lambda i, place: (place[i], 0))
    piece = whole_spec((step, depth))
    specs = [piece] * count
    specs += [spot, whole_spec(w_up.shape), vec_spec(wide), whole_spec(w_down.shape)]
    operands = [*lifted, in_hbm(dy), in_hbm(w_up), b_up[None], in_hbm(w_down)]
    aliases = {}
    if before is not None:
        base = 1 + len(operands)
        specs += [pl.BlockSpec(memory_space=pl.ANY)] * 3
        operands += [in_hbm(b) for b in before]
        aliases = {base: 0, base + 1: 1, base + 2: 2}
    made = pl.pallas_call(
        functools.partial(units_kernel, count),
        out_shape=(
            pltpu.HBM((length, depth), BF),
            pltpu.HBM((length, wide), BF),
            pltpu.HBM((length, wide), BF),
        )
        + (jax.ShapeDtypeStruct((step, depth), BF),) * (2 * count),
        grid_spec=grid_of(count, specs, (spot, spot_wide, spot_wide) + (piece,) * (2 * count)),
        input_output_aliases=aliases,
        compiler_params=pltpu.CompilerParams(vmem_limit_bytes=48 << 20),
        cost_estimate=takes(10),
        name="units",
    )(place, *operands)
    return made[:3], made[3 : 3 + count], made[3 + count :]


def unit_grads_kernel(at_ref, lift_ref, pre_ref, active_ref, dy_ref, out_ref, sum_ref, acc):
    @pl.when(pl.program_id(0) == 0)
    def _():
        acc[...] = jnp.zeros_like(acc)
        sum_ref[...] = jnp.zeros_like(sum_ref)

    acc[0] += dot(lift_ref[...], pre_ref[...], TN)
    acc[1] += dot(active_ref[...], dy_ref[...], TN)
    sum_ref[0:1, :] += jnp.sum(pre_ref[...].astype(F4), 0, keepdims=True)

    @pl.when(pl.program_id(0) == pl.num_programs(0) - 1)
    def _():
        out_ref[...] = acc[...].astype(BF)


def unit_grads(lifted, grad_pre, active, dy, at):
    rows, depth = lifted.shape
    wide = active.shape[1]
    step = min(1024, rows)
    spec = own_rows_spec(depth, step)
    return pl.pallas_call(
        unit_grads_kernel,
        out_shape=(
            pltpu.HBM((2, depth, wide), BF),
            jax.ShapeDtypeStruct((8, wide), F4),
        ),
        grid_spec=grid_of(
            rows // step,
            [spec, spec, spec, spec],
            (whole_spec((2, depth, wide)), whole_spec((8, wide))),
            [pltpu.VMEM((2, depth, wide), F4)],
        ),
        compiler_params=pltpu.CompilerParams(vmem_limit_bytes=48 << 20),
        cost_estimate=takes(8),
        name="unit_grads",
    )(at, *[in_hbm(v) for v in (lifted, grad_pre, active, dy)])


def send(values, axis, partner):
    size = lax.axis_size(axis)
    return lax.ppermute(values, axis, [(i, partner(i)) for i in range(size)])


def hop(values, step):
    return send(values, "tensor", lambda i: i ^ step)


def cross(values):
    return send(values, "seq", lambda i: i ^ 1)


def both(values, step_seq, step_tensor):
    return send(
        values, ("seq", "tensor"), lambda i: (i // 4 ^ step_seq) * 4 + (i % 4 ^ step_tensor)
    )


def add_low(left, right):
    return (left.astype(F4) + right.astype(F4)).astype(BF)


def add_all(arrays):
    return functools.reduce(jnp.add, [a.astype(F4) for a in arrays])


def tie(*values):
    return lax.optimization_barrier(values)


def slot(values, index, size, axis=0):
    return lax.dynamic_slice_in_dim(values, index * size, size, axis)


class Paired:
    def __init__(self, block_len):
        self.me = lax.axis_index("seq")
        self.rank = lax.axis_index("tensor")
        self.sub = block_len // 4
        self.per = self.sub // BLK

    def position(self, natural, blocks):
        half = blocks // 2
        s, b = natural // half, natural % half
        return half * (s ^ self.me) + self.per * ((b // self.per) ^ self.rank) + b % self.per

    def place(self):
        return jnp.stack([self.rank ^ r for r in range(4)]).astype(jnp.int32)

    def far(self, values):
        mine = cross(slot(values, self.rank, self.sub))
        other = hop(mine, 2)
        return mine, hop(mine, 1), other

    def gather_weight(self, own):
        return jnp.stack([own, hop(own, 1), hop(own, 2), hop(own, 3)])

    def collect(self, piece, after=None):
        away = add_low(piece[2], hop(piece[3], 1))
        terms = [piece[0], hop(piece[1], 1), hop(away, 2)]
        return terms if after is None else (terms, *tie(*after, away)[:-1])

    def halves(self, values, axis, bit):
        half = values.shape[0] // 2
        at = lax.axis_index(axis) >> bit & 1
        away = send(slot(values, 1 - at, half), axis, lambda i: i ^ (1 << bit))
        return add_low(slot(values, at, half), away)

    def doubled(self, values, axis, bit):
        at = lax.axis_index(axis) >> bit & 1
        other = send(values, axis, lambda i: i ^ (1 << bit))
        return jnp.concatenate(
            [jnp.where(at == 0, values, other), jnp.where(at == 0, other, values)], 0
        )

    def last_sums(self, parts, values):
        steps = [("dp", 0), ("seq", 0)]
        steps += [("dp", bit) for bit in range(1, lax.axis_size("dp").bit_length() - 1)]
        values = self.halves(values, *steps[0])
        one, two = [add_low(keep, hop(away, 1)) for keep, away in (parts[:2], parts[2:])]
        one, two, values = tie(one, two, values)
        one, two = [c.reshape(2, 2, self.sub, -1) for c in (one, two)]
        values = self.halves(values, *steps[1])
        one = add_low(one[0], cross(one[1]))
        two = add_low(two[:, 0], hop(two[:, 1], 2))
        one, two, values = tie(one, two, values)
        for step in steps[2:]:
            values = self.halves(values, *step)
        left = [one[0], hop(one[1], 2)]
        right = [two[0], cross(two[1])]
        for step in steps[::-1]:
            values = self.doubled(values, *step)
        return left, right, values

    def sum_small(self, shared, ranked):
        rows = []
        if shared is not None:
            shared = shared + hop(shared, 1)
            rows.append(shared + hop(shared, 2))
        if ranked is not None:
            rows.append(ranked)
        values = jnp.concatenate(rows, 0)
        values = values + cross(values)
        dp = lax.axis_size("dp")
        others = [
            lax.ppermute(values, "dp", [(i, (i + r) % dp) for i in range(dp)])
            for r in range(1, dp)
        ]
        return functools.reduce(jnp.add, others, values)

    def to_tokens(self, mixture):
        blocks, rows, width = mixture.shape
        piece = mixture.reshape(2, 4, self.per, rows, width)
        columns = []
        for r in range(4):
            here = piece[0, r] if r == 0 else both(piece[0, r], 0, r)
            there = both(piece[1, r], 1, r)
            first = jnp.where(self.me == 0, here, there)
            second = jnp.where(self.me == 0, there, here)
            columns.append(jnp.stack([first, second], 1).reshape(self.sub, width))
        return jnp.stack(columns)

    def to_heads(self, grads, rows):
        parts = grads.reshape(4, self.per, 2, rows, grads.shape[2])
        mine = jnp.where(self.me == 0, parts[:, :, 0], parts[:, :, 1])
        theirs = jnp.where(self.me == 0, parts[:, :, 1], parts[:, :, 0])
        here = [mine[r] if r == 0 else both(mine[r], 0, r) for r in range(4)]
        there = [both(theirs[r], 1, r) for r in range(4)]
        return jnp.concatenate(here + there, 0)


class Plain:
    def __init__(self, block_len):
        self.me = lax.axis_index("seq")
        self.rank = lax.axis_index("tensor")
        self.seq = lax.axis_size("seq")
        self.tensor = lax.axis_size("tensor")
        self.block_len = block_len
        self.sub = block_len // self.tensor

    def position(self, natural, blocks):
        return natural

    def gather_weight(self, own):
        return lax.all_gather(own, "tensor", axis=0)

    def collect(self, piece, after=None):
        whole = jnp.concatenate(piece, 0)
        terms = [lax.psum_scatter(whole, "tensor", scatter_dimension=0, tiled=True)]
        return terms if after is None else (terms, *after)

    def last_sums(self, parts, values):
        sides = []
        for keep, away in (parts[:2], parts[2:]):
            half = keep.shape[1]
            keep, away = [v.reshape(PIECES // 2, -1, half) for v in (keep, away)]
            whole = jnp.stack([keep, away], 1).reshape(-1, half)
            sides.append(
                [lax.psum_scatter(whole, ("seq", "tensor"), scatter_dimension=0, tiled=True)]
            )
        return *sides, lax.psum(values, ("dp", "seq"))

    def sum_small(self, shared, ranked):
        rows = []
        if shared is not None:
            rows.append(lax.psum(shared, ("dp", "seq", "tensor")))
        if ranked is not None:
            rows.append(lax.psum(ranked, ("dp", "seq")))
        return jnp.concatenate(rows, 0)

    def to_tokens(self, mixture):
        blocks, rows, width = mixture.shape
        full = lax.all_gather(mixture, ("seq", "tensor"), axis=0)
        full = full.reshape(self.seq, self.tensor, blocks, rows, width)
        full = full.transpose(1, 2, 0, 3, 4).reshape(self.tensor, -1, width)
        return slot(full, self.me * self.tensor + self.rank, self.sub, 1)

    def to_heads(self, grads, rows):
        full = lax.all_gather(grads, ("seq", "tensor"), axis=1, tiled=True)
        full = full.reshape(self.tensor, -1, self.seq, rows, grads.shape[2])
        return slot(slot(full, self.me, 1, 2)[:, :, 0], self.rank, 1)[0]


def tree_order(seg_row, parent_row, position):
    blocks = seg_row.shape[0] // BLK
    segs = parent_row.shape[0]
    slot_seg = seg_row[::BLK]
    labels = jnp.arange(segs, dtype=jnp.int32)
    above = jnp.sum(jnp.where(slot_seg[:, None] == labels[None, :], parent_row[None, :], 0), 1)
    natural = jnp.arange(blocks, dtype=jnp.int32)
    key = jnp.where(
        slot_seg == 0,
        natural,
        jnp.where(above == 0, 100 + slot_seg, 1000 + 16 * above + slot_seg),
    )
    rank = jnp.sum((key[None, :] < key[:, None]).astype(jnp.int32), 1)
    where = position(natural, blocks)
    order = jnp.sum(jnp.where(rank[:, None] == natural[None, :], where[:, None], 0), 0)
    base = order[0] // TRUNK_BLOCKS * TRUNK_BLOCKS
    return jnp.concatenate([order, base[None]]).astype(jnp.int32)


def padded(values, axis):
    widths = [(0, 0)] * values.ndim
    widths[axis] = (0, LANE - values.shape[axis])
    return jnp.pad(values, widths)


def total(values):
    return jnp.sum(values, axis=0)


def scatter_sum(values):
    return lax.psum_scatter(values, ("dp", "seq"), scatter_dimension=0, tiled=True)


def gather_back(values):
    return lax.all_gather(values, ("dp", "seq"), axis=0, tiled=True)


def local(
    inputs,
    pass_embed,
    norm1_gain,
    norm1_shift,
    w_qkv,
    b_qv,
    w_out,
    b_out,
    norm2_gain,
    norm2_shift,
    w_up,
    b_up,
    w_down,
    b_down,
    out_grad,
    seg_id,
    parent,
):
    x = inputs[0]
    dy_block = out_grad[0]
    block_len, depth = x.shape
    length = seg_id.shape[1]
    seq, tensor = lax.axis_size("seq"), lax.axis_size("tensor")
    width = w_qkv.shape[2]
    heads = width // HD
    rows = BLK // seq
    paired = seq == 2 and tensor == 4 and block_len % (4 * BLK) == 0
    move = Paired(block_len) if paired else Plain(block_len)

    order = tree_order(seg_id[0], parent[0], move.position)
    part = move.me[None].astype(jnp.int32)

    w_cols = jnp.concatenate([padded(w_qkv[i], 1) for i in range(3)], 1)
    zero = jnp.zeros((LANE,), F4)
    b_cols = jnp.concatenate([padded(b_qv[0], 0), zero, padded(b_qv[1], 0)])
    norm_args = (length, pass_embed, norm1_gain, norm1_shift, w_cols, b_cols)
    if paired:
        mine, core, other = move.far(x)
        made = project([x], move.place(), 0, *norm_args)
        first, second = jnp.zeros((1,), jnp.int32), jnp.ones((1,), jnp.int32)
        made = project([mine, core], first, 4, *norm_args, before=made)
        other, _ = tie(other, made[0][:8])
        normed, qkv = project([other, hop(other, 1)], second, 6, *norm_args, before=made)
    else:
        full = lax.all_gather(x, "seq", axis=0, tiled=True)
        place = jnp.arange(pl.cdiv(length, 512), dtype=jnp.int32)
        normed, qkv = project([full], place, 0, *norm_args)

    mixture, lse = attend(qkv, order, part, heads, rows)

    at = move.rank[None].astype(jnp.int32)
    out_weight = move.gather_weight(w_out)
    mixed = move.to_tokens(mixture)
    middle, lifted_own = own_forward(
        x, at, pass_embed, mixed, out_weight, b_out, norm2_gain, norm2_shift
    )

    unit_args = (w_up, b_up, w_down)
    if paired:
        core, other = hop(lifted_own, 1), hop(lifted_own, 2)
        kept, near_lift, near_out = units(
            [lifted_own, core], dy_block, move.place()[:2], *unit_args
        )
        other, _ = tie(other, near_lift)
        diag = hop(other, 1)
        kept, far_lift, far_out = units(
            [diag, other], dy_block, move.place()[:1:-1], *unit_args, kept
        )
        lift_made = [*near_lift, *far_lift[::-1]]
        out_made = [*near_out, *far_out[::-1]]
    else:
        lifted = lax.all_gather(lifted_own, "tensor", axis=0, tiled=True)
        kept, lift_made, out_made = units(
            [lifted], dy_block, jnp.zeros((1,), jnp.int32), *unit_args
        )
    grad_lift, lift_all, active, grad_pre = move.collect(lift_made, kept)
    grad_units, up_sums = unit_grads(lift_all, grad_pre, active, dy_block, at)
    units_part = scatter_sum(grad_units.reshape(-1, depth))

    grad_middle, grad_mix, grad_w_out, early = own_backward(
        grad_lift, middle, dy_block, at, norm2_gain, out_weight, mixed
    )
    out_made, grad_mix = tie(out_made, grad_mix)
    out_terms = move.collect(out_made)
    grad_mix = move.to_heads(grad_mix, rows)
    grad_w_out = move.collect(list(grad_w_out))

    *norm_parts, grad_w_cols, col_sums = attend_back(
        qkv, mixture, grad_mix, lse, normed, w_cols, grad_w_out, order, part, heads, rows
    )
    norm_parts[0], units_part, *out_terms = tie(norm_parts[0], units_part, *out_terms)
    output = add_all([*out_terms, middle, b_down]).astype(BF)
    left, right, grad_w_cols = move.last_sums(norm_parts, grad_w_cols)
    grad_w_cols = grad_w_cols.astype(F4)
    grad_units = gather_back(units_part).astype(F4).reshape(2, depth, -1)
    grad_w_qkv = jnp.stack([grad_w_cols[:, i * LANE : i * LANE + width] for i in range(3)])
    grad_w_out = jnp.concatenate(
        [grad_w_cols[:, i * LANE + width : (i + 1) * LANE] for i in range(3)], 1
    ).T

    input_grad, late = last_norm(left, right, x, at, pass_embed, norm1_gain, grad_middle)
    sums = move.sum_small(
        jnp.concatenate([late[:3], early[:4]], 0),
        jnp.concatenate([up_sums[:1], col_sums[:1]], 0),
    )
    grad_b_qv = jnp.stack([sums[8, :width], sums[8, 2 * LANE : 2 * LANE + width]])
    return (
        output[None],
        input_grad[None],
        sums[0],
        sums[1],
        sums[2],
        grad_w_qkv,
        grad_b_qv,
        grad_w_out,
        sums[3],
        sums[4],
        sums[5],
        grad_units[0],
        sums[7],
        grad_units[1],
        sums[6],
    )


def solution(mesh):
    return jax.shard_map(
        local,
        mesh=mesh,
        in_specs=(
            P("dp", "seq", None),
            P(),
            P(),
            P(),
            P(None, None, "tensor"),
            P(None, "tensor"),
            P("tensor", None),
            P(),
            P(),
            P(),
            P(None, "tensor"),
            P("tensor"),
            P("tensor", None),
            P(),
            P("dp", "seq", None),
            P("dp", None),
            P("dp", None),
        ),
        out_specs=(
            P("dp", ("seq", "tensor"), None),
            P("dp", ("seq", "tensor"), None),
            P(),
            P(),
            P(),
            P(None, None, "tensor"),
            P(None, "tensor"),
            P("tensor", None),
            P(),
            P(),
            P(),
            P(None, "tensor"),
            P("tensor"),
            P("tensor", None),
            P(),
        ),
        check_vma=False,
    )
```

```python
import functools

import jax
import jax.numpy as jnp
from jax import lax
from jax.experimental import pallas as pl
from jax.experimental.pallas import tpu as pltpu
from jax.sharding import PartitionSpec as P

HD = 64
BLK = 256
TRUNK_BLOCKS = 4
LANE = 256
PIECES = 8
EPS = 1e-05
ROOT = 0.7978845608028654
BF = jnp.bfloat16
F4 = jnp.float32
NT = (((1,), (1,)), ((), ()))
NN = (((1,), (0,)), ((), ()))
TN = (((0,), (0,)), ((), ()))
LIGHT = pl.CostEstimate(flops=1000, bytes_accessed=1000, transcendentals=0)


def takes(us):
    return pl.CostEstimate(flops=int(us * 1.1e9), bytes_accessed=1000, transcendentals=0)


def in_hbm(values):
    return pltpu.with_memory_space_constraint(values, pltpu.HBM)


def in_vmem_space(values):
    return pltpu.with_memory_space_constraint(values, pltpu.VMEM)


def dot(left, right, dims=NN):
    return lax.dot_general(left, right, dims, preferred_element_type=F4)


def norm_stats(values):
    row_mean = jnp.mean(values, -1, keepdims=True)
    centred = values - row_mean
    inv_std = lax.rsqrt(jnp.mean(centred * centred, -1, keepdims=True) + EPS)
    return (centred * inv_std, inv_std)


def norm_back(grad_out, normal, inv_std, gain_vec):
    scaled = grad_out * gain_vec
    return inv_std * (
        scaled
        - jnp.mean(scaled, -1, keepdims=True)
        - normal * jnp.mean(scaled * normal, -1, keepdims=True)
    )


def gelu_parts(pre_act):
    cubic_term = 0.044715 * pre_act * pre_act * pre_act
    tangent = jnp.tanh(ROOT * (pre_act + cubic_term))
    gelu_value = 0.5 * pre_act * (1.0 + tangent)
    gelu_slope = 0.5 * (1.0 + tangent) + 0.5 * pre_act * (1.0 - tangent * tangent) * ROOT * (
        1.0 + 3.0 * 0.044715 * pre_act * pre_act
    )
    return (gelu_value, gelu_slope)


def block_rows(pos, count=1):
    return pl.ds(pl.multiple_of(pos * BLK, BLK), count * BLK)


def head_masks(shape, heads):
    lane = lax.broadcasted_iota(jnp.int32, shape, 1) // HD
    return [lane == h for h in range(heads)]


def each_tile(order_ref, tile):
    trunk = [order_ref[i] for i in range(TRUNK_BLOCKS)]
    base = order_ref[16]
    tile(trunk[0], trunk[1], [], [(trunk[0], True)], [(trunk[0], False), (trunk[1], True)])
    tile(
        trunk[2],
        trunk[3],
        [(trunk[0], 2)],
        [(trunk[2], True)],
        [(trunk[2], False), (trunk[3], True)],
    )

    def deep(i, carry):
        one, two = order_ref[4 + 2 * i], order_ref[5 + 2 * i]
        above = order_ref[jnp.maximum(2 + i, 4)]
        tile(one, two, [(base, 4), (above, 1)], [(one, True)], [(two, True)], i >= 2)
        return carry

    lax.fori_loop(0, 6, deep, 0)


def lanes_of(arrays):
    return [a[:, i : i + 128] for a in arrays for i in range(0, a.shape[1], 128)]


def attend_kernel(heads, rows, count, order_ref, part_ref, *refs):
    out_ref, lse_ref, kt_ref, all_ref, normed_ref, qkv_ref, sems = refs[2 * count :]
    part = part_ref[0]
    length = qkv_ref.shape[0]
    start = 0
    copies = []
    for piece, normed in zip(refs[:count], refs[count : 2 * count]):
        at = pl.ds(start, piece.shape[0])
        for one, whole in ((piece, all_ref), (normed, normed_ref)):
            copies.append(pltpu.make_async_copy(one, whole.at[at], sems.at[len(copies)]))
            copies[-1].start()
        qkv_ref[at] = piece[...]
        start += piece.shape[0]

    def turn(i, carry):
        at = pl.ds(pl.multiple_of(i * 512, 512), 512)
        kt_ref[:, at] = jnp.transpose(qkv_ref[at, LANE : 2 * LANE])
        return carry

    lax.fori_loop(0, length // 512, turn, 0)

    def q_at(pos):
        return qkv_ref[pl.ds(pl.multiple_of(pos * BLK + part * rows, rows), rows), 0:LANE]

    def k_at(pos, count=1):
        return kt_ref[:, block_rows(pos, count)]

    def v_at(pos, count=1):
        return qkv_ref[block_rows(pos, count), 2 * LANE : 3 * LANE]

    row_at = lax.broadcasted_iota(jnp.int32, (rows, BLK), 0) + part * rows
    causal = row_at >= lax.broadcasted_iota(jnp.int32, (rows, BLK), 1)
    masks = head_masks((2 * rows, LANE), heads)

    def tile(first, second, shared, parts_a, parts_b, use_last=None):
        q = jnp.concatenate([q_at(first), q_at(second)], 0) * BF(0.125)
        result = jnp.zeros((2 * rows, LANE), F4)
        log_cols = []
        for h in range(heads):
            qm = jnp.where(masks[h], q, BF(0))
            wide = [dot(qm, k_at(p, c)) for p, c in shared]
            if use_last is not None:
                wide[-1] = wide[-1] + jnp.where(use_last, 0.0, -jnp.inf)
            own = []
            for cut, parts in ((qm[:rows], parts_a), (qm[rows:], parts_b)):
                scores = [dot(cut, k_at(p)) for p, _ in parts]
                own.append(
                    [jnp.where(causal, s, -jnp.inf) if d else s for s, (_, d) in zip(scores, parts)]
                )
            top = jnp.concatenate([functools.reduce(jnp.maximum, lanes_of(o)) for o in own], 0)
            top = functools.reduce(jnp.maximum, lanes_of(wide), top)
            top = jnp.max(top, 1, keepdims=True)
            mix = []
            sums = []
            for i, parts in enumerate((parts_a, parts_b)):
                cut = top[i * rows : (i + 1) * rows]
                es = [jnp.exp(s - cut) for s in own[i]]
                sums.append(functools.reduce(jnp.add, lanes_of(es)))
                terms = [dot(e.astype(BF), v_at(p)) for e, (p, _) in zip(es, parts)]
                mix.append(functools.reduce(jnp.add, terms))
            mix = jnp.concatenate(mix, 0)
            total = jnp.concatenate(sums, 0)
            for s, (p, c) in zip(wide, shared):
                e = jnp.exp(s - top)
                total = functools.reduce(jnp.add, lanes_of([e]), total)
                mix = mix + dot(e.astype(BF), v_at(p, c))
            total = jnp.sum(total, 1, keepdims=True)
            result = jnp.where(masks[h], mix / total, result)
            log_cols.append(top + jnp.log(total))
        low = result.astype(BF)[:, : heads * HD]
        out_ref[first] = low[:rows]
        out_ref[second] = low[rows:]
        lane = lax.broadcasted_iota(jnp.int32, (2 * rows, 128), 1)
        cols = jnp.zeros((2 * rows, 128), F4)
        for h in range(heads):
            cols = jnp.where(lane == h, log_cols[h], cols)
        flat = jnp.transpose(cols)[:8]
        lse_ref[first] = flat[:, :rows]
        lse_ref[second] = flat[:, rows:]

    each_tile(order_ref, tile)
    for copy in copies:
        copy.wait()


def in_vmem(count):
    return [pl.BlockSpec(memory_space=pltpu.VMEM)] * count


def in_smem(count):
    return [pl.BlockSpec(memory_space=pltpu.SMEM)] * count


def attend(pieces, order, part, heads, rows):
    normed, qkv = zip(*pieces)
    length = sum(q.shape[0] for q in qkv)
    blocks = length // BLK
    return pl.pallas_call(
        functools.partial(attend_kernel, heads, rows, len(pieces)),
        out_shape=(
            pltpu.HBM((blocks, rows, heads * HD), BF),
            pltpu.HBM((blocks, 8, rows), F4),
            pltpu.VMEM((LANE, length), BF),
            pltpu.HBM((length, 3 * LANE), BF),
            pltpu.HBM((length, normed[0].shape[1]), BF),
        ),
        in_specs=in_smem(2) + in_vmem(2 * len(pieces)),
        out_specs=in_vmem(3) + [pl.BlockSpec(memory_space=pltpu.HBM)] * 2,
        scratch_shapes=[
            pltpu.VMEM((length, 3 * LANE), BF),
            pltpu.SemaphoreType.DMA((2 * len(pieces),)),
        ],
        compiler_params=pltpu.CompilerParams(vmem_limit_bytes=26 << 20),
        cost_estimate=takes(25),
        name="tree_attend",
    )(order, part, *[in_vmem_space(v) for v in qkv + normed])


def attend_back_kernel(heads, rows, order_ref, part_ref, *refs):
    all_ref, kt_ref, mix_ref, grad_ref, lse_ref, far_normed_ref, w_ref = refs[:7]
    norm_refs = refs[7:11]
    proj_ref, sum_ref, acc_q, acc_k, acc_v, acc_w, wt_ref, qkv_ref, normed_ref, sems = refs[11:]
    bring = pltpu.make_async_copy(all_ref, qkv_ref, sems.at[0])
    bring.start()
    bring_normed = pltpu.make_async_copy(far_normed_ref, normed_ref, sems.at[1])
    length = qkv_ref.shape[0]
    part = part_ref[0]
    width = heads * HD

    def q_rows(pos):
        return pl.ds(pl.multiple_of(pos * BLK + part * rows, rows), rows)

    def k_at(pos, count=1):
        return qkv_ref[block_rows(pos, count), LANE : 2 * LANE]

    def v_at(pos, count=1):
        return qkv_ref[block_rows(pos, count), 2 * LANE : 3 * LANE]

    key_at = lax.broadcasted_iota(jnp.int32, (BLK, rows), 0)
    causal = (lax.broadcasted_iota(jnp.int32, (BLK, rows), 1) + part * rows) >= key_at
    masks = head_masks((2 * rows, LANE), heads)
    row_head = lax.broadcasted_iota(jnp.int32, (LANE, 2 * rows), 0) // HD
    acc_k[...] = jnp.zeros_like(acc_k)
    acc_v[...] = jnp.zeros_like(acc_v)
    acc_q[...] = jnp.zeros_like(acc_q)
    pad = jnp.zeros((2 * rows, LANE - width), BF)
    wt_ref[...] = jnp.transpose(w_ref[...])
    bring.wait()
    bring_normed.start()

    def tile(first, second, shared, parts_a, parts_b, use_last=None):
        q = jnp.concatenate(
            [qkv_ref[q_rows(first), 0:LANE], qkv_ref[q_rows(second), 0:LANE]], 0
        ) * BF(0.125)
        grad = jnp.concatenate([jnp.concatenate([grad_ref[first], grad_ref[second]], 0), pad], 1)
        mix = jnp.concatenate([jnp.concatenate([mix_ref[first], mix_ref[second]], 0), pad], 1)
        qt, gt, mt = jnp.transpose(q), jnp.transpose(grad), jnp.transpose(mix)
        terms = gt.astype(F4) * mt.astype(F4)
        inner = [
            jnp.sum(terms[h * HD : (h + 1) * HD], 0, keepdims=True) for h in range(heads)
        ]
        lse = jnp.concatenate([lse_ref[first], lse_ref[second]], 1)
        qms = [jnp.where(masks[h], q, BF(0)) for h in range(heads)]
        gms = [jnp.where(masks[h], grad, BF(0)) for h in range(heads)]
        qts = [jnp.where(row_head == h, qt, BF(0)) for h in range(heads)]
        gts = [jnp.where(row_head == h, gt, BF(0)) for h in range(heads)]

        def pieces(keys, values, h, cut, diag, bias):
            e = jnp.exp(dot(keys, qts[h][:, cut]) - (lse[h : h + 1, cut] + bias))
            if diag:
                e = jnp.where(causal, e, 0.0)
            t = dot(values, gts[h][:, cut])
            return e.astype(BF), (e * (t - inner[h][:, cut])).astype(BF)

        def strip(pos, count, cut, diag, grad_q, bias=0.0):
            keys, values = k_at(pos, count), v_at(pos, count)
            es = []
            ds = []
            for h in range(heads):
                e, d = pieces(keys, values, h, cut, diag, bias)
                es.append(e)
                ds.append(d)
                head_keys = kt_ref[h * HD : (h + 1) * HD, block_rows(pos, count)]
                grad_q[h] = grad_q[h] + dot(head_keys, d)
            acc_v[block_rows(pos, count), :] += dot(
                jnp.concatenate(es, 1), jnp.concatenate([g[cut] for g in gms], 0)
            )
            acc_k[block_rows(pos, count), :] += dot(
                jnp.concatenate(ds, 1), jnp.concatenate([g[cut] for g in qms], 0)
            )
            return grad_q

        grad_q = [jnp.zeros((HD, 2 * rows), F4) for _ in range(heads)]
        for i, (pos, count) in enumerate(shared):
            bias = 0.0
            if use_last is not None and i == len(shared) - 1:
                bias = jnp.where(use_last, 0.0, jnp.inf)
            grad_q = strip(pos, count, slice(0, 2 * rows), False, grad_q, bias)
        halves = []
        for i, parts in enumerate((parts_a, parts_b)):
            half = [jnp.zeros((HD, rows), F4) for _ in range(heads)]
            for pos, diag in parts:
                half = strip(pos, 1, slice(i * rows, (i + 1) * rows), diag, half)
            halves.append(half)
        grad_q = jnp.concatenate(
            [g + jnp.concatenate([a, b], 1) for g, a, b in zip(grad_q, *halves)]
            + [jnp.zeros((LANE - width, 2 * rows), F4)],
            0,
        )
        grad_q = jnp.transpose((grad_q * 0.125).astype(BF))
        acc_q[q_rows(first), :] = grad_q[:rows]
        acc_q[q_rows(second), :] = grad_q[rows:]

    each_tile(order_ref, tile)

    half = w_ref.shape[0] // 2
    size = length // PIECES
    acc_w[...] = jnp.zeros_like(acc_w)
    sum_ref[...] = jnp.zeros_like(sum_ref)
    bring_normed.wait()

    def pair(i, carry):
        for odd in range(2):
            at = pl.ds(pl.multiple_of((2 * i + odd) * size, size), size)
            grads = jnp.concatenate(
                [acc_q[at, :], acc_k[at, :].astype(BF), acc_v[at, :].astype(BF)], 1
            )
            spot = pl.ds(pl.multiple_of(i * size, size), size)
            for side in range(2):
                low = dot(grads, wt_ref[:, side * half : (side + 1) * half]).astype(BF)
                norm_refs[2 * side + odd][spot, :] = low
            acc_w[...] += dot(normed_ref[at, :], grads, TN)
            sum_ref[0:1, :] += jnp.sum(grads.astype(F4), 0, keepdims=True)
        return carry

    lax.fori_loop(0, PIECES // 2, pair, 0)
    proj_ref[...] = acc_w[...].astype(BF)


def attend_back(qkv, keys, mix, grad, lse, normed, weight, order, part, heads, rows):
    length, depth = normed.shape
    half = jax.ShapeDtypeStruct((length // 2, depth // 2), BF)
    return pl.pallas_call(
        functools.partial(attend_back_kernel, heads, rows),
        out_shape=(
            half,
            half,
            half,
            half,
            jax.ShapeDtypeStruct((depth, 3 * LANE), BF),
            jax.ShapeDtypeStruct((8, 3 * LANE), F4),
        ),
        in_specs=in_smem(2)
        + [pl.BlockSpec(memory_space=pltpu.HBM)]
        + in_vmem(4)
        + [pl.BlockSpec(memory_space=pltpu.HBM)]
        + in_vmem(1),
        out_specs=in_vmem(6),
        scratch_shapes=[
            pltpu.VMEM((length, LANE), BF),
            pltpu.VMEM((length, LANE), F4),
            pltpu.VMEM((length, LANE), F4),
            pltpu.VMEM((depth, 3 * LANE), F4),
            pltpu.VMEM((3 * LANE, depth), BF),
            pltpu.VMEM((length, 3 * LANE), BF),
            pltpu.VMEM((length, depth), BF),
            pltpu.SemaphoreType.DMA((2,)),
        ],
        compiler_params=pltpu.CompilerParams(vmem_limit_bytes=48 << 20),
        cost_estimate=takes(0.1),
        name="tree_attend_back",
    )(
        order,
        part,
        qkv,
        in_vmem_space(keys),
        mix,
        grad,
        lse,
        normed,
        weight,
    )


def project_kernel(count, place_ref, *refs):
    x_refs = refs[:count]
    pass_ref, gain_ref, shift_ref, w_ref, b_ref = refs[count : count + 5]
    normed_ref, qkv_ref = refs[-2:]
    x = x_refs[0][...]
    for i in range(1, count):
        x = jnp.where(pl.program_id(0) == i, x_refs[i][...], x)
    normal, _ = norm_stats(x.astype(F4) + pass_ref[...])
    normed = (normal * gain_ref[...] + shift_ref[...]).astype(BF)
    normed_ref[...] = normed
    qkv_ref[...] = (dot(normed, w_ref[...]) + b_ref[...]).astype(BF)


def project(pieces, place, pass_embed, gain, shift, weight, bias):
    width = weight.shape[1]
    depth = weight.shape[0]
    count = len(pieces)
    step = pieces[0].shape[0] if count > 1 else min(512, pieces[0].shape[0])
    if count > 1:
        specs = [whole_spec((step, depth))] * count
    else:
        specs = [pl.BlockSpec((step, depth), lambda i, place: (place[i], 0))]
    length = step * place.shape[0]
    vec = vec_spec(depth)
    return pl.pallas_call(
        functools.partial(project_kernel, count),
        out_shape=(pltpu.VMEM((length, depth), BF), pltpu.VMEM((length, width), BF)),
        grid_spec=grid_of(
            length // step,
            specs + [vec, vec, vec, whole_spec((depth, width)), vec_spec(width)],
            (own_rows_spec(depth, step), own_rows_spec(width, step)),
        ),
        compiler_params=pltpu.CompilerParams(vmem_limit_bytes=20 << 20),
        cost_estimate=takes(5),
        name="norm_project",
    )(place, *pieces, pass_embed[None], gain[None], shift[None], weight, bias[None])


def vec_spec(depth):
    return pl.BlockSpec((1, depth), lambda i, at: (0, 0))


def own_rows_spec(depth, step, fixed=False):
    if fixed:
        return pl.BlockSpec((step, depth), lambda i, at: (at[0] + i, 0))
    return pl.BlockSpec((step, depth), lambda i, at: (i, 0))


def pieces_spec(count, step, width):
    return pl.BlockSpec((count, step, width), lambda i, at: (0, i, 0))


def whole_spec(shape):
    return pl.BlockSpec(shape, lambda i, at: (0,) * len(shape))


def grid_of(steps, ins, outs, scratch=()):
    return pltpu.PrefetchScalarGridSpec(
        num_scalar_prefetch=1,
        grid=(steps,),
        in_specs=ins,
        out_specs=outs,
        scratch_shapes=list(scratch),
    )


def own_forward_kernel(
    count, at_ref, x_ref, pass_ref, mix_ref, w_ref, b_ref, gain_ref, shift_ref, mid_ref, lift_ref
):
    middle = x_ref[...].astype(F4) + pass_ref[...] + b_ref[...]
    for r in range(count):
        middle = middle + dot(mix_ref[r], w_ref[r])
    mid_ref[...] = middle
    normal, _ = norm_stats(middle)
    lift_ref[...] = (normal * gain_ref[...] + shift_ref[...]).astype(BF)


def own_forward(x, at, pass_embed, mixed, weight, bias, gain, shift):
    count, sub, width = mixed.shape
    depth = x.shape[1]
    step = min(512, sub)
    vec = vec_spec(depth)
    return pl.pallas_call(
        functools.partial(own_forward_kernel, count),
        out_shape=(
            pltpu.HBM((sub, depth), F4),
            jax.ShapeDtypeStruct((sub, depth), BF),
        ),
        grid_spec=grid_of(
            sub // step,
            [
                own_rows_spec(depth, step, True),
                vec,
                pieces_spec(count, step, width),
                whole_spec(weight.shape),
                vec,
                vec,
                vec,
            ],
            (own_rows_spec(depth, step), own_rows_spec(depth, step)),
        ),
        cost_estimate=takes(3),
        compiler_params=pltpu.CompilerParams(vmem_limit_bytes=14 << 20),
        name="own_forward",
    )(at * (sub // step), x, pass_embed[None], mixed, weight, bias[None], gain[None], shift[None])


def own_backward_kernel(count, parts, at_ref, *refs):
    grad_parts = refs[:parts]
    mid_ref, dy_ref, gain_ref, w_ref, mix_ref, gm_ref, gmix_ref, gw_ref, sums_ref, acc = refs[parts:]
    step = pl.program_id(0)

    @pl.when(step == 0)
    def _():
        acc[...] = jnp.zeros_like(acc)
        sums_ref[...] = jnp.zeros_like(sums_ref)

    grad_lift = functools.reduce(jnp.add, [g[...].astype(F4) for g in grad_parts])
    normal, inv = norm_stats(mid_ref[...])
    dy = dy_ref[...].astype(F4)
    grad_middle = dy + norm_back(grad_lift, normal, inv, gain_ref[...])
    gm_ref[...] = grad_middle
    low = grad_middle.astype(BF)
    for r in range(count):
        gmix_ref[r] = dot(low, w_ref[r], NT).astype(BF)
        acc[r] += dot(low, mix_ref[r], TN)
    for i, values in enumerate((grad_middle, grad_lift * normal, grad_lift, dy)):
        sums_ref[i : i + 1, :] += jnp.sum(values, 0, keepdims=True)

    @pl.when(step == pl.num_programs(0) - 1)
    def _():
        gw_ref[...] = acc[...].astype(BF)


def own_backward(grad_parts, middle, dy, at, gain, weight, mixed):
    count, sub, width = mixed.shape
    depth = dy.shape[1]
    step = min(512, sub)
    rows = own_rows_spec(depth, step)
    return pl.pallas_call(
        functools.partial(own_backward_kernel, count, len(grad_parts)),
        out_shape=(
            pltpu.HBM((sub, depth), F4),
            jax.ShapeDtypeStruct((count, sub, width), BF),
            jax.ShapeDtypeStruct((count, depth, width), BF),
            jax.ShapeDtypeStruct((8, depth), F4),
        ),
        grid_spec=grid_of(
            sub // step,
            [rows] * len(grad_parts)
            + [
                rows,
                own_rows_spec(depth, step, True),
                vec_spec(depth),
                whole_spec(weight.shape),
                pieces_spec(count, step, width),
            ],
            (
                rows,
                pieces_spec(count, step, width),
                whole_spec((count, depth, width)),
                whole_spec((8, depth)),
            ),
            [pltpu.VMEM((count, depth, width), F4)],
        ),
        cost_estimate=takes(6),
        compiler_params=pltpu.CompilerParams(vmem_limit_bytes=18 << 20),
        name="own_backward",
    )(at * (sub // step), *grad_parts, in_hbm(middle), dy, gain[None], weight, mixed)


def last_norm_kernel(counts, at_ref, *refs):
    split = counts[0]
    left, right = refs[:split], refs[split : split + counts[1]]
    x_ref, pass_ref, gain_ref, gm_ref, out_ref, sums_ref = refs[split + counts[1] :]

    @pl.when(pl.program_id(0) == 0)
    def _():
        sums_ref[...] = jnp.zeros_like(sums_ref)

    grad_norm = jnp.concatenate(
        [functools.reduce(jnp.add, [g[...].astype(F4) for g in side]) for side in (left, right)], 1
    )
    normal, inv = norm_stats(x_ref[...].astype(F4) + pass_ref[...])
    grad_resid = gm_ref[...] + norm_back(grad_norm, normal, inv, gain_ref[...])
    out_ref[...] = grad_resid.astype(BF)
    for i, values in enumerate((grad_resid, grad_norm * normal, grad_norm)):
        sums_ref[i : i + 1, :] += jnp.sum(values, 0, keepdims=True)


def last_norm(left, right, x, at, pass_embed, gain, grad_middle):
    sub, depth = grad_middle.shape
    step = min(512, sub)
    return pl.pallas_call(
        functools.partial(last_norm_kernel, (len(left), len(right))),
        out_shape=(
            jax.ShapeDtypeStruct((sub, depth), BF),
            jax.ShapeDtypeStruct((8, depth), F4),
        ),
        grid_spec=grid_of(
            sub // step,
            [own_rows_spec(depth // 2, step)] * (len(left) + len(right))
            + [
                own_rows_spec(depth, step, True),
                vec_spec(depth),
                vec_spec(depth),
                own_rows_spec(depth, step),
            ],
            (own_rows_spec(depth, step), whole_spec((8, depth))),
        ),
        compiler_params=pltpu.CompilerParams(vmem_limit_bytes=14 << 20),
        name="last_norm",
    )(at * (sub // step), *left, *right, x, pass_embed[None], gain[None], in_hbm(grad_middle))


def units_kernel(count, place_ref, *refs):
    lift_refs = refs[:count]
    dy_ref, up_ref, bias_ref, down_ref, active_ref, pre_ref = refs[count : count + 6]
    outs = refs[count + 6 :]
    step = pl.program_id(0)
    lifted = lift_refs[0][...]
    for i in range(1, count):
        lifted = jnp.where(step == i, lift_refs[i][...], lifted)
    pre_act = dot(lifted, up_ref[...]) + bias_ref[...]
    value, slope = gelu_parts(pre_act)
    active = value.astype(BF)
    active_ref[...] = active
    size = lifted.shape[0]
    dy = dy_ref[pl.ds(pl.multiple_of(place_ref[step] * size, size), size), :]
    grad_pre = (dot(dy, down_ref[...], NT) * slope).astype(BF)
    pre_ref[...] = grad_pre
    grad_lift = dot(grad_pre, up_ref[...], NT).astype(BF)
    out = dot(active, down_ref[...]).astype(BF)
    for i in range(count):

        @pl.when(step == i)
        def _():
            outs[i][...] = grad_lift
            outs[count + i][...] = out


def units(lifted, dy, place, w_up, b_up, w_down):
    step, depth = lifted[0].shape
    count = len(lifted)
    wide = w_up.shape[1]
    piece = whole_spec((step, depth))
    specs = [piece] * count
    specs += [pl.BlockSpec(memory_space=pltpu.VMEM)] * 4
    made = pl.pallas_call(
        functools.partial(units_kernel, count),
        out_shape=(pltpu.VMEM((count * step, wide), BF),) * 2
        + (jax.ShapeDtypeStruct((step, depth), BF),) * (2 * count),
        grid_spec=grid_of(
            count, specs, (own_rows_spec(wide, step),) * 2 + (piece,) * (2 * count)
        ),
        compiler_params=pltpu.CompilerParams(vmem_limit_bytes=22 << 20),
        cost_estimate=takes(10),
        name="units",
    )(place, *lifted, *[in_vmem_space(v) for v in (dy, w_up)], b_up[None], in_vmem_space(w_down))
    return made[:2], made[2 : 2 + count], made[2 + count :]


def unit_grads_kernel(groups, place_ref, dy_ref, *refs):
    out_ref, sum_ref, acc = refs[-3:]
    acc[...] = jnp.zeros_like(acc)
    sum_ref[...] = jnp.zeros_like(sum_ref)
    refs = list(refs[:-3])
    piece = 0
    for count in groups:
        lift_refs = refs[:count]
        active_ref, pre_ref = refs[count : count + 2]
        refs = refs[count + 2 :]
        size = lift_refs[0].shape[0]
        part = min(BLK, size)
        for i in range(count):

            def rows(j, carry):
                near = pl.ds(pl.multiple_of(j * part, part), part)
                here = pl.ds(pl.multiple_of(i * size + j * part, part), part)
                there = pl.ds(pl.multiple_of(place_ref[piece] * size + j * part, part), part)
                pre = pre_ref[here, :]
                acc[0] += dot(lift_refs[i][near, :], pre, TN)
                acc[1] += dot(active_ref[here, :], dy_ref[there, :], TN)
                sum_ref[0:1, :] += jnp.sum(pre.astype(F4), 0, keepdims=True)
                return carry

            lax.fori_loop(0, size // part, rows, 0)
            piece += 1
    out_ref[...] = acc[...].astype(BF)


def unit_grads(groups, dy, place):
    depth = dy.shape[1]
    wide = groups[0][1][0].shape[1]
    operands = []
    for lifted, made in groups:
        operands += [in_vmem_space(v) for v in (*lifted, *made)]
    return pl.pallas_call(
        functools.partial(unit_grads_kernel, [len(g[0]) for g in groups]),
        out_shape=(
            pltpu.HBM((2, depth, wide), BF),
            jax.ShapeDtypeStruct((8, wide), F4),
        ),
        in_specs=in_smem(1) + in_vmem(1 + len(operands)),
        out_specs=in_vmem(2),
        scratch_shapes=[pltpu.VMEM((2, depth, wide), F4)],
        compiler_params=pltpu.CompilerParams(vmem_limit_bytes=18 << 20),
        cost_estimate=takes(8),
        name="unit_grads",
    )(place, in_vmem_space(dy), *operands)


def send(values, axis, partner):
    size = lax.axis_size(axis)
    return lax.ppermute(values, axis, [(i, partner(i)) for i in range(size)])


def hop(values, step):
    return send(values, "tensor", lambda i: i ^ step)


def cross(values):
    return send(values, "seq", lambda i: i ^ 1)


def both(values, step_seq, step_tensor):
    return send(
        values, ("seq", "tensor"), lambda i: (i // 4 ^ step_seq) * 4 + (i % 4 ^ step_tensor)
    )


def add_low(left, right):
    return (left.astype(F4) + right.astype(F4)).astype(BF)


def add_all(arrays):
    return functools.reduce(jnp.add, [a.astype(F4) for a in arrays])


def tie(*values):
    return lax.optimization_barrier(values)


def slot(values, index, size, axis=0):
    return lax.dynamic_slice_in_dim(values, index * size, size, axis)


class Paired:
    def __init__(self, block_len):
        self.me = lax.axis_index("seq")
        self.rank = lax.axis_index("tensor")
        self.sub = block_len // 4
        self.per = self.sub // BLK

    def position(self, natural, blocks):
        half = blocks // 2
        s, b = natural // half, natural % half
        return half * (s ^ self.me) + self.per * ((b // self.per) ^ self.rank) + b % self.per

    def place(self):
        return jnp.stack([self.rank ^ r for r in range(4)]).astype(jnp.int32)

    def far(self, values):
        mine = cross(slot(values, self.rank, self.sub))
        other = hop(mine, 2)
        return mine, hop(mine, 1), other

    def gather_weight(self, own):
        return jnp.stack([own, hop(own, 1), hop(own, 2), hop(own, 3)])

    def collect(self, piece, after=None):
        away = add_low(piece[2], hop(piece[3], 1))
        terms = [piece[0], hop(piece[1], 1), hop(away, 2)]
        return terms if after is None else (terms, *tie(*after, away)[:-1])

    def halves(self, values, axis, bit, after=()):
        half = values.shape[0] // 2
        at = lax.axis_index(axis) >> bit & 1
        away = send(slot(values, 1 - at, half), axis, lambda i: i ^ (1 << bit))
        if after:
            away = tie(away, *after)[0]
        return add_low(slot(values, at, half), away)

    def doubled(self, values, axis, bit):
        at = lax.axis_index(axis) >> bit & 1
        other = send(values, axis, lambda i: i ^ (1 << bit))
        return jnp.concatenate(
            [jnp.where(at == 0, values, other), jnp.where(at == 0, other, values)], 0
        )

    def last_sums(self, parts, values, early):
        steps = [("dp", 0), ("seq", 0)]
        steps += [("dp", bit) for bit in range(1, lax.axis_size("dp").bit_length() - 1)]
        one = add_low(parts[0], hop(parts[1], 1))
        keep, early = tie(parts[2], early, one)[:2]
        two = add_low(keep, hop(parts[3], 1))
        values = self.halves(values, *steps[0], (one, two))
        one, two = [c.reshape(2, 2, self.sub, -1) for c in (one, two)]
        one = add_low(one[0], cross(one[1]))
        two = add_low(two[:, 0], hop(two[:, 1], 2))
        for step in steps[1:]:
            values = self.halves(values, *step)
        left = [one[0], hop(one[1], 2)]
        right = [two[0], cross(two[1])]
        for step in steps[::-1]:
            values = self.doubled(values, *step)
        return left, right, values, early

    def sum_small(self, shared, ranked, beside):
        shared = shared + hop(shared, 1)
        shared = shared + hop(shared, 2)
        values, *beside = tie(jnp.concatenate([shared, ranked], 0), *beside)
        values = values + cross(values)
        dp = lax.axis_size("dp")
        others = [
            lax.ppermute(values, "dp", [(i, (i + r) % dp) for i in range(dp)])
            for r in range(1, dp)
        ]
        return functools.reduce(jnp.add, others, values), *beside

    def to_tokens(self, mixture):
        blocks, rows, width = mixture.shape
        piece = mixture.reshape(2, 4, self.per, rows, width)
        columns = []
        for r in range(4):
            here = piece[0, r] if r == 0 else both(piece[0, r], 0, r)
            there = both(piece[1, r], 1, r)
            first = jnp.where(self.me == 0, here, there)
            second = jnp.where(self.me == 0, there, here)
            columns.append(jnp.stack([first, second], 1).reshape(self.sub, width))
        return jnp.stack(columns)

    def to_heads(self, grads, rows):
        parts = grads.reshape(4, self.per, 2, rows, grads.shape[2])
        mine = jnp.where(self.me == 0, parts[:, :, 0], parts[:, :, 1])
        theirs = jnp.where(self.me == 0, parts[:, :, 1], parts[:, :, 0])
        here = [mine[r] if r == 0 else both(mine[r], 0, r) for r in range(4)]
        there = [both(theirs[r], 1, r) for r in range(4)]
        return jnp.concatenate(here + there, 0)


class Plain:
    def __init__(self, block_len):
        self.me = lax.axis_index("seq")
        self.rank = lax.axis_index("tensor")
        self.seq = lax.axis_size("seq")
        self.tensor = lax.axis_size("tensor")
        self.block_len = block_len
        self.sub = block_len // self.tensor

    def position(self, natural, blocks):
        return natural

    def gather_weight(self, own):
        return lax.all_gather(own, "tensor", axis=0)

    def collect(self, piece, after=None):
        whole = jnp.concatenate(piece, 0)
        terms = [lax.psum_scatter(whole, "tensor", scatter_dimension=0, tiled=True)]
        return terms if after is None else (terms, *after)

    def last_sums(self, parts, values, early):
        sides = []
        for keep, away in (parts[:2], parts[2:]):
            half = keep.shape[1]
            keep, away = [v.reshape(PIECES // 2, -1, half) for v in (keep, away)]
            whole = jnp.stack([keep, away], 1).reshape(-1, half)
            sides.append(
                [lax.psum_scatter(whole, ("seq", "tensor"), scatter_dimension=0, tiled=True)]
            )
        return *sides, lax.psum(values, ("dp", "seq")), early

    def sum_small(self, shared, ranked, beside):
        shared = lax.psum(shared, ("dp", "seq", "tensor"))
        return jnp.concatenate([shared, lax.psum(ranked, ("dp", "seq"))], 0), *beside

    def to_tokens(self, mixture):
        blocks, rows, width = mixture.shape
        full = lax.all_gather(mixture, ("seq", "tensor"), axis=0)
        full = full.reshape(self.seq, self.tensor, blocks, rows, width)
        full = full.transpose(1, 2, 0, 3, 4).reshape(self.tensor, -1, width)
        return slot(full, self.me * self.tensor + self.rank, self.sub, 1)

    def to_heads(self, grads, rows):
        full = lax.all_gather(grads, ("seq", "tensor"), axis=1, tiled=True)
        full = full.reshape(self.tensor, -1, self.seq, rows, grads.shape[2])
        return slot(slot(full, self.me, 1, 2)[:, :, 0], self.rank, 1)[0]


def tree_order(seg_row, parent_row, position):
    blocks = seg_row.shape[0] // BLK
    segs = parent_row.shape[0]
    slot_seg = seg_row[::BLK]
    labels = jnp.arange(segs, dtype=jnp.int32)
    above = jnp.sum(jnp.where(slot_seg[:, None] == labels[None, :], parent_row[None, :], 0), 1)
    natural = jnp.arange(blocks, dtype=jnp.int32)
    key = jnp.where(
        slot_seg == 0,
        natural,
        jnp.where(above == 0, 100 + slot_seg, 1000 + 16 * above + slot_seg),
    )
    rank = jnp.sum((key[None, :] < key[:, None]).astype(jnp.int32), 1)
    where = position(natural, blocks)
    order = jnp.sum(jnp.where(rank[:, None] == natural[None, :], where[:, None], 0), 0)
    base = order[0] // TRUNK_BLOCKS * TRUNK_BLOCKS
    return jnp.concatenate([order, base[None]]).astype(jnp.int32)


def padded(values, axis):
    widths = [(0, 0)] * values.ndim
    widths[axis] = (0, LANE - values.shape[axis])
    return jnp.pad(values, widths)


def total(values):
    return jnp.sum(values, axis=0)


def local(
    inputs,
    pass_embed,
    norm1_gain,
    norm1_shift,
    w_qkv,
    b_qv,
    w_out,
    b_out,
    norm2_gain,
    norm2_shift,
    w_up,
    b_up,
    w_down,
    b_down,
    out_grad,
    seg_id,
    parent,
):
    x = inputs[0]
    dy_block = out_grad[0]
    block_len, depth = x.shape
    length = seg_id.shape[1]
    seq, tensor = lax.axis_size("seq"), lax.axis_size("tensor")
    width = w_qkv.shape[2]
    heads = width // HD
    rows = BLK // seq
    paired = seq == 2 and tensor == 4 and block_len % (4 * BLK) == 0
    move = Paired(block_len) if paired else Plain(block_len)

    order = tree_order(seg_id[0], parent[0], move.position)
    part = move.me[None].astype(jnp.int32)

    w_cols = jnp.concatenate([padded(w_qkv[i], 1) for i in range(3)], 1)
    zero = jnp.zeros((LANE,), F4)
    b_cols = jnp.concatenate([padded(b_qv[0], 0), zero, padded(b_qv[1], 0)])
    norm_args = (pass_embed, norm1_gain, norm1_shift, w_cols, b_cols)
    if paired:
        mine, core, other = move.far(x)
        pair = jnp.arange(2, dtype=jnp.int32)
        pieces = [project([x], move.place(), *norm_args)]
        pieces.append(project(tie(mine, core, pieces[0][0])[:2], pair, *norm_args))
        other = tie(other, pieces[1][0])[0]
        pieces.append(project([other, hop(other, 1)], pair, *norm_args))
    else:
        full = lax.all_gather(x, "seq", axis=0, tiled=True)
        place = jnp.arange(pl.cdiv(length, 512), dtype=jnp.int32)
        pieces = [project([full], place, *norm_args)]

    mixture, lse, keys, qkv, normed = attend(pieces, order, part, heads, rows)

    at = move.rank[None].astype(jnp.int32)
    out_weight = move.gather_weight(w_out)
    mixed = move.to_tokens(mixture)
    middle, lifted_own = own_forward(
        x, at, pass_embed, mixed, out_weight, b_out, norm2_gain, norm2_shift
    )

    unit_args = (w_up, b_up, w_down)
    if paired:
        core, other = hop(lifted_own, 1), hop(lifted_own, 2)
        near = [lifted_own, core]
        place = move.place()
        near_kept, near_lift, near_out = units(near, dy_block, place[:2], *unit_args)
        other = tie(other, near_lift[1])[0]
        far = [hop(other, 1), other]
        far_place = place[:1:-1]
        far_kept, far_lift, far_out = units(far, dy_block, far_place, *unit_args)
        lift_made = [*near_lift, *far_lift[::-1]]
        out_made = [*near_out, *far_out[::-1]]
        place = jnp.concatenate([place[:2], far_place])
        groups = [(near, near_kept), (far, far_kept)]
    else:
        near = [lax.all_gather(lifted_own, "tensor", axis=0, tiled=True)]
        place = jnp.zeros((1,), jnp.int32)
        near_kept, lift_made, out_made = units(near, dy_block, place, *unit_args)
        groups = [(near, near_kept)]
    grad_lift, place = move.collect(lift_made, [place])
    grad_units, up_sums = unit_grads(groups, dy_block, place)
    units_sum = lax.psum(grad_units, ("dp", "seq"))

    grad_middle, grad_mix, grad_w_out, early = own_backward(
        grad_lift, middle, dy_block, at, norm2_gain, out_weight, mixed
    )
    out_made, grad_mix = tie(out_made, grad_mix)
    grad_mix = move.to_heads(grad_mix, rows)
    out_terms = move.collect(out_made)
    grad_w_out = move.collect(list(grad_w_out))
    grad_mix, *grad_w_out = tie(grad_mix, *grad_w_out)

    *norm_parts, grad_w_cols, col_sums = attend_back(
        qkv, keys, mixture, grad_mix, lse, normed, w_cols, order, part, heads, rows
    )
    *grad_w_out, grad_w_cols = tie(*grad_w_out, grad_w_cols)
    rest = add_all(grad_w_out).astype(BF)
    fill = LANE - width
    grad_w_cols = grad_w_cols + jnp.concatenate(
        [jnp.pad(rest[:, i * fill : (i + 1) * fill], ((0, 0), (width, 0))) for i in range(3)], 1
    )
    left, right, grad_w_cols, units_sum = move.last_sums(norm_parts, grad_w_cols, units_sum)
    grad_w_cols = grad_w_cols.astype(F4)
    grad_w_qkv = jnp.stack([grad_w_cols[:, i * LANE : i * LANE + width] for i in range(3)])
    grad_w_out = jnp.concatenate(
        [grad_w_cols[:, i * LANE + width : (i + 1) * LANE] for i in range(3)], 1
    ).T

    input_grad, late = last_norm(left, right, x, at, pass_embed, norm1_gain, grad_middle)
    sums, *out_terms = move.sum_small(
        jnp.concatenate([late[:3], early[:4]], 0),
        jnp.concatenate([up_sums[:1], col_sums[:1]], 0),
        out_terms,
    )
    output = add_all([*out_terms, middle, b_down]).astype(BF)
    grad_units = units_sum.astype(F4)
    grad_b_qv = jnp.stack([sums[8, :width], sums[8, 2 * LANE : 2 * LANE + width]])
    return (
        output[None],
        input_grad[None],
        sums[0],
        sums[1],
        sums[2],
        grad_w_qkv,
        grad_b_qv,
        grad_w_out,
        sums[3],
        sums[4],
        sums[5],
        grad_units[0],
        sums[7],
        grad_units[1],
        sums[6],
    )


def solution(mesh):
    return jax.shard_map(
        local,
        mesh=mesh,
        in_specs=(
            P("dp", "seq", None),
            P(),
            P(),
            P(),
            P(None, None, "tensor"),
            P(None, "tensor"),
            P("tensor", None),
            P(),
            P(),
            P(),
            P(None, "tensor"),
            P("tensor"),
            P("tensor", None),
            P(),
            P("dp", "seq", None),
            P("dp", None),
            P("dp", None),
        ),
        out_specs=(
            P("dp", ("seq", "tensor"), None),
            P("dp", ("seq", "tensor"), None),
            P(),
            P(),
            P(),
            P(None, None, "tensor"),
            P(None, "tensor"),
            P("tensor", None),
            P(),
            P(),
            P(),
            P(None, "tensor"),
            P("tensor"),
            P("tensor", None),
            P(),
        ),
        check_vma=False,
    )
```

```python
import functools

import jax
import jax.numpy as jnp
from jax import lax
from jax.experimental import pallas as pl
from jax.experimental.pallas import tpu as pltpu
from jax.sharding import PartitionSpec as P

HD = 64
BLK = 256
TRUNK_BLOCKS = 4
LANE = 256
PIECES = 8
EPS = 1e-05
ROOT = 0.7978845608028654
BF = jnp.bfloat16
F4 = jnp.float32
NT = (((1,), (1,)), ((), ()))
NN = (((1,), (0,)), ((), ()))
TN = (((0,), (0,)), ((), ()))
LIGHT = pl.CostEstimate(flops=1000, bytes_accessed=1000, transcendentals=0)


def takes(us):
    return pl.CostEstimate(flops=int(us * 1.1e9), bytes_accessed=1000, transcendentals=0)


def in_hbm(values):
    return pltpu.with_memory_space_constraint(values, pltpu.HBM)


def in_vmem_space(values):
    return pltpu.with_memory_space_constraint(values, pltpu.VMEM)


def dot(left, right, dims=NN):
    return lax.dot_general(left, right, dims, preferred_element_type=F4)


def norm_stats(values):
    row_mean = jnp.mean(values, -1, keepdims=True)
    centred = values - row_mean
    inv_std = lax.rsqrt(jnp.mean(centred * centred, -1, keepdims=True) + EPS)
    return (centred * inv_std, inv_std)


def norm_back(grad_out, normal, inv_std, gain_vec):
    scaled = grad_out * gain_vec
    return inv_std * (
        scaled
        - jnp.mean(scaled, -1, keepdims=True)
        - normal * jnp.mean(scaled * normal, -1, keepdims=True)
    )


def gelu_parts(pre_act):
    cubic_term = 0.044715 * pre_act * pre_act * pre_act
    tangent = jnp.tanh(ROOT * (pre_act + cubic_term))
    gelu_value = 0.5 * pre_act * (1.0 + tangent)
    gelu_slope = 0.5 * (1.0 + tangent) + 0.5 * pre_act * (1.0 - tangent * tangent) * ROOT * (
        1.0 + 3.0 * 0.044715 * pre_act * pre_act
    )
    return (gelu_value, gelu_slope)


def block_rows(pos, count=1):
    return pl.ds(pl.multiple_of(pos * BLK, BLK), count * BLK)


def head_masks(shape, heads):
    lane = lax.broadcasted_iota(jnp.int32, shape, 1) // HD
    return [lane == h for h in range(heads)]


def each_tile(order_ref, tile):
    trunk = [order_ref[i] for i in range(TRUNK_BLOCKS)]
    base = order_ref[16]
    tile(trunk[0], trunk[1], [], [(trunk[0], True)], [(trunk[0], False), (trunk[1], True)])
    tile(
        trunk[2],
        trunk[3],
        [(trunk[0], 2)],
        [(trunk[2], True)],
        [(trunk[2], False), (trunk[3], True)],
    )

    def deep(i, carry):
        one, two = order_ref[4 + 2 * i], order_ref[5 + 2 * i]
        above = order_ref[jnp.maximum(2 + i, 4)]
        tile(one, two, [(base, 4), (above, 1)], [(one, True)], [(two, True)], i >= 2)
        return carry

    lax.fori_loop(0, 6, deep, 0)


def lanes_of(arrays):
    return [a[:, i : i + 128] for a in arrays for i in range(0, a.shape[1], 128)]


def attend_kernel(heads, rows, count, order_ref, part_ref, *refs):
    out_ref, lse_ref, kt_ref, all_ref, normed_ref, qkv_ref, sems = refs[2 * count :]
    part = part_ref[0]
    length = qkv_ref.shape[0]
    start = 0
    copies = []
    for piece, normed in zip(refs[:count], refs[count : 2 * count]):
        at = pl.ds(start, piece.shape[0])
        for one, whole in ((piece, all_ref), (normed, normed_ref)):
            copies.append(pltpu.make_async_copy(one, whole.at[at], sems.at[len(copies)]))
            copies[-1].start()
        qkv_ref[at] = piece[...]
        start += piece.shape[0]

    def turn(i, carry):
        at = pl.ds(pl.multiple_of(i * 512, 512), 512)
        kt_ref[:, at] = jnp.transpose(qkv_ref[at, LANE : 2 * LANE])
        return carry

    lax.fori_loop(0, length // 512, turn, 0)

    def q_at(pos):
        return qkv_ref[pl.ds(pl.multiple_of(pos * BLK + part * rows, rows), rows), 0:LANE]

    def k_at(pos, count=1):
        return kt_ref[:, block_rows(pos, count)]

    def v_at(pos, count=1):
        return qkv_ref[block_rows(pos, count), 2 * LANE : 3 * LANE]

    row_at = lax.broadcasted_iota(jnp.int32, (rows, BLK), 0) + part * rows
    causal = row_at >= lax.broadcasted_iota(jnp.int32, (rows, BLK), 1)
    masks = head_masks((2 * rows, LANE), heads)

    def tile(first, second, shared, parts_a, parts_b, use_last=None):
        q = jnp.concatenate([q_at(first), q_at(second)], 0) * BF(0.125)
        result = jnp.zeros((2 * rows, LANE), F4)
        log_cols = []
        for h in range(heads):
            qm = jnp.where(masks[h], q, BF(0))
            wide = [dot(qm, k_at(p, c)) for p, c in shared]
            if use_last is not None:
                wide[-1] = wide[-1] + jnp.where(use_last, 0.0, -jnp.inf)
            own = []
            for cut, parts in ((qm[:rows], parts_a), (qm[rows:], parts_b)):
                scores = [dot(cut, k_at(p)) for p, _ in parts]
                own.append(
                    [jnp.where(causal, s, -jnp.inf) if d else s for s, (_, d) in zip(scores, parts)]
                )
            top = jnp.concatenate([functools.reduce(jnp.maximum, lanes_of(o)) for o in own], 0)
            top = functools.reduce(jnp.maximum, lanes_of(wide), top)
            top = jnp.max(top, 1, keepdims=True)
            mix = []
            sums = []
            for i, parts in enumerate((parts_a, parts_b)):
                cut = top[i * rows : (i + 1) * rows]
                es = [jnp.exp(s - cut) for s in own[i]]
                sums.append(functools.reduce(jnp.add, lanes_of(es)))
                terms = [dot(e.astype(BF), v_at(p)) for e, (p, _) in zip(es, parts)]
                mix.append(functools.reduce(jnp.add, terms))
            mix = jnp.concatenate(mix, 0)
            total = jnp.concatenate(sums, 0)
            for s, (p, c) in zip(wide, shared):
                e = jnp.exp(s - top)
                total = functools.reduce(jnp.add, lanes_of([e]), total)
                mix = mix + dot(e.astype(BF), v_at(p, c))
            total = jnp.sum(total, 1, keepdims=True)
            result = jnp.where(masks[h], mix / total, result)
            log_cols.append(top + jnp.log(total))
        low = result.astype(BF)[:, : heads * HD]
        out_ref[first] = low[:rows]
        out_ref[second] = low[rows:]
        lane = lax.broadcasted_iota(jnp.int32, (2 * rows, 128), 1)
        cols = jnp.zeros((2 * rows, 128), F4)
        for h in range(heads):
            cols = jnp.where(lane == h, log_cols[h], cols)
        flat = jnp.transpose(cols)[:8]
        lse_ref[first] = flat[:, :rows]
        lse_ref[second] = flat[:, rows:]

    each_tile(order_ref, tile)
    for copy in copies:
        copy.wait()


def in_vmem(count):
    return [pl.BlockSpec(memory_space=pltpu.VMEM)] * count


def in_smem(count):
    return [pl.BlockSpec(memory_space=pltpu.SMEM)] * count


def attend(pieces, order, part, heads, rows):
    normed, qkv = zip(*pieces)
    length = sum(q.shape[0] for q in qkv)
    blocks = length // BLK
    return pl.pallas_call(
        functools.partial(attend_kernel, heads, rows, len(pieces)),
        out_shape=(
            pltpu.HBM((blocks, rows, heads * HD), BF),
            pltpu.HBM((blocks, 8, rows), F4),
            pltpu.VMEM((LANE, length), BF),
            pltpu.HBM((length, 3 * LANE), BF),
            pltpu.HBM((length, normed[0].shape[1]), BF),
        ),
        in_specs=in_smem(2) + in_vmem(2 * len(pieces)),
        out_specs=in_vmem(3) + [pl.BlockSpec(memory_space=pltpu.HBM)] * 2,
        scratch_shapes=[
            pltpu.VMEM((length, 3 * LANE), BF),
            pltpu.SemaphoreType.DMA((2 * len(pieces),)),
        ],
        compiler_params=pltpu.CompilerParams(vmem_limit_bytes=26 << 20),
        cost_estimate=takes(25),
        name="tree_attend",
    )(order, part, *[in_vmem_space(v) for v in qkv + normed])


def attend_back_kernel(heads, rows, order_ref, part_ref, *refs):
    all_ref, kt_ref, mix_ref, grad_ref, lse_ref, far_normed_ref, w_ref = refs[:7]
    norm_refs = refs[7:11]
    proj_ref, sum_ref, acc_q, acc_k, acc_v, acc_w, qkv_ref, normed_ref, sems = refs[11:]
    bring = pltpu.make_async_copy(all_ref, qkv_ref, sems.at[0])
    bring.start()
    bring_normed = pltpu.make_async_copy(far_normed_ref, normed_ref, sems.at[1])
    part = part_ref[0]
    width = heads * HD

    def q_rows(pos):
        return pl.ds(pl.multiple_of(pos * BLK + part * rows, rows), rows)

    def k_at(pos, count=1):
        return qkv_ref[block_rows(pos, count), LANE : 2 * LANE]

    def v_at(pos, count=1):
        return qkv_ref[block_rows(pos, count), 2 * LANE : 3 * LANE]

    key_at = lax.broadcasted_iota(jnp.int32, (BLK, rows), 0)
    causal = (lax.broadcasted_iota(jnp.int32, (BLK, rows), 1) + part * rows) >= key_at
    masks = head_masks((2 * rows, LANE), heads)
    row_head = lax.broadcasted_iota(jnp.int32, (LANE, 2 * rows), 0) // HD
    acc_k[...] = jnp.zeros_like(acc_k)
    acc_v[...] = jnp.zeros_like(acc_v)
    acc_q[...] = jnp.zeros_like(acc_q)
    pad = jnp.zeros((2 * rows, LANE - width), BF)
    bring.wait()
    bring_normed.start()

    def tile(first, second, shared, parts_a, parts_b, use_last=None):
        q = jnp.concatenate(
            [qkv_ref[q_rows(first), 0:LANE], qkv_ref[q_rows(second), 0:LANE]], 0
        ) * BF(0.125)
        grad = jnp.concatenate([jnp.concatenate([grad_ref[first], grad_ref[second]], 0), pad], 1)
        mix = jnp.concatenate([jnp.concatenate([mix_ref[first], mix_ref[second]], 0), pad], 1)
        qt, gt, mt = jnp.transpose(q), jnp.transpose(grad), jnp.transpose(mix)
        terms = gt.astype(F4) * mt.astype(F4)
        inner = [
            jnp.sum(terms[h * HD : (h + 1) * HD], 0, keepdims=True) for h in range(heads)
        ]
        lse = jnp.concatenate([lse_ref[first], lse_ref[second]], 1)
        qms = [jnp.where(masks[h], q, BF(0)) for h in range(heads)]
        gms = [jnp.where(masks[h], grad, BF(0)) for h in range(heads)]
        qts = [jnp.where(row_head == h, qt, BF(0)) for h in range(heads)]
        gts = [jnp.where(row_head == h, gt, BF(0)) for h in range(heads)]

        def pieces(keys, values, h, cut, diag, bias):
            e = jnp.exp(dot(keys, qts[h][:, cut]) - (lse[h : h + 1, cut] + bias))
            if diag:
                e = jnp.where(causal, e, 0.0)
            t = dot(values, gts[h][:, cut])
            return e.astype(BF), (e * (t - inner[h][:, cut])).astype(BF)

        def strip(pos, count, cut, diag, grad_q, bias=0.0):
            keys, values = k_at(pos, count), v_at(pos, count)
            es = []
            ds = []
            for h in range(heads):
                e, d = pieces(keys, values, h, cut, diag, bias)
                es.append(e)
                ds.append(d)
                head_keys = kt_ref[h * HD : (h + 1) * HD, block_rows(pos, count)]
                grad_q[h] = grad_q[h] + dot(head_keys, d)
            acc_v[block_rows(pos, count), :] += dot(
                jnp.concatenate(es, 1), jnp.concatenate([g[cut] for g in gms], 0)
            )
            acc_k[block_rows(pos, count), :] += dot(
                jnp.concatenate(ds, 1), jnp.concatenate([g[cut] for g in qms], 0)
            )
            return grad_q

        grad_q = [jnp.zeros((HD, 2 * rows), F4) for _ in range(heads)]
        for i, (pos, count) in enumerate(shared):
            bias = 0.0
            if use_last is not None and i == len(shared) - 1:
                bias = jnp.where(use_last, 0.0, jnp.inf)
            grad_q = strip(pos, count, slice(0, 2 * rows), False, grad_q, bias)
        halves = []
        for i, parts in enumerate((parts_a, parts_b)):
            half = [jnp.zeros((HD, rows), F4) for _ in range(heads)]
            for pos, diag in parts:
                half = strip(pos, 1, slice(i * rows, (i + 1) * rows), diag, half)
            halves.append(half)
        grad_q = jnp.concatenate(
            [g + jnp.concatenate([a, b], 1) for g, a, b in zip(grad_q, *halves)]
            + [jnp.zeros((LANE - width, 2 * rows), F4)],
            0,
        )
        grad_q = jnp.transpose((grad_q * 0.125).astype(BF))
        acc_q[q_rows(first), :] = grad_q[:rows]
        acc_q[q_rows(second), :] = grad_q[rows:]

    each_tile(order_ref, tile)

    half = w_ref.shape[1] // 2
    size = acc_q.shape[0] // PIECES
    acc_w[...] = jnp.zeros_like(acc_w)
    sum_ref[...] = jnp.zeros_like(sum_ref)
    bring_normed.wait()

    def pair(i, carry):
        spot = pl.ds(pl.multiple_of(i * size, size), size)
        for odd in range(2):
            at = pl.ds(pl.multiple_of((2 * i + odd) * size, size), size)
            grads = jnp.concatenate(
                [acc_q[at, :], acc_k[at, :].astype(BF), acc_v[at, :].astype(BF)], 1
            )
            for side in range(2):
                low = dot(grads, w_ref[:, side * half : (side + 1) * half]).astype(BF)
                norm_refs[2 * side + odd][spot, :] = low
            acc_w[...] += dot(grads, normed_ref[at, :], TN)
            sum_ref[0:1, :] += jnp.sum(grads.astype(F4), 0, keepdims=True)
        return carry

    lax.fori_loop(0, PIECES // 2, pair, 0)
    proj_ref[...] = acc_w[...].astype(BF)


def attend_back(qkv, keys, mix, grad, lse, normed, weight, order, part, heads, rows):
    length, depth = normed.shape
    half = jax.ShapeDtypeStruct((length // 2, depth // 2), BF)
    far = pl.BlockSpec(memory_space=pltpu.HBM)
    return pl.pallas_call(
        functools.partial(attend_back_kernel, heads, rows),
        out_shape=(
            half,
            half,
            half,
            half,
            jax.ShapeDtypeStruct((3 * LANE, depth), BF),
            jax.ShapeDtypeStruct((8, 3 * LANE), F4),
        ),
        in_specs=in_smem(2) + [far] + in_vmem(4) + [far] + in_vmem(1),
        out_specs=in_vmem(6),
        scratch_shapes=[
            pltpu.VMEM((length, LANE), BF),
            pltpu.VMEM((length, LANE), F4),
            pltpu.VMEM((length, LANE), F4),
            pltpu.VMEM((3 * LANE, depth), F4),
            pltpu.VMEM((length, 3 * LANE), BF),
            pltpu.VMEM((length, depth), BF),
            pltpu.SemaphoreType.DMA((2,)),
        ],
        compiler_params=pltpu.CompilerParams(vmem_limit_bytes=46 << 20),
        cost_estimate=LIGHT,
        name="tree_attend_back",
    )(order, part, qkv, in_vmem_space(keys), mix, grad, lse, normed, weight)


def project_kernel(count, turned, place_ref, *refs):
    x_refs = refs[:count]
    pass_ref, gain_ref, shift_ref, w_ref, b_ref, normed_ref, qkv_ref = refs[count : count + 7]
    if not turned:
        rows_ref, w_ref = w_ref, refs[-1]

        @pl.when(pl.program_id(0) == 0)
        def _():
            w_ref[...] = jnp.transpose(rows_ref[...])

    x = x_refs[0][...]
    for i in range(1, count):
        x = jnp.where(pl.program_id(0) == i, x_refs[i][...], x)
    normal, _ = norm_stats(x.astype(F4) + pass_ref[...])
    normed = (normal * gain_ref[...] + shift_ref[...]).astype(BF)
    normed_ref[...] = normed
    qkv_ref[...] = (dot(normed, w_ref[...]) + b_ref[...]).astype(BF)


def project(pieces, place, weight, pass_embed, gain, shift, bias, turned=True):
    depth = pass_embed.shape[0]
    width = bias.shape[0]
    count = len(pieces)
    step = pieces[0].shape[0] if count > 1 else min(512, pieces[0].shape[0])
    if count > 1:
        specs = [whole_spec((step, depth))] * count
    else:
        specs = [pl.BlockSpec((step, depth), lambda i, place: (place[i], 0))]
    length = step * place.shape[0]
    vec = vec_spec(depth)
    shapes = [pltpu.VMEM((length, depth), BF), pltpu.VMEM((length, width), BF)]
    outs = [own_rows_spec(depth, step), own_rows_spec(width, step)]
    if not turned:
        shapes.append(pltpu.VMEM((depth, width), BF))
        outs.append(whole_spec((depth, width)))
    return pl.pallas_call(
        functools.partial(project_kernel, count, turned),
        out_shape=shapes,
        grid_spec=grid_of(
            length // step,
            specs + [vec, vec, vec, whole_spec(weight.shape), vec_spec(width)],
            outs,
        ),
        compiler_params=pltpu.CompilerParams(vmem_limit_bytes=20 << 20),
        cost_estimate=takes(5),
        name="norm_project",
    )(place, *pieces, pass_embed[None], gain[None], shift[None], weight, bias[None])


def vec_spec(depth):
    return pl.BlockSpec((1, depth), lambda i, at: (0, 0))


def own_rows_spec(depth, step, fixed=False):
    if fixed:
        return pl.BlockSpec((step, depth), lambda i, at: (at[0] + i, 0))
    return pl.BlockSpec((step, depth), lambda i, at: (i, 0))


def pieces_spec(count, step, width):
    return pl.BlockSpec((count, step, width), lambda i, at: (0, i, 0))


def whole_spec(shape):
    return pl.BlockSpec(shape, lambda i, at: (0,) * len(shape))


def grid_of(steps, ins, outs, scratch=()):
    return pltpu.PrefetchScalarGridSpec(
        num_scalar_prefetch=1,
        grid=(steps,),
        in_specs=ins,
        out_specs=outs,
        scratch_shapes=list(scratch),
    )


def own_forward_kernel(
    count, at_ref, x_ref, pass_ref, mix_ref, w_ref, b_ref, gain_ref, shift_ref, mid_ref, lift_ref
):
    middle = x_ref[...].astype(F4) + pass_ref[...] + b_ref[...]
    for r in range(count):
        middle = middle + dot(mix_ref[r], w_ref[r])
    mid_ref[...] = middle
    normal, _ = norm_stats(middle)
    lift_ref[...] = (normal * gain_ref[...] + shift_ref[...]).astype(BF)


def own_forward(x, at, pass_embed, mixed, weight, bias, gain, shift):
    count, sub, width = mixed.shape
    depth = x.shape[1]
    step = min(512, sub)
    vec = vec_spec(depth)
    return pl.pallas_call(
        functools.partial(own_forward_kernel, count),
        out_shape=(
            pltpu.HBM((sub, depth), F4),
            jax.ShapeDtypeStruct((sub, depth), BF),
        ),
        grid_spec=grid_of(
            sub // step,
            [
                own_rows_spec(depth, step, True),
                vec,
                pieces_spec(count, step, width),
                whole_spec(weight.shape),
                vec,
                vec,
                vec,
            ],
            (own_rows_spec(depth, step), own_rows_spec(depth, step)),
        ),
        cost_estimate=takes(3),
        compiler_params=pltpu.CompilerParams(vmem_limit_bytes=14 << 20),
        name="own_forward",
    )(at * (sub // step), x, pass_embed[None], mixed, weight, bias[None], gain[None], shift[None])


def own_backward_kernel(count, parts, at_ref, *refs):
    grad_parts = refs[:parts]
    mid_ref, dy_ref, gain_ref, w_ref, mix_ref, gm_ref, gmix_ref, gw_ref, sums_ref, acc = refs[parts:]
    step = pl.program_id(0)

    @pl.when(step == 0)
    def _():
        acc[...] = jnp.zeros_like(acc)
        sums_ref[...] = jnp.zeros_like(sums_ref)

    grad_lift = functools.reduce(jnp.add, [g[...].astype(F4) for g in grad_parts])
    normal, inv = norm_stats(mid_ref[...])
    dy = dy_ref[...].astype(F4)
    grad_middle = dy + norm_back(grad_lift, normal, inv, gain_ref[...])
    gm_ref[...] = grad_middle
    low = grad_middle.astype(BF)
    for r in range(count):
        gmix_ref[r] = dot(low, w_ref[r], NT).astype(BF)
        acc[r] += dot(mix_ref[r], low, TN)
    for i, values in enumerate((grad_middle, grad_lift * normal, grad_lift, dy)):
        sums_ref[i : i + 1, :] += jnp.sum(values, 0, keepdims=True)

    @pl.when(step == pl.num_programs(0) - 1)
    def _():
        gw_ref[...] = acc[...].astype(BF)


def own_backward(grad_parts, middle, dy, at, gain, weight, mixed):
    count, sub, width = mixed.shape
    depth = dy.shape[1]
    step = min(512, sub)
    rows = own_rows_spec(depth, step)
    return pl.pallas_call(
        functools.partial(own_backward_kernel, count, len(grad_parts)),
        out_shape=(
            pltpu.HBM((sub, depth), F4),
            jax.ShapeDtypeStruct((count, sub, width), BF),
            jax.ShapeDtypeStruct((count, width, depth), BF),
            jax.ShapeDtypeStruct((8, depth), F4),
        ),
        grid_spec=grid_of(
            sub // step,
            [rows] * len(grad_parts)
            + [
                rows,
                own_rows_spec(depth, step, True),
                vec_spec(depth),
                whole_spec(weight.shape),
                pieces_spec(count, step, width),
            ],
            (
                rows,
                pieces_spec(count, step, width),
                whole_spec((count, width, depth)),
                whole_spec((8, depth)),
            ),
            [pltpu.VMEM((count, width, depth), F4)],
        ),
        cost_estimate=takes(6),
        compiler_params=pltpu.CompilerParams(vmem_limit_bytes=18 << 20),
        name="own_backward",
    )(at * (sub // step), *grad_parts, in_hbm(middle), dy, gain[None], weight, mixed)


def last_norm_kernel(counts, at_ref, *refs):
    split = counts[0]
    left, right = refs[:split], refs[split : split + counts[1]]
    x_ref, pass_ref, gain_ref, gm_ref, out_ref, sums_ref = refs[split + counts[1] :]

    @pl.when(pl.program_id(0) == 0)
    def _():
        sums_ref[...] = jnp.zeros_like(sums_ref)

    grad_norm = jnp.concatenate(
        [functools.reduce(jnp.add, [g[...].astype(F4) for g in side]) for side in (left, right)], 1
    )
    normal, inv = norm_stats(x_ref[...].astype(F4) + pass_ref[...])
    grad_resid = gm_ref[...] + norm_back(grad_norm, normal, inv, gain_ref[...])
    out_ref[...] = grad_resid.astype(BF)
    for i, values in enumerate((grad_resid, grad_norm * normal, grad_norm)):
        sums_ref[i : i + 1, :] += jnp.sum(values, 0, keepdims=True)


def last_norm(left, right, x, at, pass_embed, gain, grad_middle):
    sub, depth = grad_middle.shape
    step = min(512, sub)
    return pl.pallas_call(
        functools.partial(last_norm_kernel, (len(left), len(right))),
        out_shape=(
            jax.ShapeDtypeStruct((sub, depth), BF),
            jax.ShapeDtypeStruct((8, depth), F4),
        ),
        grid_spec=grid_of(
            sub // step,
            [own_rows_spec(depth // 2, step)] * (len(left) + len(right))
            + [
                own_rows_spec(depth, step, True),
                vec_spec(depth),
                vec_spec(depth),
                own_rows_spec(depth, step),
            ],
            (own_rows_spec(depth, step), whole_spec((8, depth))),
        ),
        compiler_params=pltpu.CompilerParams(vmem_limit_bytes=14 << 20),
        name="last_norm",
    )(at * (sub // step), *left, *right, x, pass_embed[None], gain[None], in_hbm(grad_middle))


def units_kernel(count, place_ref, *refs):
    lift_refs = refs[:count]
    dy_ref, up_ref, bias_ref, down_ref, active_ref, pre_ref = refs[count : count + 6]
    outs = refs[count + 6 :]
    step = pl.program_id(0)
    lifted = lift_refs[0][...]
    for i in range(1, count):
        lifted = jnp.where(step == i, lift_refs[i][...], lifted)
    pre_act = dot(lifted, up_ref[...]) + bias_ref[...]
    value, slope = gelu_parts(pre_act)
    active = value.astype(BF)
    active_ref[...] = active
    size = lifted.shape[0]
    dy = dy_ref[pl.ds(pl.multiple_of(place_ref[step] * size, size), size), :]
    grad_pre = (dot(dy, down_ref[...], NT) * slope).astype(BF)
    pre_ref[...] = grad_pre
    grad_lift = dot(grad_pre, up_ref[...], NT).astype(BF)
    out = dot(active, down_ref[...]).astype(BF)
    for i in range(count):

        @pl.when(step == i)
        def _():
            outs[i][...] = grad_lift
            outs[count + i][...] = out


def units(lifted, dy, place, w_up, b_up, w_down):
    step, depth = lifted[0].shape
    count = len(lifted)
    wide = w_up.shape[1]
    piece = whole_spec((step, depth))
    specs = [piece] * count
    specs += [pl.BlockSpec(memory_space=pltpu.VMEM)] * 4
    made = pl.pallas_call(
        functools.partial(units_kernel, count),
        out_shape=(pltpu.VMEM((count * step, wide), BF),) * 2
        + (jax.ShapeDtypeStruct((step, depth), BF),) * (2 * count),
        grid_spec=grid_of(
            count, specs, (own_rows_spec(wide, step),) * 2 + (piece,) * (2 * count)
        ),
        compiler_params=pltpu.CompilerParams(vmem_limit_bytes=22 << 20),
        cost_estimate=takes(10),
        name="units",
    )(place, *lifted, dy, w_up, b_up[None], w_down)
    return made[:2], made[2 : 2 + count], made[2 + count :]


def unit_grads_kernel(groups, place_ref, dy_ref, *refs):
    out_ref, sum_ref, acc = refs[-3:]
    acc[...] = jnp.zeros_like(acc)
    sum_ref[...] = jnp.zeros_like(sum_ref)
    refs = list(refs[:-3])
    piece = 0
    for count in groups:
        lift_refs = refs[:count]
        active_ref, pre_ref = refs[count : count + 2]
        refs = refs[count + 2 :]
        size = lift_refs[0].shape[0]
        part = min(BLK, size)
        for i in range(count):

            def rows(j, carry):
                near = pl.ds(pl.multiple_of(j * part, part), part)
                here = pl.ds(pl.multiple_of(i * size + j * part, part), part)
                there = pl.ds(pl.multiple_of(place_ref[piece] * size + j * part, part), part)
                pre = pre_ref[here, :]
                acc[0] += dot(lift_refs[i][near, :], pre, TN)
                acc[1] += dot(active_ref[here, :], dy_ref[there, :], TN)
                sum_ref[0:1, :] += jnp.sum(pre.astype(F4), 0, keepdims=True)
                return carry

            lax.fori_loop(0, size // part, rows, 0)
            piece += 1
    out_ref[...] = acc[...].astype(BF)


def unit_grads(groups, dy, place):
    depth = dy.shape[1]
    wide = groups[0][1][0].shape[1]
    operands = []
    for lifted, made in groups:
        operands += [in_vmem_space(v) for v in (*lifted, *made)]
    return pl.pallas_call(
        functools.partial(unit_grads_kernel, [len(g[0]) for g in groups]),
        out_shape=(
            pltpu.HBM((2, depth, wide), BF),
            jax.ShapeDtypeStruct((8, wide), F4),
        ),
        in_specs=in_smem(1) + in_vmem(1 + len(operands)),
        out_specs=in_vmem(2),
        scratch_shapes=[pltpu.VMEM((2, depth, wide), F4)],
        compiler_params=pltpu.CompilerParams(vmem_limit_bytes=18 << 20),
        cost_estimate=takes(8),
        name="unit_grads",
    )(place, dy, *operands)


def send(values, axis, partner):
    size = lax.axis_size(axis)
    return lax.ppermute(values, axis, [(i, partner(i)) for i in range(size)])


def hop(values, step):
    return send(values, "tensor", lambda i: i ^ step)


def cross(values):
    return send(values, "seq", lambda i: i ^ 1)


def both(values, step_seq, step_tensor):
    return send(
        values, ("seq", "tensor"), lambda i: (i // 4 ^ step_seq) * 4 + (i % 4 ^ step_tensor)
    )


def add_low(left, right):
    return (left.astype(F4) + right.astype(F4)).astype(BF)


def add_all(arrays):
    return functools.reduce(jnp.add, [a.astype(F4) for a in arrays])


def tie(*values):
    return lax.optimization_barrier(values)


def slot(values, index, size, axis=0):
    return lax.dynamic_slice_in_dim(values, index * size, size, axis)


class Paired:
    def __init__(self, block_len):
        self.me = lax.axis_index("seq")
        self.rank = lax.axis_index("tensor")
        self.sub = block_len // 4
        self.per = self.sub // BLK

    def position(self, natural, blocks):
        half = blocks // 2
        s, b = natural // half, natural % half
        return half * (s ^ self.me) + self.per * ((b // self.per) ^ self.rank) + b % self.per

    def place(self):
        return jnp.stack([self.rank ^ r for r in range(4)]).astype(jnp.int32)

    def far(self, values, first):
        mine = tie(cross(slot(values, self.rank, self.sub)), first)[0]
        other = hop(mine, 2)
        return mine, hop(mine, 1), other

    def gather_weight(self, own):
        return jnp.stack([own, hop(own, 1), hop(own, 2), hop(own, 3)])

    def collect(self, piece, after=None):
        away = add_low(piece[2], hop(piece[3], 1))
        terms = [piece[0], hop(piece[1], 1), hop(away, 2)]
        return terms if after is None else (terms, *tie(*after, away)[:-1])

    def halved(self, values, axis, bit):
        half = values.shape[0] // 2
        at = lax.axis_index(axis) >> bit & 1
        away = send(slot(values, 1 - at, half), axis, lambda i: i ^ (1 << bit))
        return slot(values, at, half), away

    def doubled(self, values, axis, bit, beside):
        at = lax.axis_index(axis) >> bit & 1
        other, beside = tie(send(values, axis, lambda i: i ^ (1 << bit)), beside)
        both = [jnp.where(at == 0, values, other), jnp.where(at == 0, other, values)]
        return jnp.concatenate(both, 0), beside

    def last_sums(self, parts, values, early):
        near_one, near_two = hop(parts[1], 1), hop(parts[3], 1)
        ones = [v.reshape(2, 2, self.sub, -1) for v in (parts[0], near_one)]
        away_one = add_all([v[1] for v in ones]).astype(BF)
        keep, early = tie(parts[2], early, away_one)[:2]
        twos = [v.reshape(2, 2, self.sub, -1) for v in (keep, near_two)]
        away_two = add_all([v[:, 1] for v in twos]).astype(BF)
        kept, away = self.halved(values, "dp", 0)
        got_one, got_two, away = tie(cross(away_one), hop(away_two, 2), away)
        away_one = add_all([v[0, 1] for v in ones] + [got_one[1]]).astype(BF)
        away_two = add_all([v[1, 0] for v in twos] + [got_two[1]]).astype(BF)
        kept, away = self.halved(add_low(kept, away), "seq", 0)
        end_one, end_two, away = tie(hop(away_one, 2), cross(away_two), away)
        values = add_low(kept, away)
        flat = [v.reshape(2 * self.sub, -1) for v in (got_one, got_two)]
        left = [parts[0], near_one, flat[0], end_one]
        right = [keep, near_two, flat[1], end_two]
        return left, right, values, early

    def sum_small(self, shared, ranked, values, beside):
        kept, away = self.halved(values, "dp", 1)
        shared, away, *beside = tie(shared, away, *beside)
        values, got = self.doubled(add_low(kept, away), "dp", 1, hop(shared, 1))
        shared = shared + got
        values, got = self.doubled(values, "seq", 0, hop(shared, 2))
        small = jnp.concatenate([shared + got, ranked], 0)
        small = small + cross(small)
        small = small + send(small, "dp", lambda i: i ^ 1)
        small = small + send(small, "dp", lambda i: i ^ 2)
        values, small = self.doubled(values, "dp", 0, small)
        return small, values, *beside

    def to_tokens(self, mixture):
        blocks, rows, width = mixture.shape
        piece = mixture.reshape(2, 4, self.per, rows, width)
        columns = []
        for r in range(4):
            here = piece[0, r] if r == 0 else both(piece[0, r], 0, r)
            there = both(piece[1, r], 1, r)
            first = jnp.where(self.me == 0, here, there)
            second = jnp.where(self.me == 0, there, here)
            columns.append(jnp.stack([first, second], 1).reshape(self.sub, width))
        return jnp.stack(columns)

    def to_heads(self, grads, rows):
        parts = grads.reshape(4, self.per, 2, rows, grads.shape[2])
        mine = jnp.where(self.me == 0, parts[:, :, 0], parts[:, :, 1])
        theirs = jnp.where(self.me == 0, parts[:, :, 1], parts[:, :, 0])
        here = [mine[r] if r == 0 else both(mine[r], 0, r) for r in range(4)]
        there = [both(theirs[r], 1, r) for r in range(4)]
        return jnp.concatenate(here + there, 0)


class Plain:
    def __init__(self, block_len):
        self.me = lax.axis_index("seq")
        self.rank = lax.axis_index("tensor")
        self.seq = lax.axis_size("seq")
        self.tensor = lax.axis_size("tensor")
        self.block_len = block_len
        self.sub = block_len // self.tensor

    def position(self, natural, blocks):
        return natural

    def gather_weight(self, own):
        return lax.all_gather(own, "tensor", axis=0)

    def collect(self, piece, after=None):
        whole = jnp.concatenate(piece, 0)
        terms = [lax.psum_scatter(whole, "tensor", scatter_dimension=0, tiled=True)]
        return terms if after is None else (terms, *after)

    def last_sums(self, parts, values, early):
        sides = []
        for keep, away in (parts[:2], parts[2:]):
            half = keep.shape[1]
            keep, away = [v.reshape(PIECES // 2, -1, half) for v in (keep, away)]
            whole = jnp.stack([keep, away], 1).reshape(-1, half)
            sides.append(
                [lax.psum_scatter(whole, ("seq", "tensor"), scatter_dimension=0, tiled=True)]
            )
        return *sides, lax.psum(values, ("dp", "seq")), early

    def sum_small(self, shared, ranked, values, beside):
        shared = lax.psum(shared, ("dp", "seq", "tensor"))
        return jnp.concatenate([shared, lax.psum(ranked, ("dp", "seq"))], 0), values, *beside

    def to_tokens(self, mixture):
        blocks, rows, width = mixture.shape
        full = lax.all_gather(mixture, ("seq", "tensor"), axis=0)
        full = full.reshape(self.seq, self.tensor, blocks, rows, width)
        full = full.transpose(1, 2, 0, 3, 4).reshape(self.tensor, -1, width)
        return slot(full, self.me * self.tensor + self.rank, self.sub, 1)

    def to_heads(self, grads, rows):
        full = lax.all_gather(grads, ("seq", "tensor"), axis=1, tiled=True)
        full = full.reshape(self.tensor, -1, self.seq, rows, grads.shape[2])
        return slot(slot(full, self.me, 1, 2)[:, :, 0], self.rank, 1)[0]


def tree_order(seg_row, parent_row, position):
    blocks = seg_row.shape[0] // BLK
    segs = parent_row.shape[0]
    slot_seg = seg_row[::BLK]
    labels = jnp.arange(segs, dtype=jnp.int32)
    above = jnp.sum(jnp.where(slot_seg[:, None] == labels[None, :], parent_row[None, :], 0), 1)
    natural = jnp.arange(blocks, dtype=jnp.int32)
    key = jnp.where(
        slot_seg == 0,
        natural,
        jnp.where(above == 0, 100 + slot_seg, 1000 + 16 * above + slot_seg),
    )
    rank = jnp.sum((key[None, :] < key[:, None]).astype(jnp.int32), 1)
    where = position(natural, blocks)
    order = jnp.sum(jnp.where(rank[:, None] == natural[None, :], where[:, None], 0), 0)
    base = order[0] // TRUNK_BLOCKS * TRUNK_BLOCKS
    return jnp.concatenate([order, base[None]]).astype(jnp.int32)


def padded(values, axis):
    widths = [(0, 0)] * values.ndim
    widths[axis] = (0, LANE - values.shape[axis])
    return jnp.pad(values, widths)


def total(values):
    return jnp.sum(values, axis=0)


def local(
    inputs,
    pass_embed,
    norm1_gain,
    norm1_shift,
    w_qkv,
    b_qv,
    w_out,
    b_out,
    norm2_gain,
    norm2_shift,
    w_up,
    b_up,
    w_down,
    b_down,
    out_grad,
    seg_id,
    parent,
):
    x = inputs[0]
    dy_block = out_grad[0]
    block_len, depth = x.shape
    length = seg_id.shape[1]
    seq, tensor = lax.axis_size("seq"), lax.axis_size("tensor")
    width = w_qkv.shape[2]
    heads = width // HD
    rows = BLK // seq
    paired = (seq, tensor, lax.axis_size("dp")) == (2, 4, 4) and block_len % (4 * BLK) == 0
    move = Paired(block_len) if paired else Plain(block_len)

    order = tree_order(seg_id[0], parent[0], move.position)
    part = move.me[None].astype(jnp.int32)

    w_rows = padded(jnp.swapaxes(w_qkv, 1, 2), 1).reshape(3 * LANE, depth)
    zero = jnp.zeros((LANE,), F4)
    b_cols = jnp.concatenate([padded(b_qv[0], 0), zero, padded(b_qv[1], 0)])
    norm_args = (pass_embed, norm1_gain, norm1_shift, b_cols)
    if paired:
        *near, w_cols = project([x], move.place(), w_rows, *norm_args, turned=False)
        mine, core, other = move.far(x, near[0])
        pair = jnp.arange(2, dtype=jnp.int32)
        pieces = [near, project([mine, core], pair, w_cols, *norm_args)]
        other = tie(other, pieces[1][0])[0]
        pieces.append(project([other, hop(other, 1)], pair, w_cols, *norm_args))
    else:
        full = lax.all_gather(x, "seq", axis=0, tiled=True)
        place = jnp.arange(pl.cdiv(length, 512), dtype=jnp.int32)
        pieces = [project([full], place, w_rows, *norm_args, turned=False)[:2]]

    mixture, lse, keys, qkv, normed = attend(pieces, order, part, heads, rows)

    at = move.rank[None].astype(jnp.int32)
    out_weight = move.gather_weight(w_out)
    mixed = move.to_tokens(mixture)
    middle, lifted_own = own_forward(
        x, at, pass_embed, mixed, out_weight, b_out, norm2_gain, norm2_shift
    )

    unit_args = (in_vmem_space(w_up), b_up, in_vmem_space(w_down))
    dy_near = in_vmem_space(dy_block)
    if paired:
        core, other = hop(lifted_own, 1), hop(lifted_own, 2)
        near = [lifted_own, core]
        place = move.place()
        near_kept, near_lift, near_out = units(near, dy_near, place[:2], *unit_args)
        other = tie(other, near_lift[1])[0]
        far = [hop(other, 1), other]
        far_place = place[:1:-1]
        far_kept, far_lift, far_out = units(far, dy_near, far_place, *unit_args)
        lift_made = [*near_lift, *far_lift[::-1]]
        out_made = [*near_out, *far_out[::-1]]
        place = jnp.concatenate([place[:2], far_place])
        groups = [(near, near_kept), (far, far_kept)]
    else:
        near = [lax.all_gather(lifted_own, "tensor", axis=0, tiled=True)]
        place = jnp.zeros((1,), jnp.int32)
        near_kept, lift_made, out_made = units(near, dy_near, place, *unit_args)
        groups = [(near, near_kept)]
    grad_lift, place = move.collect(lift_made, [place])
    grad_units, up_sums = unit_grads(groups, dy_near, place)
    units_sum = lax.psum(grad_units, ("dp", "seq"))

    grad_middle, grad_mix, grad_w_out, early = own_backward(
        grad_lift, middle, dy_block, at, norm2_gain, out_weight, mixed
    )
    out_made, grad_mix = tie(out_made, grad_mix)
    grad_mix = move.to_heads(grad_mix, rows)
    out_terms = move.collect(out_made)
    grad_w_out = move.collect(list(grad_w_out))
    made = attend_back(
        qkv, keys, mixture, grad_mix, lse, normed, w_rows, order, part, heads, rows
    )
    *norm_parts, grad_w_rows, col_sums = made
    count = len(out_terms)
    *norm_parts, grad_w_rows = tie(*norm_parts, grad_w_rows, *out_terms, *grad_w_out)
    norm_parts, grad_w_rows, terms = norm_parts[:4], norm_parts[4], [*norm_parts[5:], grad_w_rows]
    out_terms, grad_w_out = terms[:count], terms[count:]
    rest = add_all(grad_w_out).astype(BF).reshape(3, LANE - width, depth)
    rest = jnp.pad(rest, ((0, 0), (width, 0), (0, 0))).reshape(3 * LANE, depth)
    grad_w_rows = grad_w_rows + rest
    left, right, grad_w_rows, units_sum = move.last_sums(norm_parts, grad_w_rows, units_sum)
    input_grad, late = last_norm(left, right, x, at, pass_embed, norm1_gain, grad_middle)
    sums, grad_w_rows, *out_terms = move.sum_small(
        jnp.concatenate([late[:3], early[:4]], 0),
        jnp.concatenate([up_sums[:1], col_sums[:1]], 0),
        grad_w_rows,
        out_terms,
    )
    output = add_all([*out_terms, middle, b_down]).astype(BF)
    grad_units = units_sum.astype(F4)
    grad_w_rows = grad_w_rows.astype(F4).reshape(3, LANE, depth)
    grad_w_qkv = jnp.swapaxes(grad_w_rows[:, :width], 1, 2)
    grad_w_out = grad_w_rows[:, width:].reshape(width, depth)
    grad_b_qv = jnp.stack([sums[8, :width], sums[8, 2 * LANE : 2 * LANE + width]])
    return (
        output[None],
        input_grad[None],
        sums[0],
        sums[1],
        sums[2],
        grad_w_qkv,
        grad_b_qv,
        grad_w_out,
        sums[3],
        sums[4],
        sums[5],
        grad_units[0],
        sums[7],
        grad_units[1],
        sums[6],
    )


def solution(mesh):
    return jax.shard_map(
        local,
        mesh=mesh,
        in_specs=(
            P("dp", "seq", None),
            P(),
            P(),
            P(),
            P(None, None, "tensor"),
            P(None, "tensor"),
            P("tensor", None),
            P(),
            P(),
            P(),
            P(None, "tensor"),
            P("tensor"),
            P("tensor", None),
            P(),
            P("dp", "seq", None),
            P("dp", None),
            P("dp", None),
        ),
        out_specs=(
            P("dp", ("seq", "tensor"), None),
            P("dp", ("seq", "tensor"), None),
            P(),
            P(),
            P(),
            P(None, None, "tensor"),
            P(None, "tensor"),
            P("tensor", None),
            P(),
            P(),
            P(),
            P(None, "tensor"),
            P("tensor"),
            P("tensor", None),
            P(),
        ),
        check_vma=False,
    )
```

```python
import functools

import jax
import jax.numpy as jnp
from jax import lax
from jax.experimental import pallas as pl
from jax.experimental.pallas import tpu as pltpu
from jax.sharding import PartitionSpec as P

HD = 64
BLK = 256
TRUNK_BLOCKS = 4
LANE = 256
PIECES = 8
EPS = 1e-05
ROOT = 0.7978845608028654
BF = jnp.bfloat16
F4 = jnp.float32
NT = (((1,), (1,)), ((), ()))
NN = (((1,), (0,)), ((), ()))
TN = (((0,), (0,)), ((), ()))
LIGHT = pl.CostEstimate(flops=1000, bytes_accessed=1000, transcendentals=0)


def takes(us):
    return pl.CostEstimate(flops=int(us * 1.1e9), bytes_accessed=1000, transcendentals=0)


def in_hbm(values):
    return pltpu.with_memory_space_constraint(values, pltpu.HBM)


def in_vmem_space(values):
    return pltpu.with_memory_space_constraint(values, pltpu.VMEM)


def dot(left, right, dims=NN):
    return lax.dot_general(left, right, dims, preferred_element_type=F4)


def norm_stats(values):
    row_mean = jnp.mean(values, -1, keepdims=True)
    centred = values - row_mean
    inv_std = lax.rsqrt(jnp.mean(centred * centred, -1, keepdims=True) + EPS)
    return (centred * inv_std, inv_std)


def norm_back(grad_out, normal, inv_std, gain_vec):
    scaled = grad_out * gain_vec
    return inv_std * (
        scaled
        - jnp.mean(scaled, -1, keepdims=True)
        - normal * jnp.mean(scaled * normal, -1, keepdims=True)
    )


def gelu_parts(pre_act):
    cubic_term = 0.044715 * pre_act * pre_act * pre_act
    tangent = jnp.tanh(ROOT * (pre_act + cubic_term))
    gelu_value = 0.5 * pre_act * (1.0 + tangent)
    gelu_slope = 0.5 * (1.0 + tangent) + 0.5 * pre_act * (1.0 - tangent * tangent) * ROOT * (
        1.0 + 3.0 * 0.044715 * pre_act * pre_act
    )
    return (gelu_value, gelu_slope)


def block_rows(pos, count=1):
    return pl.ds(pl.multiple_of(pos * BLK, BLK), count * BLK)


def head_masks(shape, heads):
    lane = lax.broadcasted_iota(jnp.int32, shape, 1) // HD
    return [lane == h for h in range(heads)]


def each_tile(order_ref, tile):
    trunk = [order_ref[i] for i in range(TRUNK_BLOCKS)]
    base = order_ref[16]
    tile(trunk[0], trunk[1], [], [(trunk[0], True)], [(trunk[0], False), (trunk[1], True)])
    tile(
        trunk[2],
        trunk[3],
        [(trunk[0], 2)],
        [(trunk[2], True)],
        [(trunk[2], False), (trunk[3], True)],
    )

    def deep(i, carry):
        one, two = order_ref[4 + 2 * i], order_ref[5 + 2 * i]
        above = order_ref[jnp.maximum(2 + i, 4)]
        tile(one, two, [(base, 4), (above, 1)], [(one, True)], [(two, True)], i >= 2)
        return carry

    lax.fori_loop(0, 6, deep, 0)


def lanes_of(arrays):
    return [a[:, i : i + 128] for a in arrays for i in range(0, a.shape[1], 128)]


def attend_kernel(heads, rows, count, order_ref, part_ref, *refs):
    out_ref, lse_ref, kt_ref, all_ref, normed_ref = refs[2 * count : 2 * count + 5]
    piece_refs = refs[2 * count + 5 : -2]
    qkv_ref, sems = refs[-2:]
    part = part_ref[0]
    length = qkv_ref.shape[0]
    start = 0
    copies = []
    for piece, normed in zip(refs[:count], refs[count : 2 * count]):
        at = pl.ds(start, piece.shape[0])
        for one, whole in ((piece, all_ref), (normed, normed_ref)):
            copies.append(pltpu.make_async_copy(one, whole.at[at], sems.at[len(copies)]))
            copies[-1].start()
        qkv_ref[at] = piece[...]
        start += piece.shape[0]

    def turn(i, carry):
        at = pl.ds(pl.multiple_of(i * 512, 512), 512)
        kt_ref[:, at] = jnp.transpose(qkv_ref[at, LANE : 2 * LANE])
        return carry

    lax.fori_loop(0, length // 512, turn, 0)

    def q_at(pos):
        return qkv_ref[pl.ds(pl.multiple_of(pos * BLK + part * rows, rows), rows), 0:LANE]

    def k_at(pos, count=1):
        return kt_ref[:, block_rows(pos, count)]

    def v_at(pos, count=1):
        return qkv_ref[block_rows(pos, count), 2 * LANE : 3 * LANE]

    row_at = lax.broadcasted_iota(jnp.int32, (rows, BLK), 0) + part * rows
    causal = row_at >= lax.broadcasted_iota(jnp.int32, (rows, BLK), 1)
    masks = head_masks((2 * rows, LANE), heads)

    def tile(first, second, shared, parts_a, parts_b, use_last=None):
        q = jnp.concatenate([q_at(first), q_at(second)], 0) * BF(0.125)
        result = jnp.zeros((2 * rows, LANE), F4)
        log_cols = []
        for h in range(heads):
            qm = jnp.where(masks[h], q, BF(0))
            wide = [dot(qm, k_at(p, c)) for p, c in shared]
            if use_last is not None:
                wide[-1] = wide[-1] + jnp.where(use_last, 0.0, -jnp.inf)
            own = []
            for cut, parts in ((qm[:rows], parts_a), (qm[rows:], parts_b)):
                scores = [dot(cut, k_at(p)) for p, _ in parts]
                own.append(
                    [jnp.where(causal, s, -jnp.inf) if d else s for s, (_, d) in zip(scores, parts)]
                )
            top = jnp.concatenate([functools.reduce(jnp.maximum, lanes_of(o)) for o in own], 0)
            top = functools.reduce(jnp.maximum, lanes_of(wide), top)
            top = jnp.max(top, 1, keepdims=True)
            mix = []
            sums = []
            for i, parts in enumerate((parts_a, parts_b)):
                cut = top[i * rows : (i + 1) * rows]
                es = [jnp.exp(s - cut) for s in own[i]]
                sums.append(functools.reduce(jnp.add, lanes_of(es)))
                terms = [dot(e.astype(BF), v_at(p)) for e, (p, _) in zip(es, parts)]
                mix.append(functools.reduce(jnp.add, terms))
            mix = jnp.concatenate(mix, 0)
            total = jnp.concatenate(sums, 0)
            for s, (p, c) in zip(wide, shared):
                e = jnp.exp(s - top)
                total = functools.reduce(jnp.add, lanes_of([e]), total)
                mix = mix + dot(e.astype(BF), v_at(p, c))
            total = jnp.sum(total, 1, keepdims=True)
            result = jnp.where(masks[h], mix / total, result)
            log_cols.append(top + jnp.log(total))
        low = result.astype(BF)[:, : heads * HD]
        out_ref[first] = low[:rows]
        out_ref[second] = low[rows:]
        lane = lax.broadcasted_iota(jnp.int32, (2 * rows, 128), 1)
        cols = jnp.zeros((2 * rows, 128), F4)
        for h in range(heads):
            cols = jnp.where(lane == h, log_cols[h], cols)
        flat = jnp.transpose(cols)[:8]
        lse_ref[first] = flat[:, :rows]
        lse_ref[second] = flat[:, rows:]

    each_tile(order_ref, tile)
    size = out_ref.shape[0] // max(len(piece_refs), 1)
    for i, piece in enumerate(piece_refs):
        piece[...] = out_ref[i * size : (i + 1) * size]
    for copy in copies:
        copy.wait()


def in_vmem(count):
    return [pl.BlockSpec(memory_space=pltpu.VMEM)] * count


def in_smem(count):
    return [pl.BlockSpec(memory_space=pltpu.SMEM)] * count


def attend(pieces, order, part, heads, rows, cuts):
    normed, qkv = zip(*pieces)
    length = sum(q.shape[0] for q in qkv)
    blocks = length // BLK
    return pl.pallas_call(
        functools.partial(attend_kernel, heads, rows, len(pieces)),
        out_shape=(
            pltpu.HBM((blocks, rows, heads * HD), BF),
            pltpu.HBM((blocks, 8, rows), F4),
            pltpu.VMEM((LANE, length), BF),
            pltpu.HBM((length, 3 * LANE), BF),
            pltpu.HBM((length, normed[0].shape[1]), BF),
        )
        + (jax.ShapeDtypeStruct((blocks // max(cuts, 1), rows, heads * HD), BF),) * cuts,
        in_specs=in_smem(2) + in_vmem(2 * len(pieces)),
        out_specs=in_vmem(3) + [pl.BlockSpec(memory_space=pltpu.HBM)] * 2 + in_vmem(cuts),
        scratch_shapes=[
            pltpu.VMEM((length, 3 * LANE), BF),
            pltpu.SemaphoreType.DMA((2 * len(pieces),)),
        ],
        compiler_params=pltpu.CompilerParams(vmem_limit_bytes=26 << 20),
        cost_estimate=takes(25),
        name="tree_attend",
    )(order, part, *[in_vmem_space(v) for v in qkv + normed])


def attend_back_kernel(heads, rows, order_ref, part_ref, *refs):
    all_ref, kt_ref, mix_ref, grad_ref, lse_ref, far_normed_ref, w_ref = refs[:7]
    norm_refs = refs[7:11]
    proj_ref, sum_ref, acc_q, acc_k, acc_v, acc_w, qkv_ref, normed_ref, sems = refs[11:]
    bring = pltpu.make_async_copy(all_ref, qkv_ref, sems.at[0])
    bring.start()
    bring_normed = pltpu.make_async_copy(far_normed_ref, normed_ref, sems.at[1])
    part = part_ref[0]
    width = heads * HD

    def q_rows(pos):
        return pl.ds(pl.multiple_of(pos * BLK + part * rows, rows), rows)

    def k_at(pos, count=1):
        return qkv_ref[block_rows(pos, count), LANE : 2 * LANE]

    def v_at(pos, count=1):
        return qkv_ref[block_rows(pos, count), 2 * LANE : 3 * LANE]

    key_at = lax.broadcasted_iota(jnp.int32, (BLK, rows), 0)
    causal = (lax.broadcasted_iota(jnp.int32, (BLK, rows), 1) + part * rows) >= key_at
    masks = head_masks((2 * rows, LANE), heads)
    row_head = lax.broadcasted_iota(jnp.int32, (LANE, 2 * rows), 0) // HD
    acc_k[...] = jnp.zeros_like(acc_k)
    acc_v[...] = jnp.zeros_like(acc_v)
    acc_q[...] = jnp.zeros_like(acc_q)
    pad = jnp.zeros((2 * rows, LANE - width), BF)
    bring.wait()
    bring_normed.start()

    def tile(first, second, shared, parts_a, parts_b, use_last=None):
        q = jnp.concatenate(
            [qkv_ref[q_rows(first), 0:LANE], qkv_ref[q_rows(second), 0:LANE]], 0
        ) * BF(0.125)
        grad = jnp.concatenate([jnp.concatenate([grad_ref[first], grad_ref[second]], 0), pad], 1)
        mix = jnp.concatenate([jnp.concatenate([mix_ref[first], mix_ref[second]], 0), pad], 1)
        qt, gt, mt = jnp.transpose(q), jnp.transpose(grad), jnp.transpose(mix)
        terms = gt.astype(F4) * mt.astype(F4)
        inner = [
            jnp.sum(terms[h * HD : (h + 1) * HD], 0, keepdims=True) for h in range(heads)
        ]
        lse = jnp.concatenate([lse_ref[first], lse_ref[second]], 1)
        qms = [jnp.where(masks[h], q, BF(0)) for h in range(heads)]
        gms = [jnp.where(masks[h], grad, BF(0)) for h in range(heads)]
        qts = [jnp.where(row_head == h, qt, BF(0)) for h in range(heads)]
        gts = [jnp.where(row_head == h, gt, BF(0)) for h in range(heads)]

        def pieces(keys, values, h, cut, diag, bias):
            e = jnp.exp(dot(keys, qts[h][:, cut]) - (lse[h : h + 1, cut] + bias))
            if diag:
                e = jnp.where(causal, e, 0.0)
            t = dot(values, gts[h][:, cut])
            return e.astype(BF), (e * (t - inner[h][:, cut])).astype(BF)

        def strip(pos, count, cut, diag, grad_q, bias=0.0):
            keys, values = k_at(pos, count), v_at(pos, count)
            es = []
            ds = []
            for h in range(heads):
                e, d = pieces(keys, values, h, cut, diag, bias)
                es.append(e)
                ds.append(d)
                head_keys = kt_ref[h * HD : (h + 1) * HD, block_rows(pos, count)]
                grad_q[h] = grad_q[h] + dot(head_keys, d)
            acc_v[block_rows(pos, count), :] += dot(
                jnp.concatenate(es, 1), jnp.concatenate([g[cut] for g in gms], 0)
            )
            acc_k[block_rows(pos, count), :] += dot(
                jnp.concatenate(ds, 1), jnp.concatenate([g[cut] for g in qms], 0)
            )
            return grad_q

        grad_q = [jnp.zeros((HD, 2 * rows), F4) for _ in range(heads)]
        for i, (pos, count) in enumerate(shared):
            bias = 0.0
            if use_last is not None and i == len(shared) - 1:
                bias = jnp.where(use_last, 0.0, jnp.inf)
            grad_q = strip(pos, count, slice(0, 2 * rows), False, grad_q, bias)
        halves = []
        for i, parts in enumerate((parts_a, parts_b)):
            half = [jnp.zeros((HD, rows), F4) for _ in range(heads)]
            for pos, diag in parts:
                half = strip(pos, 1, slice(i * rows, (i + 1) * rows), diag, half)
            halves.append(half)
        grad_q = jnp.concatenate(
            [g + jnp.concatenate([a, b], 1) for g, a, b in zip(grad_q, *halves)]
            + [jnp.zeros((LANE - width, 2 * rows), F4)],
            0,
        )
        grad_q = jnp.transpose((grad_q * 0.125).astype(BF))
        acc_q[q_rows(first), :] = grad_q[:rows]
        acc_q[q_rows(second), :] = grad_q[rows:]

    each_tile(order_ref, tile)

    half = w_ref.shape[1] // 2
    size = acc_q.shape[0] // PIECES
    acc_w[...] = jnp.zeros_like(acc_w)
    sum_ref[...] = jnp.zeros_like(sum_ref)
    bring_normed.wait()

    def pair(i, carry):
        spot = pl.ds(pl.multiple_of(i * size, size), size)
        for odd in range(2):
            at = pl.ds(pl.multiple_of((2 * i + odd) * size, size), size)
            grads = jnp.concatenate(
                [acc_q[at, :], acc_k[at, :].astype(BF), acc_v[at, :].astype(BF)], 1
            )
            for side in range(2):
                low = dot(grads, w_ref[:, side * half : (side + 1) * half]).astype(BF)
                norm_refs[2 * side + odd][spot, :] = low
            acc_w[...] += dot(grads, normed_ref[at, :], TN)
            sum_ref[0:1, :] += jnp.sum(grads.astype(F4), 0, keepdims=True)
        return carry

    lax.fori_loop(0, PIECES // 2, pair, 0)
    proj_ref[...] = acc_w[...].astype(BF)


def attend_back(qkv, keys, mix, grad, lse, normed, weight, order, part, heads, rows):
    length, depth = normed.shape
    half = jax.ShapeDtypeStruct((length // 2, depth // 2), BF)
    far = pl.BlockSpec(memory_space=pltpu.HBM)
    return pl.pallas_call(
        functools.partial(attend_back_kernel, heads, rows),
        out_shape=(
            half,
            half,
            half,
            half,
            jax.ShapeDtypeStruct((3 * LANE, depth), BF),
            jax.ShapeDtypeStruct((8, 3 * LANE), F4),
        ),
        in_specs=in_smem(2) + [far] + in_vmem(4) + [far] + in_vmem(1),
        out_specs=in_vmem(6),
        scratch_shapes=[
            pltpu.VMEM((length, LANE), BF),
            pltpu.VMEM((length, LANE), F4),
            pltpu.VMEM((length, LANE), F4),
            pltpu.VMEM((3 * LANE, depth), F4),
            pltpu.VMEM((length, 3 * LANE), BF),
            pltpu.VMEM((length, depth), BF),
            pltpu.SemaphoreType.DMA((2,)),
        ],
        compiler_params=pltpu.CompilerParams(vmem_limit_bytes=46 << 20),
        cost_estimate=LIGHT,
        name="tree_attend_back",
    )(order, part, qkv, in_vmem_space(keys), mix, grad, lse, normed, weight)


def project_kernel(count, turned, place_ref, *refs):
    x_refs = refs[:count]
    pass_ref, gain_ref, shift_ref, w_ref, b_ref, normed_ref, qkv_ref = refs[count : count + 7]
    if not turned:
        rows_ref, w_ref = w_ref, refs[-1]

        @pl.when(pl.program_id(0) == 0)
        def _():
            w_ref[...] = jnp.transpose(rows_ref[...])

    x = x_refs[0][...]
    for i in range(1, count):
        x = jnp.where(pl.program_id(0) == i, x_refs[i][...], x)
    normal, _ = norm_stats(x.astype(F4) + pass_ref[...])
    normed = (normal * gain_ref[...] + shift_ref[...]).astype(BF)
    normed_ref[...] = normed
    qkv_ref[...] = (dot(normed, w_ref[...]) + b_ref[...]).astype(BF)


def project(pieces, place, weight, pass_embed, gain, shift, bias, turned=True):
    depth = pass_embed.shape[0]
    width = bias.shape[0]
    count = len(pieces)
    step = pieces[0].shape[0] if count > 1 else min(512, pieces[0].shape[0])
    if count > 1:
        specs = [whole_spec((step, depth))] * count
    else:
        specs = [pl.BlockSpec((step, depth), lambda i, place: (place[i], 0))]
    length = step * place.shape[0]
    vec = vec_spec(depth)
    shapes = [pltpu.VMEM((length, depth), BF), pltpu.VMEM((length, width), BF)]
    outs = [own_rows_spec(depth, step), own_rows_spec(width, step)]
    if not turned:
        shapes.append(pltpu.VMEM((depth, width), BF))
        outs.append(whole_spec((depth, width)))
    return pl.pallas_call(
        functools.partial(project_kernel, count, turned),
        out_shape=shapes,
        grid_spec=grid_of(
            length // step,
            specs + [vec, vec, vec, whole_spec(weight.shape), vec_spec(width)],
            outs,
        ),
        compiler_params=pltpu.CompilerParams(vmem_limit_bytes=20 << 20),
        cost_estimate=takes(5),
        name="norm_project",
    )(place, *pieces, pass_embed[None], gain[None], shift[None], weight, bias[None])


def vec_spec(depth):
    return pl.BlockSpec((1, depth), lambda i, at: (0, 0))


def own_rows_spec(depth, step, fixed=False):
    if fixed:
        return pl.BlockSpec((step, depth), lambda i, at: (at[0] + i, 0))
    return pl.BlockSpec((step, depth), lambda i, at: (i, 0))


def pieces_spec(count, step, width):
    return pl.BlockSpec((count, step, width), lambda i, at: (0, i, 0))


def whole_spec(shape):
    return pl.BlockSpec(shape, lambda i, at: (0,) * len(shape))


def grid_of(steps, ins, outs, scratch=()):
    return pltpu.PrefetchScalarGridSpec(
        num_scalar_prefetch=1,
        grid=(steps,),
        in_specs=ins,
        out_specs=outs,
        scratch_shapes=list(scratch),
    )


def own_forward_kernel(
    count, at_ref, x_ref, pass_ref, mix_ref, b_ref, gain_ref, shift_ref, *refs
):
    mid_ref, lift_ref = refs[count:]
    middle = x_ref[...].astype(F4) + pass_ref[...] + b_ref[...]
    for r in range(count):
        middle = middle + dot(mix_ref[r], refs[r][...])
    mid_ref[...] = middle
    normal, _ = norm_stats(middle)
    lift_ref[...] = (normal * gain_ref[...] + shift_ref[...]).astype(BF)


def own_forward(x, at, pass_embed, mixed, weight, bias, gain, shift):
    count, sub, width = mixed.shape
    depth = x.shape[1]
    step = min(512, sub)
    vec = vec_spec(depth)
    return pl.pallas_call(
        functools.partial(own_forward_kernel, count),
        out_shape=(
            pltpu.HBM((sub, depth), F4),
            jax.ShapeDtypeStruct((sub, depth), BF),
        ),
        grid_spec=grid_of(
            sub // step,
            [
                own_rows_spec(depth, step, True),
                vec,
                pieces_spec(count, step, width),
                vec,
                vec,
                vec,
            ]
            + [whole_spec(weight[0].shape)] * count,
            (own_rows_spec(depth, step), own_rows_spec(depth, step)),
        ),
        cost_estimate=takes(3),
        compiler_params=pltpu.CompilerParams(vmem_limit_bytes=14 << 20),
        name="own_forward",
    )(
        at * (sub // step),
        in_hbm(x),
        pass_embed[None],
        mixed,
        bias[None],
        gain[None],
        shift[None],
        *weight,
    )


def own_backward_kernel(count, parts, at_ref, *refs):
    grad_parts = refs[:parts]
    mid_ref, dy_ref, gain_ref = refs[parts : parts + 3]
    w_refs = refs[parts + 3 : parts + 3 + count]
    mix_ref, gm_ref, gmix_ref, gw_ref, sums_ref, acc = refs[parts + 3 + count :]
    step = pl.program_id(0)

    @pl.when(step == 0)
    def _():
        acc[...] = jnp.zeros_like(acc)
        sums_ref[...] = jnp.zeros_like(sums_ref)

    grad_lift = functools.reduce(jnp.add, [g[...].astype(F4) for g in grad_parts])
    normal, inv = norm_stats(mid_ref[...])
    dy = dy_ref[...].astype(F4)
    grad_middle = dy + norm_back(grad_lift, normal, inv, gain_ref[...])
    gm_ref[...] = grad_middle
    low = grad_middle.astype(BF)
    for r in range(count):
        gmix_ref[r] = dot(low, w_refs[r][...], NT).astype(BF)
        acc[r] += dot(mix_ref[r], low, TN)
    for i, values in enumerate((grad_middle, grad_lift * normal, grad_lift, dy)):
        sums_ref[i : i + 1, :] += jnp.sum(values, 0, keepdims=True)

    @pl.when(step == pl.num_programs(0) - 1)
    def _():
        gw_ref[...] = acc[...].astype(BF)


def own_backward(grad_parts, middle, dy, at, gain, weight, mixed):
    count, sub, width = mixed.shape
    depth = dy.shape[1]
    step = min(512, sub)
    rows = own_rows_spec(depth, step)
    return pl.pallas_call(
        functools.partial(own_backward_kernel, count, len(grad_parts)),
        out_shape=(
            pltpu.HBM((sub, depth), F4),
            jax.ShapeDtypeStruct((count, sub, width), BF),
            jax.ShapeDtypeStruct((count, width, depth), BF),
            jax.ShapeDtypeStruct((8, depth), F4),
        ),
        grid_spec=grid_of(
            sub // step,
            [rows] * len(grad_parts)
            + [
                rows,
                own_rows_spec(depth, step, True),
                vec_spec(depth),
            ]
            + [whole_spec(weight[0].shape)] * count
            + [pieces_spec(count, step, width)],
            (
                rows,
                pieces_spec(count, step, width),
                whole_spec((count, width, depth)),
                whole_spec((8, depth)),
            ),
            [pltpu.VMEM((count, width, depth), F4)],
        ),
        cost_estimate=takes(6),
        compiler_params=pltpu.CompilerParams(vmem_limit_bytes=18 << 20),
        name="own_backward",
    )(at * (sub // step), *grad_parts, in_hbm(middle), in_hbm(dy), gain[None], *weight, in_hbm(mixed))


def last_norm_kernel(counts, at_ref, *refs):
    split = counts[0]
    left, right = refs[:split], refs[split : split + counts[1]]
    x_ref, pass_ref, gain_ref, gm_ref, out_ref, sums_ref = refs[split + counts[1] :]

    @pl.when(pl.program_id(0) == 0)
    def _():
        sums_ref[...] = jnp.zeros_like(sums_ref)

    grad_norm = jnp.concatenate(
        [functools.reduce(jnp.add, [g[...].astype(F4) for g in side]) for side in (left, right)], 1
    )
    normal, inv = norm_stats(x_ref[...].astype(F4) + pass_ref[...])
    grad_resid = gm_ref[...] + norm_back(grad_norm, normal, inv, gain_ref[...])
    out_ref[...] = grad_resid.astype(BF)
    for i, values in enumerate((grad_resid, grad_norm * normal, grad_norm)):
        sums_ref[i : i + 1, :] += jnp.sum(values, 0, keepdims=True)


def last_norm(left, right, x, at, pass_embed, gain, grad_middle):
    sub, depth = grad_middle.shape
    step = min(512, sub)
    return pl.pallas_call(
        functools.partial(last_norm_kernel, (len(left), len(right))),
        out_shape=(
            jax.ShapeDtypeStruct((sub, depth), BF),
            jax.ShapeDtypeStruct((8, depth), F4),
        ),
        grid_spec=grid_of(
            sub // step,
            [own_rows_spec(depth // 2, step)] * (len(left) + len(right))
            + [
                own_rows_spec(depth, step, True),
                vec_spec(depth),
                vec_spec(depth),
                own_rows_spec(depth, step),
            ],
            (own_rows_spec(depth, step), whole_spec((8, depth))),
        ),
        compiler_params=pltpu.CompilerParams(vmem_limit_bytes=14 << 20),
        name="last_norm",
    )(at * (sub // step), *left, *right, x, pass_embed[None], gain[None], in_hbm(grad_middle))


def units_kernel(count, place_ref, *refs):
    lift_refs = refs[:count]
    dy_ref, up_ref, bias_ref, down_ref, active_ref, pre_ref = refs[count : count + 6]
    outs = refs[count + 6 :]
    step = pl.program_id(0)
    lifted = lift_refs[0][...]
    for i in range(1, count):
        lifted = jnp.where(step == i, lift_refs[i][...], lifted)
    pre_act = dot(lifted, up_ref[...]) + bias_ref[...]
    value, slope = gelu_parts(pre_act)
    active = value.astype(BF)
    active_ref[...] = active
    grad_pre = (dot(dy_ref[...], down_ref[...], NT) * slope).astype(BF)
    pre_ref[...] = grad_pre
    grad_lift = dot(grad_pre, up_ref[...], NT).astype(BF)
    out = dot(active, down_ref[...]).astype(BF)
    for i in range(count):

        @pl.when(step == i)
        def _():
            outs[i][...] = grad_lift
            outs[count + i][...] = out


def units(lifted, dy, place, w_up, b_up, w_down):
    step, depth = lifted[0].shape
    count = len(lifted)
    wide = w_up.shape[1]
    piece = whole_spec((step, depth))
    specs = [piece] * count
    specs += [pl.BlockSpec((step, depth), lambda i, place: (place[i], 0))]
    specs += [whole_spec(w_up.shape), vec_spec(wide), whole_spec(w_down.shape)]
    made = pl.pallas_call(
        functools.partial(units_kernel, count),
        out_shape=(pltpu.VMEM((count * step, wide), BF),) * 2
        + (jax.ShapeDtypeStruct((step, depth), BF),) * (2 * count),
        grid_spec=grid_of(
            count, specs, (own_rows_spec(wide, step),) * 2 + (piece,) * (2 * count)
        ),
        compiler_params=pltpu.CompilerParams(vmem_limit_bytes=22 << 20),
        cost_estimate=takes(10),
        name="units",
    )(place, *lifted, in_hbm(dy), in_hbm(w_up), b_up[None], in_hbm(w_down))
    return made[:2], made[2 : 2 + count], made[2 + count :]


def unit_grads_kernel(count, place_ref, dy_ref, *refs):
    lift_refs = refs[:count]
    active_ref, pre_ref = refs[count : count + 2]
    before = refs[count + 2 : -3]
    out_ref, sum_ref, acc = refs[-3:]
    if before:
        acc[...], sum_ref[...] = before[0][...], before[1][...]
    else:
        acc[...], sum_ref[...] = jnp.zeros_like(acc), jnp.zeros_like(sum_ref)
    size = lift_refs[0].shape[0]
    part = min(BLK, size)
    for i in range(count):

        def rows(j, carry):
            near = pl.ds(pl.multiple_of(j * part, part), part)
            here = pl.ds(pl.multiple_of(i * size + j * part, part), part)
            there = pl.ds(pl.multiple_of(place_ref[i] * size + j * part, part), part)
            pre = pre_ref[here, :]
            acc[0] += dot(lift_refs[i][near, :], pre, TN)
            acc[1] += dot(active_ref[here, :], dy_ref[there, :], TN)
            sum_ref[0:1, :] += jnp.sum(pre.astype(F4), 0, keepdims=True)
            return carry

        lax.fori_loop(0, size // part, rows, 0)
    out_ref[...] = acc[...].astype(out_ref.dtype)


def unit_grads(lifted, made, dy, place, before=(), last=True):
    depth = dy.shape[1]
    wide = made[0].shape[1]
    shape = (2, depth, wide)
    operands = [in_vmem_space(v) for v in (*lifted, *made, *before)]
    return pl.pallas_call(
        functools.partial(unit_grads_kernel, len(lifted)),
        out_shape=(
            pltpu.HBM(shape, BF) if last else pltpu.VMEM(shape, F4),
            jax.ShapeDtypeStruct((8, wide), F4),
        ),
        in_specs=in_smem(1) + in_vmem(1 + len(operands)),
        out_specs=in_vmem(2),
        scratch_shapes=[pltpu.VMEM(shape, F4)],
        compiler_params=pltpu.CompilerParams(vmem_limit_bytes=18 << 20),
        cost_estimate=takes(5),
        name="unit_grads",
    )(place, dy, *operands)


def send(values, axis, partner):
    size = lax.axis_size(axis)
    return lax.ppermute(values, axis, [(i, partner(i)) for i in range(size)])


def hop(values, step):
    return send(values, "tensor", lambda i: i ^ step)


def cross(values):
    return send(values, "seq", lambda i: i ^ 1)


def both(values, step_seq, step_tensor):
    return send(
        values, ("seq", "tensor"), lambda i: (i // 4 ^ step_seq) * 4 + (i % 4 ^ step_tensor)
    )


def add_low(left, right):
    return (left.astype(F4) + right.astype(F4)).astype(BF)


def add_all(arrays):
    return functools.reduce(jnp.add, [a.astype(F4) for a in arrays])


def tie(*values):
    return lax.optimization_barrier(values)


def slot(values, index, size, axis=0):
    return lax.dynamic_slice_in_dim(values, index * size, size, axis)


class Paired:
    def __init__(self, block_len):
        self.me = lax.axis_index("seq")
        self.rank = lax.axis_index("tensor")
        self.sub = block_len // 4
        self.per = self.sub // BLK

    def position(self, natural, blocks):
        half = blocks // 2
        s, b = natural // half, natural % half
        return half * (s ^ self.me) + self.per * ((b // self.per) ^ self.rank) + b % self.per

    def place(self):
        return jnp.stack([self.rank ^ r for r in range(4)]).astype(jnp.int32)

    def far(self, values, first):
        mine = tie(cross(slot(values, self.rank, self.sub)), first)[0]
        other = hop(mine, 2)
        return mine, hop(mine, 1), other

    def gather_weight(self, own):
        return [own, hop(own, 1), hop(own, 2), hop(own, 3)]

    def collect(self, piece, after=None):
        near, away = self.collect_near(piece)
        terms = [*near, hop(away, 2)]
        return terms if after is None else (terms, *tie(*after, away)[:-1])

    def collect_near(self, piece):
        return [piece[0], hop(piece[1], 1)], add_low(piece[2], hop(piece[3], 1))

    def halved(self, values, axis, bit):
        half = values.shape[0] // 2
        at = lax.axis_index(axis) >> bit & 1
        away = send(slot(values, 1 - at, half), axis, lambda i: i ^ (1 << bit))
        return slot(values, at, half), away

    def doubled(self, values, axis, bit, beside):
        at = lax.axis_index(axis) >> bit & 1
        other, beside = tie(send(values, axis, lambda i: i ^ (1 << bit)), beside)
        both = [jnp.where(at == 0, values, other), jnp.where(at == 0, other, values)]
        return jnp.concatenate(both, 0), beside

    def last_sums(self, parts, values, early):
        near_one, near_two = hop(parts[1], 1), hop(parts[3], 1)
        ones = [v.reshape(2, 2, self.sub, -1) for v in (parts[0], near_one)]
        away_one = add_all([v[1] for v in ones]).astype(BF)
        keep, early = tie(parts[2], early, away_one)[:2]
        twos = [v.reshape(2, 2, self.sub, -1) for v in (keep, near_two)]
        away_two = add_all([v[:, 1] for v in twos]).astype(BF)
        kept, away = self.halved(values, "dp", 0)
        got_one, got_two, away = tie(cross(away_one), hop(away_two, 2), away)
        away_one = add_all([v[0, 1] for v in ones] + [got_one[1]]).astype(BF)
        away_two = add_all([v[1, 0] for v in twos] + [got_two[1]]).astype(BF)
        kept, away = self.halved(add_low(kept, away), "seq", 0)
        end_one, end_two, away = tie(hop(away_one, 2), cross(away_two), away)
        values = add_low(kept, away)
        flat = [v.reshape(2 * self.sub, -1) for v in (got_one, got_two)]
        left = [parts[0], near_one, flat[0], end_one]
        right = [keep, near_two, flat[1], end_two]
        return left, right, values, early

    def sum_small(self, shared, ranked, values, beside):
        kept, away = self.halved(values, "dp", 1)
        shared, away, *beside = tie(shared, away, *beside)
        values, got = self.doubled(add_low(kept, away), "dp", 1, hop(shared, 1))
        shared = shared + got
        values, got = self.doubled(values, "seq", 0, hop(shared, 2))
        small = jnp.concatenate([shared + got, ranked], 0)
        small = small + cross(small)
        small = small + send(small, "dp", lambda i: i ^ 1)
        small = small + send(small, "dp", lambda i: i ^ 2)
        values, small = self.doubled(values, "dp", 0, small)
        return small, values, *beside

    def to_tokens(self, mixture):
        width = mixture[0].shape[2]
        columns = []
        for r in range(4):
            here = mixture[r] if r == 0 else both(mixture[r], 0, r)
            there = both(mixture[4 + r], 1, r)
            first = jnp.where(self.me == 0, here, there)
            second = jnp.where(self.me == 0, there, here)
            columns.append(jnp.stack([first, second], 1).reshape(self.sub, width))
        return jnp.stack(columns)

    def to_heads(self, grads, rows):
        parts = grads.reshape(4, self.per, 2, rows, grads.shape[2])
        mine = jnp.where(self.me == 0, parts[:, :, 0], parts[:, :, 1])
        theirs = jnp.where(self.me == 0, parts[:, :, 1], parts[:, :, 0])
        here = [mine[r] if r == 0 else both(mine[r], 0, r) for r in range(4)]
        there = [both(theirs[r], 1, r) for r in range(4)]
        return jnp.concatenate(here + there, 0)


class Plain:
    def __init__(self, block_len):
        self.me = lax.axis_index("seq")
        self.rank = lax.axis_index("tensor")
        self.seq = lax.axis_size("seq")
        self.tensor = lax.axis_size("tensor")
        self.block_len = block_len
        self.sub = block_len // self.tensor

    def position(self, natural, blocks):
        return natural

    def gather_weight(self, own):
        whole = lax.all_gather(own, "tensor", axis=0)
        return [whole[r] for r in range(self.tensor)]

    def collect(self, piece, after=None):
        whole = jnp.concatenate(piece, 0)
        terms = [lax.psum_scatter(whole, "tensor", scatter_dimension=0, tiled=True)]
        return terms if after is None else (terms, *after)

    def last_sums(self, parts, values, early):
        sides = []
        for keep, away in (parts[:2], parts[2:]):
            half = keep.shape[1]
            keep, away = [v.reshape(PIECES // 2, -1, half) for v in (keep, away)]
            whole = jnp.stack([keep, away], 1).reshape(-1, half)
            sides.append(
                [lax.psum_scatter(whole, ("seq", "tensor"), scatter_dimension=0, tiled=True)]
            )
        return *sides, lax.psum(values, ("dp", "seq")), early

    def sum_small(self, shared, ranked, values, beside):
        shared = lax.psum(shared, ("dp", "seq", "tensor"))
        return jnp.concatenate([shared, lax.psum(ranked, ("dp", "seq"))], 0), values, *beside

    def to_tokens(self, mixture):
        blocks, rows, width = mixture.shape
        full = lax.all_gather(mixture, ("seq", "tensor"), axis=0)
        full = full.reshape(self.seq, self.tensor, blocks, rows, width)
        full = full.transpose(1, 2, 0, 3, 4).reshape(self.tensor, -1, width)
        return slot(full, self.me * self.tensor + self.rank, self.sub, 1)

    def to_heads(self, grads, rows):
        full = lax.all_gather(grads, ("seq", "tensor"), axis=1, tiled=True)
        full = full.reshape(self.tensor, -1, self.seq, rows, grads.shape[2])
        return slot(slot(full, self.me, 1, 2)[:, :, 0], self.rank, 1)[0]


def tree_order(seg_row, parent_row, position):
    blocks = seg_row.shape[0] // BLK
    segs = parent_row.shape[0]
    slot_seg = seg_row[::BLK]
    labels = jnp.arange(segs, dtype=jnp.int32)
    above = jnp.sum(jnp.where(slot_seg[:, None] == labels[None, :], parent_row[None, :], 0), 1)
    natural = jnp.arange(blocks, dtype=jnp.int32)
    key = jnp.where(
        slot_seg == 0,
        natural,
        jnp.where(above == 0, 100 + slot_seg, 1000 + 16 * above + slot_seg),
    )
    rank = jnp.sum((key[None, :] < key[:, None]).astype(jnp.int32), 1)
    where = position(natural, blocks)
    order = jnp.sum(jnp.where(rank[:, None] == natural[None, :], where[:, None], 0), 0)
    base = order[0] // TRUNK_BLOCKS * TRUNK_BLOCKS
    return jnp.concatenate([order, base[None]]).astype(jnp.int32)


def padded(values, axis):
    widths = [(0, 0)] * values.ndim
    widths[axis] = (0, LANE - values.shape[axis])
    return jnp.pad(values, widths)


def total(values):
    return jnp.sum(values, axis=0)


def local(
    inputs,
    pass_embed,
    norm1_gain,
    norm1_shift,
    w_qkv,
    b_qv,
    w_out,
    b_out,
    norm2_gain,
    norm2_shift,
    w_up,
    b_up,
    w_down,
    b_down,
    out_grad,
    seg_id,
    parent,
):
    x = inputs[0]
    dy_block = out_grad[0]
    block_len, depth = x.shape
    length = seg_id.shape[1]
    seq, tensor = lax.axis_size("seq"), lax.axis_size("tensor")
    width = w_qkv.shape[2]
    heads = width // HD
    rows = BLK // seq
    paired = (seq, tensor, lax.axis_size("dp")) == (2, 4, 4) and block_len % (4 * BLK) == 0
    move = Paired(block_len) if paired else Plain(block_len)

    order = tree_order(seg_id[0], parent[0], move.position)
    part = move.me[None].astype(jnp.int32)

    w_rows = padded(jnp.swapaxes(w_qkv, 1, 2), 1).reshape(3 * LANE, depth)
    zero = jnp.zeros((LANE,), F4)
    b_cols = jnp.concatenate([padded(b_qv[0], 0), zero, padded(b_qv[1], 0)])
    norm_args = (pass_embed, norm1_gain, norm1_shift, b_cols)
    if paired:
        *near, w_cols = project([x], move.place(), w_rows, *norm_args, turned=False)
        mine, core, other = move.far(x, near[0])
        pair = jnp.arange(2, dtype=jnp.int32)
        pieces = [near, project([mine, core], pair, w_cols, *norm_args)]
        other = tie(other, pieces[1][0])[0]
        pieces.append(project([other, hop(other, 1)], pair, w_cols, *norm_args))
    else:
        full = lax.all_gather(x, "seq", axis=0, tiled=True)
        place = jnp.arange(pl.cdiv(length, 512), dtype=jnp.int32)
        pieces = [project([full], place, w_rows, *norm_args, turned=False)[:2]]

    cuts = 8 if paired else 0
    mixture, lse, keys, qkv, normed, *parts = attend(pieces, order, part, heads, rows, cuts)

    at = move.rank[None].astype(jnp.int32)
    out_weight = move.gather_weight(w_out)
    if paired:
        both_parts = tie(*parts, *out_weight)
        parts, out_weight = both_parts[:cuts], both_parts[cuts:]
    mixed = move.to_tokens(parts or mixture)
    middle, lifted_own = own_forward(
        x, at, pass_embed, mixed, out_weight, b_out, norm2_gain, norm2_shift
    )

    unit_args = (w_up, b_up, w_down)
    if paired:
        core, other = hop(lifted_own, 1), hop(lifted_own, 2)
        near = [lifted_own, core]
        place = move.place()
        near_kept, near_lift, near_out = units(near, dy_block, place[:2], *unit_args)
        so_far = unit_grads(near, near_kept, dy_block, place[:2], last=False)
        other = tie(other, near_lift[1], so_far[1])[0]
        far = [hop(other, 1), other]
        far_place = place[:1:-1]
        far_kept, far_lift, far_out = units(far, dy_block, far_place, *unit_args)
        lift_made = [*near_lift, *far_lift[::-1]]
        out_made = [*near_out, *far_out[::-1]]
        grad_lift, far_place = move.collect(lift_made, [far_place])
        grad_units, up_sums = unit_grads(far, far_kept, dy_block, far_place, so_far)
    else:
        near = [lax.all_gather(lifted_own, "tensor", axis=0, tiled=True)]
        place = jnp.zeros((1,), jnp.int32)
        near_kept, lift_made, out_made = units(near, dy_block, place, *unit_args)
        grad_lift = move.collect(lift_made)
        grad_units, up_sums = unit_grads(near, near_kept, dy_block, place)
    units_sum = lax.psum(grad_units, ("dp", "seq"))
    middle, grad_units = tie(middle, grad_units)
    grad_middle, grad_mix, grad_w_out, early = own_backward(
        grad_lift, middle, dy_block, at, norm2_gain, out_weight, mixed
    )
    out_made, grad_mix = tie(out_made, grad_mix)
    grad_mix = move.to_heads(grad_mix, rows)
    out_terms = move.collect(out_made)
    grad_w_out = move.collect(list(grad_w_out))
    made = attend_back(
        qkv, keys, mixture, grad_mix, lse, normed, w_rows, order, part, heads, rows
    )
    *norm_parts, grad_w_rows, col_sums = made
    count = len(out_terms)
    *norm_parts, grad_w_rows = tie(*norm_parts, grad_w_rows, *out_terms, *grad_w_out)
    norm_parts, grad_w_rows, terms = norm_parts[:4], norm_parts[4], [*norm_parts[5:], grad_w_rows]
    out_terms, grad_w_out = terms[:count], terms[count:]
    rest = add_all(grad_w_out).astype(BF).reshape(3, LANE - width, depth)
    rest = jnp.pad(rest, ((0, 0), (width, 0), (0, 0))).reshape(3 * LANE, depth)
    grad_w_rows = grad_w_rows + rest
    left, right, grad_w_rows, units_sum = move.last_sums(norm_parts, grad_w_rows, units_sum)
    input_grad, late = last_norm(left, right, x, at, pass_embed, norm1_gain, grad_middle)
    sums, grad_w_rows, *out_terms = move.sum_small(
        jnp.concatenate([late[:3], early[:4]], 0),
        jnp.concatenate([up_sums[:1], col_sums[:1]], 0),
        grad_w_rows,
        out_terms,
    )
    output = add_all([*out_terms, middle, b_down]).astype(BF)
    grad_units = units_sum.astype(F4)
    grad_w_rows = grad_w_rows.astype(F4).reshape(3, LANE, depth)
    grad_w_qkv = jnp.swapaxes(grad_w_rows[:, :width], 1, 2)
    grad_w_out = grad_w_rows[:, width:].reshape(width, depth)
    grad_b_qv = jnp.stack([sums[8, :width], sums[8, 2 * LANE : 2 * LANE + width]])
    return (
        output[None],
        input_grad[None],
        sums[0],
        sums[1],
        sums[2],
        grad_w_qkv,
        grad_b_qv,
        grad_w_out,
        sums[3],
        sums[4],
        sums[5],
        grad_units[0],
        sums[7],
        grad_units[1],
        sums[6],
    )


def solution(mesh):
    return jax.shard_map(
        local,
        mesh=mesh,
        in_specs=(
            P("dp", "seq", None),
            P(),
            P(),
            P(),
            P(None, None, "tensor"),
            P(None, "tensor"),
            P("tensor", None),
            P(),
            P(),
            P(),
            P(None, "tensor"),
            P("tensor"),
            P("tensor", None),
            P(),
            P("dp", "seq", None),
            P("dp", None),
            P("dp", None),
        ),
        out_specs=(
            P("dp", ("seq", "tensor"), None),
            P("dp", ("seq", "tensor"), None),
            P(),
            P(),
            P(),
            P(None, None, "tensor"),
            P(None, "tensor"),
            P("tensor", None),
            P(),
            P(),
            P(),
            P(None, "tensor"),
            P("tensor"),
            P("tensor", None),
            P(),
        ),
        check_vma=False,
    )
```

```python
import functools

import jax
import jax.numpy as jnp
from jax import lax
from jax.experimental import pallas as pl
from jax.experimental.pallas import tpu as pltpu
from jax.sharding import PartitionSpec as P

HD = 64
BLK = 256
TRUNK_BLOCKS = 4
LANE = 256
PIECES = 8
EPS = 1e-05
ROOT = 0.7978845608028654
BF = jnp.bfloat16
F4 = jnp.float32
NT = (((1,), (1,)), ((), ()))
NN = (((1,), (0,)), ((), ()))
TN = (((0,), (0,)), ((), ()))
LIGHT = pl.CostEstimate(flops=1000, bytes_accessed=1000, transcendentals=0)


def takes(us):
    return pl.CostEstimate(flops=int(us * 1.1e9), bytes_accessed=1000, transcendentals=0)


def in_hbm(values):
    return pltpu.with_memory_space_constraint(values, pltpu.HBM)


def in_vmem_space(values):
    return pltpu.with_memory_space_constraint(values, pltpu.VMEM)


def dot(left, right, dims=NN):
    return lax.dot_general(left, right, dims, preferred_element_type=F4)


def norm_stats(values):
    row_mean = jnp.mean(values, -1, keepdims=True)
    centred = values - row_mean
    inv_std = lax.rsqrt(jnp.mean(centred * centred, -1, keepdims=True) + EPS)
    return (centred * inv_std, inv_std)


def norm_back(grad_out, normal, inv_std, gain_vec):
    scaled = grad_out * gain_vec
    return inv_std * (
        scaled
        - jnp.mean(scaled, -1, keepdims=True)
        - normal * jnp.mean(scaled * normal, -1, keepdims=True)
    )


def gelu_parts(pre_act):
    cubic_term = 0.044715 * pre_act * pre_act * pre_act
    tangent = jnp.tanh(ROOT * (pre_act + cubic_term))
    gelu_value = 0.5 * pre_act * (1.0 + tangent)
    gelu_slope = 0.5 * (1.0 + tangent) + 0.5 * pre_act * (1.0 - tangent * tangent) * ROOT * (
        1.0 + 3.0 * 0.044715 * pre_act * pre_act
    )
    return (gelu_value, gelu_slope)


def block_rows(pos, count=1):
    return pl.ds(pl.multiple_of(pos * BLK, BLK), count * BLK)


def head_masks(shape, heads):
    lane = lax.broadcasted_iota(jnp.int32, shape, 1) // HD
    return [lane == h for h in range(heads)]


def each_tile(order_ref, tile):
    trunk = [order_ref[i] for i in range(TRUNK_BLOCKS)]
    base = order_ref[16]
    tile(trunk[0], trunk[1], [], [(trunk[0], True)], [(trunk[0], False), (trunk[1], True)])
    tile(
        trunk[2],
        trunk[3],
        [(trunk[0], 2)],
        [(trunk[2], True)],
        [(trunk[2], False), (trunk[3], True)],
    )

    def deep(i, carry):
        one, two = order_ref[4 + 2 * i], order_ref[5 + 2 * i]
        above = order_ref[jnp.maximum(2 + i, 4)]
        tile(one, two, [(base, 4), (above, 1)], [(one, True)], [(two, True)], i >= 2)
        return carry

    lax.fori_loop(0, 6, deep, 0)


def lanes_of(arrays):
    return [a[:, i : i + 128] for a in arrays for i in range(0, a.shape[1], 128)]


def attend_kernel(heads, rows, count, order_ref, part_ref, *refs):
    out_ref, lse_ref, keys_ref, all_ref, normed_ref = refs[2 * count : 2 * count + 5]
    piece_refs = refs[2 * count + 5 : -3]
    qkv_ref, kt_ref, sems = refs[-3:]
    part = part_ref[0]
    length = qkv_ref.shape[0]
    start = 0
    copies = []
    for piece, normed in zip(refs[:count], refs[count : 2 * count]):
        at = pl.ds(start, piece.shape[0])
        for one, whole in ((piece, all_ref), (normed, normed_ref)):
            copies.append(pltpu.make_async_copy(one, whole.at[at], sems.at[len(copies)]))
            copies[-1].start()
        qkv_ref[at] = piece[...]
        start += piece.shape[0]

    def turn(i, carry):
        at = pl.ds(pl.multiple_of(i * 512, 512), 512)
        kt_ref[:, at] = jnp.transpose(qkv_ref[at, LANE : 2 * LANE])
        return carry

    lax.fori_loop(0, length // 512, turn, 0)
    copies.append(pltpu.make_async_copy(kt_ref, keys_ref, sems.at[len(copies)]))
    copies[-1].start()

    def q_at(pos):
        return qkv_ref[pl.ds(pl.multiple_of(pos * BLK + part * rows, rows), rows), 0:LANE]

    def k_at(pos, count=1):
        return kt_ref[:, block_rows(pos, count)]

    def v_at(pos, count=1):
        return qkv_ref[block_rows(pos, count), 2 * LANE : 3 * LANE]

    row_at = lax.broadcasted_iota(jnp.int32, (rows, BLK), 0) + part * rows
    causal = row_at >= lax.broadcasted_iota(jnp.int32, (rows, BLK), 1)
    masks = head_masks((2 * rows, LANE), heads)

    def tile(first, second, shared, parts_a, parts_b, use_last=None):
        q = jnp.concatenate([q_at(first), q_at(second)], 0) * BF(0.125)
        result = jnp.zeros((2 * rows, LANE), F4)
        log_cols = []
        for h in range(heads):
            qm = jnp.where(masks[h], q, BF(0))
            wide = [dot(qm, k_at(p, c)) for p, c in shared]
            if use_last is not None:
                wide[-1] = wide[-1] + jnp.where(use_last, 0.0, -jnp.inf)
            own = []
            for cut, parts in ((qm[:rows], parts_a), (qm[rows:], parts_b)):
                scores = [dot(cut, k_at(p)) for p, _ in parts]
                own.append(
                    [jnp.where(causal, s, -jnp.inf) if d else s for s, (_, d) in zip(scores, parts)]
                )
            top = jnp.concatenate([functools.reduce(jnp.maximum, lanes_of(o)) for o in own], 0)
            top = functools.reduce(jnp.maximum, lanes_of(wide), top)
            top = jnp.max(top, 1, keepdims=True)
            mix = []
            sums = []
            for i, parts in enumerate((parts_a, parts_b)):
                cut = top[i * rows : (i + 1) * rows]
                es = [jnp.exp(s - cut) for s in own[i]]
                sums.append(functools.reduce(jnp.add, lanes_of(es)))
                terms = [dot(e.astype(BF), v_at(p)) for e, (p, _) in zip(es, parts)]
                mix.append(functools.reduce(jnp.add, terms))
            mix = jnp.concatenate(mix, 0)
            total = jnp.concatenate(sums, 0)
            for s, (p, c) in zip(wide, shared):
                e = jnp.exp(s - top)
                total = functools.reduce(jnp.add, lanes_of([e]), total)
                mix = mix + dot(e.astype(BF), v_at(p, c))
            total = jnp.sum(total, 1, keepdims=True)
            result = jnp.where(masks[h], mix / total, result)
            log_cols.append(top + jnp.log(total))
        low = result.astype(BF)[:, : heads * HD]
        out_ref[first] = low[:rows]
        out_ref[second] = low[rows:]
        lane = lax.broadcasted_iota(jnp.int32, (2 * rows, 128), 1)
        cols = jnp.zeros((2 * rows, 128), F4)
        for h in range(heads):
            cols = jnp.where(lane == h, log_cols[h], cols)
        flat = jnp.transpose(cols)[:8]
        lse_ref[first] = flat[:, :rows]
        lse_ref[second] = flat[:, rows:]

    each_tile(order_ref, tile)
    size = out_ref.shape[0] // max(len(piece_refs), 1)
    for i, piece in enumerate(piece_refs):
        piece[...] = out_ref[i * size : (i + 1) * size]
    for copy in copies:
        copy.wait()


def in_vmem(count):
    return [pl.BlockSpec(memory_space=pltpu.VMEM)] * count


def in_smem(count):
    return [pl.BlockSpec(memory_space=pltpu.SMEM)] * count


def attend(pieces, order, part, heads, rows, cuts):
    normed, qkv = zip(*pieces)
    length = sum(q.shape[0] for q in qkv)
    blocks = length // BLK
    return pl.pallas_call(
        functools.partial(attend_kernel, heads, rows, len(pieces)),
        out_shape=(
            pltpu.HBM((blocks, rows, heads * HD), BF),
            pltpu.HBM((blocks, 8, rows), F4),
            pltpu.HBM((LANE, length), BF),
            pltpu.HBM((length, 3 * LANE), BF),
            pltpu.HBM((length, normed[0].shape[1]), BF),
        )
        + (jax.ShapeDtypeStruct((blocks // max(cuts, 1), rows, heads * HD), BF),) * cuts,
        in_specs=in_smem(2) + in_vmem(2 * len(pieces)),
        out_specs=in_vmem(2) + [pl.BlockSpec(memory_space=pltpu.HBM)] * 3 + in_vmem(cuts),
        scratch_shapes=[
            pltpu.VMEM((length, 3 * LANE), BF),
            pltpu.VMEM((LANE, length), BF),
            pltpu.SemaphoreType.DMA((2 * len(pieces) + 1,)),
        ],
        compiler_params=pltpu.CompilerParams(vmem_limit_bytes=26 << 20),
        cost_estimate=takes(25),
        name="tree_attend",
    )(order, part, *[in_vmem_space(v) for v in qkv + normed])


def attend_back_kernel(heads, rows, order_ref, part_ref, *refs):
    far_refs, (lse_ref, w_ref) = refs[:5], refs[5:7]
    norm_refs = refs[7:11]
    proj_ref, sum_ref, acc_q, acc_k, acc_v, acc_w = refs[11:17]
    here_refs, sems = refs[17:22], refs[22]
    qkv_ref, kt_ref, mix_ref, grad_ref, normed_ref = here_refs
    *brings, bring_normed = [
        pltpu.make_async_copy(far, here, sems.at[i])
        for i, (far, here) in enumerate(zip(far_refs, here_refs))
    ]
    for bring in brings:
        bring.start()
    part = part_ref[0]
    width = heads * HD

    def q_rows(pos):
        return pl.ds(pl.multiple_of(pos * BLK + part * rows, rows), rows)

    def k_at(pos, count=1):
        return qkv_ref[block_rows(pos, count), LANE : 2 * LANE]

    def v_at(pos, count=1):
        return qkv_ref[block_rows(pos, count), 2 * LANE : 3 * LANE]

    key_at = lax.broadcasted_iota(jnp.int32, (BLK, rows), 0)
    causal = (lax.broadcasted_iota(jnp.int32, (BLK, rows), 1) + part * rows) >= key_at
    masks = head_masks((2 * rows, LANE), heads)
    row_head = lax.broadcasted_iota(jnp.int32, (LANE, 2 * rows), 0) // HD
    acc_k[...] = jnp.zeros_like(acc_k)
    acc_v[...] = jnp.zeros_like(acc_v)
    acc_q[...] = jnp.zeros_like(acc_q)
    pad = jnp.zeros((2 * rows, LANE - width), BF)
    for bring in brings:
        bring.wait()
    bring_normed.start()

    def tile(first, second, shared, parts_a, parts_b, use_last=None):
        q = jnp.concatenate(
            [qkv_ref[q_rows(first), 0:LANE], qkv_ref[q_rows(second), 0:LANE]], 0
        ) * BF(0.125)
        grad = jnp.concatenate([jnp.concatenate([grad_ref[first], grad_ref[second]], 0), pad], 1)
        mix = jnp.concatenate([jnp.concatenate([mix_ref[first], mix_ref[second]], 0), pad], 1)
        qt, gt, mt = jnp.transpose(q), jnp.transpose(grad), jnp.transpose(mix)
        terms = gt.astype(F4) * mt.astype(F4)
        inner = [
            jnp.sum(terms[h * HD : (h + 1) * HD], 0, keepdims=True) for h in range(heads)
        ]
        lse = jnp.concatenate([lse_ref[first], lse_ref[second]], 1)
        qms = [jnp.where(masks[h], q, BF(0)) for h in range(heads)]
        gms = [jnp.where(masks[h], grad, BF(0)) for h in range(heads)]
        qts = [jnp.where(row_head == h, qt, BF(0)) for h in range(heads)]
        gts = [jnp.where(row_head == h, gt, BF(0)) for h in range(heads)]

        def pieces(keys, values, h, cut, diag, bias):
            e = jnp.exp(dot(keys, qts[h][:, cut]) - (lse[h : h + 1, cut] + bias))
            if diag:
                e = jnp.where(causal, e, 0.0)
            t = dot(values, gts[h][:, cut])
            return e.astype(BF), (e * (t - inner[h][:, cut])).astype(BF)

        def strip(pos, count, cut, diag, grad_q, bias=0.0):
            keys, values = k_at(pos, count), v_at(pos, count)
            es = []
            ds = []
            for h in range(heads):
                e, d = pieces(keys, values, h, cut, diag, bias)
                es.append(e)
                ds.append(d)
                head_keys = kt_ref[h * HD : (h + 1) * HD, block_rows(pos, count)]
                grad_q[h] = grad_q[h] + dot(head_keys, d)
            acc_v[block_rows(pos, count), :] += dot(
                jnp.concatenate(es, 1), jnp.concatenate([g[cut] for g in gms], 0)
            )
            acc_k[block_rows(pos, count), :] += dot(
                jnp.concatenate(ds, 1), jnp.concatenate([g[cut] for g in qms], 0)
            )
            return grad_q

        grad_q = [jnp.zeros((HD, 2 * rows), F4) for _ in range(heads)]
        for i, (pos, count) in enumerate(shared):
            bias = 0.0
            if use_last is not None and i == len(shared) - 1:
                bias = jnp.where(use_last, 0.0, jnp.inf)
            grad_q = strip(pos, count, slice(0, 2 * rows), False, grad_q, bias)
        halves = []
        for i, parts in enumerate((parts_a, parts_b)):
            half = [jnp.zeros((HD, rows), F4) for _ in range(heads)]
            for pos, diag in parts:
                half = strip(pos, 1, slice(i * rows, (i + 1) * rows), diag, half)
            halves.append(half)
        grad_q = jnp.concatenate(
            [g + jnp.concatenate([a, b], 1) for g, a, b in zip(grad_q, *halves)]
            + [jnp.zeros((LANE - width, 2 * rows), F4)],
            0,
        )
        grad_q = jnp.transpose((grad_q * 0.125).astype(BF))
        acc_q[q_rows(first), :] = grad_q[:rows]
        acc_q[q_rows(second), :] = grad_q[rows:]

    each_tile(order_ref, tile)

    half = w_ref.shape[1] // 2
    size = acc_q.shape[0] // PIECES
    acc_w[...] = jnp.zeros_like(acc_w)
    sum_ref[...] = jnp.zeros_like(sum_ref)
    bring_normed.wait()

    def pair(i, carry):
        spot = pl.ds(pl.multiple_of(i * size, size), size)
        for odd in range(2):
            at = pl.ds(pl.multiple_of((2 * i + odd) * size, size), size)
            grads = jnp.concatenate(
                [acc_q[at, :], acc_k[at, :].astype(BF), acc_v[at, :].astype(BF)], 1
            )
            for side in range(2):
                low = dot(grads, w_ref[:, side * half : (side + 1) * half]).astype(BF)
                norm_refs[2 * side + odd][spot, :] = low
            acc_w[...] += dot(grads, normed_ref[at, :], TN)
            sum_ref[0:1, :] += jnp.sum(grads.astype(F4), 0, keepdims=True)
        return carry

    lax.fori_loop(0, PIECES // 2, pair, 0)
    proj_ref[...] = acc_w[...].astype(BF)


def attend_back(qkv, keys, mix, grad, lse, normed, weight, order, part, heads, rows):
    length, depth = normed.shape
    half = jax.ShapeDtypeStruct((length // 2, depth // 2), BF)
    far = pl.BlockSpec(memory_space=pltpu.HBM)
    return pl.pallas_call(
        functools.partial(attend_back_kernel, heads, rows),
        out_shape=(
            half,
            half,
            half,
            half,
            jax.ShapeDtypeStruct((3 * LANE, depth), BF),
            jax.ShapeDtypeStruct((8, 3 * LANE), F4),
        ),
        in_specs=in_smem(2) + [far] * 5 + in_vmem(2),
        out_specs=in_vmem(6),
        scratch_shapes=[
            pltpu.VMEM((length, LANE), BF),
            pltpu.VMEM((length, LANE), F4),
            pltpu.VMEM((length, LANE), F4),
            pltpu.VMEM((3 * LANE, depth), F4),
            pltpu.VMEM(qkv.shape, BF),
            pltpu.VMEM(keys.shape, BF),
            pltpu.VMEM(mix.shape, BF),
            pltpu.VMEM(grad.shape, BF),
            pltpu.VMEM(normed.shape, BF),
            pltpu.SemaphoreType.DMA((5,)),
        ],
        compiler_params=pltpu.CompilerParams(vmem_limit_bytes=50 << 20),
        cost_estimate=LIGHT,
        name="tree_attend_back",
    )(order, part, *[in_hbm(v) for v in (qkv, keys, mix, grad, normed)], lse, weight)


def project_kernel(count, turned, place_ref, *refs):
    x_refs = refs[:count]
    pass_ref, gain_ref, shift_ref, w_ref, b_ref, normed_ref, qkv_ref = refs[count : count + 7]
    if not turned:
        rows_ref, w_ref = w_ref, refs[-1]

        @pl.when(pl.program_id(0) == 0)
        def _():
            w_ref[...] = jnp.transpose(rows_ref[...])

    x = x_refs[0][...]
    for i in range(1, count):
        x = jnp.where(pl.program_id(0) == i, x_refs[i][...], x)
    normal, _ = norm_stats(x.astype(F4) + pass_ref[...])
    normed = (normal * gain_ref[...] + shift_ref[...]).astype(BF)
    normed_ref[...] = normed
    qkv_ref[...] = (dot(normed, w_ref[...]) + b_ref[...]).astype(BF)


def project(pieces, place, weight, pass_embed, gain, shift, bias, turned=True):
    depth = pass_embed.shape[0]
    width = bias.shape[0]
    count = len(pieces)
    step = pieces[0].shape[0] if count > 1 else min(512, pieces[0].shape[0])
    if count > 1:
        specs = [whole_spec((step, depth))] * count
    else:
        specs = [pl.BlockSpec((step, depth), lambda i, place: (place[i], 0))]
    length = step * place.shape[0]
    vec = vec_spec(depth)
    shapes = [pltpu.VMEM((length, depth), BF), pltpu.VMEM((length, width), BF)]
    outs = [own_rows_spec(depth, step), own_rows_spec(width, step)]
    if not turned:
        shapes.append(pltpu.VMEM((depth, width), BF))
        outs.append(whole_spec((depth, width)))
    return pl.pallas_call(
        functools.partial(project_kernel, count, turned),
        out_shape=shapes,
        grid_spec=grid_of(
            length // step,
            specs + [vec, vec, vec, whole_spec(weight.shape), vec_spec(width)],
            outs,
        ),
        compiler_params=pltpu.CompilerParams(vmem_limit_bytes=20 << 20),
        cost_estimate=takes(5),
        name="norm_project",
    )(place, *pieces, pass_embed[None], gain[None], shift[None], weight, bias[None])


def vec_spec(depth):
    return pl.BlockSpec((1, depth), lambda i, at: (0, 0))


def own_rows_spec(depth, step, fixed=False):
    if fixed:
        return pl.BlockSpec((step, depth), lambda i, at: (at[0] + i, 0))
    return pl.BlockSpec((step, depth), lambda i, at: (i, 0))


def pieces_spec(count, step, width):
    return pl.BlockSpec((count, step, width), lambda i, at: (0, i, 0))


def whole_spec(shape):
    return pl.BlockSpec(shape, lambda i, at: (0,) * len(shape))


def grid_of(steps, ins, outs, scratch=()):
    return pltpu.PrefetchScalarGridSpec(
        num_scalar_prefetch=1,
        grid=(steps,),
        in_specs=ins,
        out_specs=outs,
        scratch_shapes=list(scratch),
    )


def own_forward_kernel(
    count, at_ref, x_ref, pass_ref, mix_ref, b_ref, gain_ref, shift_ref, *refs
):
    mid_ref, lift_ref = refs[count:]
    middle = x_ref[...].astype(F4) + pass_ref[...] + b_ref[...]
    for r in range(count):
        middle = middle + dot(mix_ref[r], refs[r][...])
    mid_ref[...] = middle
    normal, _ = norm_stats(middle)
    lift_ref[...] = (normal * gain_ref[...] + shift_ref[...]).astype(BF)


def own_forward(x, at, pass_embed, mixed, weight, bias, gain, shift):
    count, sub, width = mixed.shape
    depth = x.shape[1]
    step = min(512, sub)
    vec = vec_spec(depth)
    return pl.pallas_call(
        functools.partial(own_forward_kernel, count),
        out_shape=(
            pltpu.HBM((sub, depth), F4),
            jax.ShapeDtypeStruct((sub, depth), BF),
        ),
        grid_spec=grid_of(
            sub // step,
            [
                own_rows_spec(depth, step, True),
                vec,
                pieces_spec(count, step, width),
                vec,
                vec,
                vec,
            ]
            + [whole_spec(weight[0].shape)] * count,
            (own_rows_spec(depth, step), own_rows_spec(depth, step)),
        ),
        cost_estimate=takes(3),
        compiler_params=pltpu.CompilerParams(vmem_limit_bytes=14 << 20),
        name="own_forward",
    )(
        at * (sub // step),
        in_hbm(x),
        pass_embed[None],
        mixed,
        bias[None],
        gain[None],
        shift[None],
        *weight,
    )


def own_backward_kernel(count, parts, at_ref, *refs):
    grad_parts = refs[:parts]
    mid_ref, dy_ref, gain_ref = refs[parts : parts + 3]
    w_refs = refs[parts + 3 : parts + 3 + count]
    mix_ref, gm_ref, gmix_ref, gw_ref, sums_ref, acc = refs[parts + 3 + count :]
    step = pl.program_id(0)

    @pl.when(step == 0)
    def _():
        acc[...] = jnp.zeros_like(acc)
        sums_ref[...] = jnp.zeros_like(sums_ref)

    grad_lift = functools.reduce(jnp.add, [g[...].astype(F4) for g in grad_parts])
    normal, inv = norm_stats(mid_ref[...])
    dy = dy_ref[...].astype(F4)
    grad_middle = dy + norm_back(grad_lift, normal, inv, gain_ref[...])
    gm_ref[...] = grad_middle
    low = grad_middle.astype(BF)
    for r in range(count):
        gmix_ref[r] = dot(low, w_refs[r][...], NT).astype(BF)
        acc[r] += dot(mix_ref[r], low, TN)
    for i, values in enumerate((grad_middle, grad_lift * normal, grad_lift, dy)):
        sums_ref[i : i + 1, :] += jnp.sum(values, 0, keepdims=True)

    @pl.when(step == pl.num_programs(0) - 1)
    def _():
        gw_ref[...] = acc[...].astype(BF)


def own_backward(grad_parts, middle, dy, at, gain, weight, mixed):
    count, sub, width = mixed.shape
    depth = dy.shape[1]
    step = min(512, sub)
    rows = own_rows_spec(depth, step)
    return pl.pallas_call(
        functools.partial(own_backward_kernel, count, len(grad_parts)),
        out_shape=(
            pltpu.HBM((sub, depth), F4),
            jax.ShapeDtypeStruct((count, sub, width), BF),
            jax.ShapeDtypeStruct((count, width, depth), BF),
            jax.ShapeDtypeStruct((8, depth), F4),
        ),
        grid_spec=grid_of(
            sub // step,
            [rows] * len(grad_parts)
            + [
                rows,
                own_rows_spec(depth, step, True),
                vec_spec(depth),
            ]
            + [whole_spec(weight[0].shape)] * count
            + [pieces_spec(count, step, width)],
            (
                rows,
                pieces_spec(count, step, width),
                whole_spec((count, width, depth)),
                whole_spec((8, depth)),
            ),
            [pltpu.VMEM((count, width, depth), F4)],
        ),
        cost_estimate=takes(6),
        compiler_params=pltpu.CompilerParams(vmem_limit_bytes=18 << 20),
        name="own_backward",
    )(at * (sub // step), *grad_parts, in_hbm(middle), in_hbm(dy), gain[None], *weight, in_hbm(mixed))


def last_norm_kernel(counts, at_ref, *refs):
    split = counts[0]
    left, right = refs[:split], refs[split : split + counts[1]]
    x_ref, pass_ref, gain_ref, gm_ref, out_ref, sums_ref = refs[split + counts[1] :]

    @pl.when(pl.program_id(0) == 0)
    def _():
        sums_ref[...] = jnp.zeros_like(sums_ref)

    grad_norm = jnp.concatenate(
        [functools.reduce(jnp.add, [g[...].astype(F4) for g in side]) for side in (left, right)], 1
    )
    normal, inv = norm_stats(x_ref[...].astype(F4) + pass_ref[...])
    grad_resid = gm_ref[...] + norm_back(grad_norm, normal, inv, gain_ref[...])
    out_ref[...] = grad_resid.astype(BF)
    for i, values in enumerate((grad_resid, grad_norm * normal, grad_norm)):
        sums_ref[i : i + 1, :] += jnp.sum(values, 0, keepdims=True)


def last_norm(left, right, x, at, pass_embed, gain, grad_middle):
    sub, depth = grad_middle.shape
    step = min(512, sub)
    return pl.pallas_call(
        functools.partial(last_norm_kernel, (len(left), len(right))),
        out_shape=(
            jax.ShapeDtypeStruct((sub, depth), BF),
            jax.ShapeDtypeStruct((8, depth), F4),
        ),
        grid_spec=grid_of(
            sub // step,
            [own_rows_spec(depth // 2, step)] * (len(left) + len(right))
            + [
                own_rows_spec(depth, step, True),
                vec_spec(depth),
                vec_spec(depth),
                own_rows_spec(depth, step),
            ],
            (own_rows_spec(depth, step), whole_spec((8, depth))),
        ),
        compiler_params=pltpu.CompilerParams(vmem_limit_bytes=14 << 20),
        name="last_norm",
    )(at * (sub // step), *left, *right, x, pass_embed[None], gain[None], in_hbm(grad_middle))


def units_kernel(count, place_ref, *refs):
    lift_refs = refs[:count]
    dy_ref, up_ref, bias_ref, down_ref, active_ref, pre_ref = refs[count : count + 6]
    outs = refs[count + 6 :]
    step = pl.program_id(0)
    lifted = lift_refs[0][...]
    for i in range(1, count):
        lifted = jnp.where(step == i, lift_refs[i][...], lifted)
    pre_act = dot(lifted, up_ref[...]) + bias_ref[...]
    value, slope = gelu_parts(pre_act)
    active = value.astype(BF)
    active_ref[...] = active
    grad_pre = (dot(dy_ref[...], down_ref[...], NT) * slope).astype(BF)
    pre_ref[...] = grad_pre
    grad_lift = dot(grad_pre, up_ref[...], NT).astype(BF)
    out = dot(active, down_ref[...]).astype(BF)
    for i in range(count):

        @pl.when(step == i)
        def _():
            outs[i][...] = grad_lift
            outs[count + i][...] = out


def units(lifted, dy, place, w_up, b_up, w_down):
    step, depth = lifted[0].shape
    count = len(lifted)
    wide = w_up.shape[1]
    piece = whole_spec((step, depth))
    specs = [piece] * count
    specs += [pl.BlockSpec((step, depth), lambda i, place: (place[i], 0))]
    specs += [whole_spec(w_up.shape), vec_spec(wide), whole_spec(w_down.shape)]
    made = pl.pallas_call(
        functools.partial(units_kernel, count),
        out_shape=(pltpu.VMEM((count * step, wide), BF),) * 2
        + (jax.ShapeDtypeStruct((step, depth), BF),) * (2 * count),
        grid_spec=grid_of(
            count, specs, (own_rows_spec(wide, step),) * 2 + (piece,) * (2 * count)
        ),
        compiler_params=pltpu.CompilerParams(vmem_limit_bytes=22 << 20),
        cost_estimate=takes(10),
        name="units",
    )(place, *lifted, in_hbm(dy), in_hbm(w_up), b_up[None], in_hbm(w_down))
    return made[:2], made[2 : 2 + count], made[2 + count :]


def unit_grads_kernel(count, place_ref, dy_ref, *refs):
    lift_refs = refs[:count]
    active_ref, pre_ref = refs[count : count + 2]
    before = refs[count + 2 : -3]
    out_ref, sum_ref, acc = refs[-3:]
    if before:
        acc[...], sum_ref[...] = before[0][...], before[1][...]
    else:
        acc[...], sum_ref[...] = jnp.zeros_like(acc), jnp.zeros_like(sum_ref)
    size = lift_refs[0].shape[0]
    part = min(BLK, size)
    for i in range(count):

        def rows(j, carry):
            near = pl.ds(pl.multiple_of(j * part, part), part)
            here = pl.ds(pl.multiple_of(i * size + j * part, part), part)
            there = pl.ds(pl.multiple_of(place_ref[i] * size + j * part, part), part)
            pre = pre_ref[here, :]
            acc[0] += dot(lift_refs[i][near, :], pre, TN)
            acc[1] += dot(active_ref[here, :], dy_ref[there, :], TN)
            sum_ref[0:1, :] += jnp.sum(pre.astype(F4), 0, keepdims=True)
            return carry

        lax.fori_loop(0, size // part, rows, 0)
    out_ref[...] = acc[...].astype(out_ref.dtype)


def unit_grads(lifted, made, dy, place, before=(), last=True):
    depth = dy.shape[1]
    wide = made[0].shape[1]
    shape = (2, depth, wide)
    operands = [in_vmem_space(v) for v in (*lifted, *made, *before)]
    return pl.pallas_call(
        functools.partial(unit_grads_kernel, len(lifted)),
        out_shape=(
            pltpu.HBM(shape, BF) if last else pltpu.VMEM(shape, F4),
            jax.ShapeDtypeStruct((8, wide), F4),
        ),
        in_specs=in_smem(1) + in_vmem(1 + len(operands)),
        out_specs=in_vmem(2),
        scratch_shapes=[pltpu.VMEM(shape, F4)],
        compiler_params=pltpu.CompilerParams(vmem_limit_bytes=18 << 20),
        cost_estimate=takes(5),
        name="unit_grads",
    )(place, dy, *operands)


def send(values, axis, partner):
    size = lax.axis_size(axis)
    return lax.ppermute(values, axis, [(i, partner(i)) for i in range(size)])


def hop(values, step):
    return send(values, "tensor", lambda i: i ^ step)


def cross(values):
    return send(values, "seq", lambda i: i ^ 1)


def both(values, step_seq, step_tensor):
    return send(
        values, ("seq", "tensor"), lambda i: (i // 4 ^ step_seq) * 4 + (i % 4 ^ step_tensor)
    )


def add_low(left, right):
    return (left.astype(F4) + right.astype(F4)).astype(BF)


def add_all(arrays):
    return functools.reduce(jnp.add, [a.astype(F4) for a in arrays])


def tie(*values):
    return lax.optimization_barrier(values)


def slot(values, index, size, axis=0):
    return lax.dynamic_slice_in_dim(values, index * size, size, axis)


class Paired:
    def __init__(self, block_len):
        self.me = lax.axis_index("seq")
        self.rank = lax.axis_index("tensor")
        self.sub = block_len // 4
        self.per = self.sub // BLK

    def position(self, natural, blocks):
        half = blocks // 2
        s, b = natural // half, natural % half
        return half * (s ^ self.me) + self.per * ((b // self.per) ^ self.rank) + b % self.per

    def place(self):
        return jnp.stack([self.rank ^ r for r in range(4)]).astype(jnp.int32)

    def far(self, values, first):
        mine = tie(cross(slot(values, self.rank, self.sub)), first)[0]
        other = hop(mine, 2)
        return mine, hop(mine, 1), other

    def gather_weight(self, own):
        return [own, hop(own, 1), hop(own, 2), hop(own, 3)]

    def collect(self, piece, after=None):
        near, away = self.collect_near(piece)
        terms = [*near, hop(away, 2)]
        return terms if after is None else (terms, *tie(*after, away)[:-1])

    def collect_near(self, piece):
        return [piece[0], hop(piece[1], 1)], add_low(piece[2], hop(piece[3], 1))

    def halved(self, values, axis, bit):
        half = values.shape[0] // 2
        at = lax.axis_index(axis) >> bit & 1
        away = send(slot(values, 1 - at, half), axis, lambda i: i ^ (1 << bit))
        return slot(values, at, half), away

    def doubled(self, values, axis, bit, beside):
        at = lax.axis_index(axis) >> bit & 1
        other, beside = tie(send(values, axis, lambda i: i ^ (1 << bit)), beside)
        both = [jnp.where(at == 0, values, other), jnp.where(at == 0, other, values)]
        return jnp.concatenate(both, 0), beside

    def last_sums(self, parts, values, early):
        near_one, near_two = hop(parts[1], 1), hop(parts[3], 1)
        ones = [v.reshape(2, 2, self.sub, -1) for v in (parts[0], near_one)]
        away_one = add_all([v[1] for v in ones]).astype(BF)
        keep, early = tie(parts[2], early, away_one)[:2]
        twos = [v.reshape(2, 2, self.sub, -1) for v in (keep, near_two)]
        away_two = add_all([v[:, 1] for v in twos]).astype(BF)
        kept, away = self.halved(values, "dp", 0)
        got_one, got_two, away = tie(cross(away_one), hop(away_two, 2), away)
        away_one = add_all([v[0, 1] for v in ones] + [got_one[1]]).astype(BF)
        away_two = add_all([v[1, 0] for v in twos] + [got_two[1]]).astype(BF)
        kept, away = self.halved(add_low(kept, away), "seq", 0)
        end_one, end_two, away = tie(hop(away_one, 2), cross(away_two), away)
        values = add_low(kept, away)
        flat = [v.reshape(2 * self.sub, -1) for v in (got_one, got_two)]
        left = [parts[0], near_one, flat[0], end_one]
        right = [keep, near_two, flat[1], end_two]
        return left, right, values, early

    def sum_small(self, shared, ranked, values, beside):
        kept, away = self.halved(values, "dp", 1)
        shared, away, *beside = tie(shared, away, *beside)
        values, got = self.doubled(add_low(kept, away), "dp", 1, hop(shared, 1))
        shared = shared + got
        values, got = self.doubled(values, "seq", 0, hop(shared, 2))
        small = jnp.concatenate([shared + got, ranked], 0)
        small = small + cross(small)
        small = small + send(small, "dp", lambda i: i ^ 1)
        small = small + send(small, "dp", lambda i: i ^ 2)
        values, small = self.doubled(values, "dp", 0, small)
        return small, values, *beside

    def to_tokens(self, mixture):
        width = mixture[0].shape[2]
        columns = []
        for r in range(4):
            here = mixture[r] if r == 0 else both(mixture[r], 0, r)
            there = both(mixture[4 + r], 1, r)
            first = jnp.where(self.me == 0, here, there)
            second = jnp.where(self.me == 0, there, here)
            columns.append(jnp.stack([first, second], 1).reshape(self.sub, width))
        return jnp.stack(columns)

    def to_heads(self, grads, rows):
        parts = grads.reshape(4, self.per, 2, rows, grads.shape[2])
        mine = jnp.where(self.me == 0, parts[:, :, 0], parts[:, :, 1])
        theirs = jnp.where(self.me == 0, parts[:, :, 1], parts[:, :, 0])
        here = [mine[r] if r == 0 else both(mine[r], 0, r) for r in range(4)]
        there = [both(theirs[r], 1, r) for r in range(4)]
        return jnp.concatenate(here + there, 0)


class Plain:
    def __init__(self, block_len):
        self.me = lax.axis_index("seq")
        self.rank = lax.axis_index("tensor")
        self.seq = lax.axis_size("seq")
        self.tensor = lax.axis_size("tensor")
        self.block_len = block_len
        self.sub = block_len // self.tensor

    def position(self, natural, blocks):
        return natural

    def gather_weight(self, own):
        whole = lax.all_gather(own, "tensor", axis=0)
        return [whole[r] for r in range(self.tensor)]

    def collect(self, piece, after=None):
        whole = jnp.concatenate(piece, 0)
        terms = [lax.psum_scatter(whole, "tensor", scatter_dimension=0, tiled=True)]
        return terms if after is None else (terms, *after)

    def last_sums(self, parts, values, early):
        sides = []
        for keep, away in (parts[:2], parts[2:]):
            half = keep.shape[1]
            keep, away = [v.reshape(PIECES // 2, -1, half) for v in (keep, away)]
            whole = jnp.stack([keep, away], 1).reshape(-1, half)
            sides.append(
                [lax.psum_scatter(whole, ("seq", "tensor"), scatter_dimension=0, tiled=True)]
            )
        return *sides, lax.psum(values, ("dp", "seq")), early

    def sum_small(self, shared, ranked, values, beside):
        shared = lax.psum(shared, ("dp", "seq", "tensor"))
        return jnp.concatenate([shared, lax.psum(ranked, ("dp", "seq"))], 0), values, *beside

    def to_tokens(self, mixture):
        blocks, rows, width = mixture.shape
        full = lax.all_gather(mixture, ("seq", "tensor"), axis=0)
        full = full.reshape(self.seq, self.tensor, blocks, rows, width)
        full = full.transpose(1, 2, 0, 3, 4).reshape(self.tensor, -1, width)
        return slot(full, self.me * self.tensor + self.rank, self.sub, 1)

    def to_heads(self, grads, rows):
        full = lax.all_gather(grads, ("seq", "tensor"), axis=1, tiled=True)
        full = full.reshape(self.tensor, -1, self.seq, rows, grads.shape[2])
        return slot(slot(full, self.me, 1, 2)[:, :, 0], self.rank, 1)[0]


def tree_order(seg_row, parent_row, position):
    blocks = seg_row.shape[0] // BLK
    segs = parent_row.shape[0]
    slot_seg = seg_row[::BLK]
    labels = jnp.arange(segs, dtype=jnp.int32)
    above = jnp.sum(jnp.where(slot_seg[:, None] == labels[None, :], parent_row[None, :], 0), 1)
    natural = jnp.arange(blocks, dtype=jnp.int32)
    key = jnp.where(
        slot_seg == 0,
        natural,
        jnp.where(above == 0, 100 + slot_seg, 1000 + 16 * above + slot_seg),
    )
    rank = jnp.sum((key[None, :] < key[:, None]).astype(jnp.int32), 1)
    where = position(natural, blocks)
    order = jnp.sum(jnp.where(rank[:, None] == natural[None, :], where[:, None], 0), 0)
    base = order[0] // TRUNK_BLOCKS * TRUNK_BLOCKS
    return jnp.concatenate([order, base[None]]).astype(jnp.int32)


def padded(values, axis):
    widths = [(0, 0)] * values.ndim
    widths[axis] = (0, LANE - values.shape[axis])
    return jnp.pad(values, widths)


def total(values):
    return jnp.sum(values, axis=0)


def local(
    inputs,
    pass_embed,
    norm1_gain,
    norm1_shift,
    w_qkv,
    b_qv,
    w_out,
    b_out,
    norm2_gain,
    norm2_shift,
    w_up,
    b_up,
    w_down,
    b_down,
    out_grad,
    seg_id,
    parent,
):
    x = inputs[0]
    dy_block = out_grad[0]
    block_len, depth = x.shape
    length = seg_id.shape[1]
    seq, tensor = lax.axis_size("seq"), lax.axis_size("tensor")
    width = w_qkv.shape[2]
    heads = width // HD
    rows = BLK // seq
    paired = (seq, tensor, lax.axis_size("dp")) == (2, 4, 4) and block_len % (4 * BLK) == 0
    move = Paired(block_len) if paired else Plain(block_len)

    order = tree_order(seg_id[0], parent[0], move.position)
    part = move.me[None].astype(jnp.int32)

    w_rows = padded(jnp.swapaxes(w_qkv, 1, 2), 1).reshape(3 * LANE, depth)
    zero = jnp.zeros((LANE,), F4)
    b_cols = jnp.concatenate([padded(b_qv[0], 0), zero, padded(b_qv[1], 0)])
    norm_args = (pass_embed, norm1_gain, norm1_shift, b_cols)
    if paired:
        *near, w_cols = project([x], move.place(), w_rows, *norm_args, turned=False)
        mine, core, other = move.far(x, near[0])
        pair = jnp.arange(2, dtype=jnp.int32)
        pieces = [near, project([mine, core], pair, w_cols, *norm_args)]
        other = tie(other, pieces[1][0])[0]
        pieces.append(project([other, hop(other, 1)], pair, w_cols, *norm_args))
    else:
        full = lax.all_gather(x, "seq", axis=0, tiled=True)
        place = jnp.arange(pl.cdiv(length, 512), dtype=jnp.int32)
        pieces = [project([full], place, w_rows, *norm_args, turned=False)[:2]]

    cuts = 8 if paired else 0
    mixture, lse, keys, qkv, normed, *parts = attend(pieces, order, part, heads, rows, cuts)

    at = move.rank[None].astype(jnp.int32)
    out_weight = move.gather_weight(w_out)
    if paired:
        both_parts = tie(*parts, *out_weight)
        parts, out_weight = both_parts[:cuts], both_parts[cuts:]
    mixed = move.to_tokens(parts or mixture)
    middle, lifted_own = own_forward(
        x, at, pass_embed, mixed, out_weight, b_out, norm2_gain, norm2_shift
    )

    unit_args = (w_up, b_up, w_down)
    if paired:
        core, other = hop(lifted_own, 1), hop(lifted_own, 2)
        near = [lifted_own, core]
        place = move.place()
        near_kept, near_lift, near_out = units(near, dy_block, place[:2], *unit_args)
        so_far = unit_grads(near, near_kept, dy_block, place[:2], last=False)
        other = tie(other, near_lift[1], so_far[1])[0]
        far = [hop(other, 1), other]
        far_place = place[:1:-1]
        far_kept, far_lift, far_out = units(far, dy_block, far_place, *unit_args)
        lift_made = [*near_lift, *far_lift[::-1]]
        out_made = [*near_out, *far_out[::-1]]
        grad_lift, far_place = move.collect(lift_made, [far_place])
        grad_units, up_sums = unit_grads(far, far_kept, dy_block, far_place, so_far)
    else:
        near = [lax.all_gather(lifted_own, "tensor", axis=0, tiled=True)]
        place = jnp.zeros((1,), jnp.int32)
        near_kept, lift_made, out_made = units(near, dy_block, place, *unit_args)
        grad_lift = move.collect(lift_made)
        grad_units, up_sums = unit_grads(near, near_kept, dy_block, place)
    units_sum = lax.psum(grad_units, ("dp", "seq"))
    middle, grad_units = tie(middle, grad_units)
    grad_middle, grad_mix, grad_w_out, early = own_backward(
        grad_lift, middle, dy_block, at, norm2_gain, out_weight, mixed
    )
    out_made, grad_mix = tie(out_made, grad_mix)
    grad_mix = move.to_heads(grad_mix, rows)
    out_terms = move.collect(out_made)
    grad_w_out = move.collect(list(grad_w_out))
    made = attend_back(
        qkv, keys, mixture, grad_mix, lse, normed, w_rows, order, part, heads, rows
    )
    *norm_parts, grad_w_rows, col_sums = made
    count = len(out_terms)
    *norm_parts, grad_w_rows = tie(*norm_parts, grad_w_rows, *out_terms, *grad_w_out)
    norm_parts, grad_w_rows, terms = norm_parts[:4], norm_parts[4], [*norm_parts[5:], grad_w_rows]
    out_terms, grad_w_out = terms[:count], terms[count:]
    rest = add_all(grad_w_out).astype(BF).reshape(3, LANE - width, depth)
    rest = jnp.pad(rest, ((0, 0), (width, 0), (0, 0))).reshape(3 * LANE, depth)
    grad_w_rows = grad_w_rows + rest
    left, right, grad_w_rows, units_sum = move.last_sums(norm_parts, grad_w_rows, units_sum)
    input_grad, late = last_norm(left, right, x, at, pass_embed, norm1_gain, grad_middle)
    sums, grad_w_rows, *out_terms = move.sum_small(
        jnp.concatenate([late[:3], early[:4]], 0),
        jnp.concatenate([up_sums[:1], col_sums[:1]], 0),
        grad_w_rows,
        out_terms,
    )
    output = add_all([*out_terms, middle, b_down]).astype(BF)
    grad_units = units_sum.astype(F4)
    grad_w_rows = grad_w_rows.astype(F4).reshape(3, LANE, depth)
    grad_w_qkv = jnp.swapaxes(grad_w_rows[:, :width], 1, 2)
    grad_w_out = grad_w_rows[:, width:].reshape(width, depth)
    grad_b_qv = jnp.stack([sums[8, :width], sums[8, 2 * LANE : 2 * LANE + width]])
    return (
        output[None],
        input_grad[None],
        sums[0],
        sums[1],
        sums[2],
        grad_w_qkv,
        grad_b_qv,
        grad_w_out,
        sums[3],
        sums[4],
        sums[5],
        grad_units[0],
        sums[7],
        grad_units[1],
        sums[6],
    )


def solution(mesh):
    return jax.shard_map(
        local,
        mesh=mesh,
        in_specs=(
            P("dp", "seq", None),
            P(),
            P(),
            P(),
            P(None, None, "tensor"),
            P(None, "tensor"),
            P("tensor", None),
            P(),
            P(),
            P(),
            P(None, "tensor"),
            P("tensor"),
            P("tensor", None),
            P(),
            P("dp", "seq", None),
            P("dp", None),
            P("dp", None),
        ),
        out_specs=(
            P("dp", ("seq", "tensor"), None),
            P("dp", ("seq", "tensor"), None),
            P(),
            P(),
            P(),
            P(None, None, "tensor"),
            P(None, "tensor"),
            P("tensor", None),
            P(),
            P(),
            P(),
            P(None, "tensor"),
            P("tensor"),
            P("tensor", None),
            P(),
        ),
        check_vma=False,
    )
```
